32 devices in a mesh: section: 4 (over y, x), expert: 8 (over z, core).
Axes of the slice: x: 2, y: 2, z: 4, core: 2. Of those that a mesh axis runs over, the one named last changes fastest.
Arguments:
- inputs: bfloat16 [4, 2, 512, 2560], P('section', None, 'expert'), may hold values from -6 to 6
- teacher: bfloat16 [4, 2, 512, 2560], P('section', None, 'expert'), may hold values from -6 to 6
- gate: float32 [4, 2, 512], P('section', None, 'expert'), may hold values from 0.2 to 1
- route: int32 [4, 2, 512], P('section', None, 'expert'), may hold values from 0 to 7, as said below
- slot: int32 [4, 2, 512], P('section', None, 'expert'), may hold values from 0 to 15
- factor: bfloat16 [4, 2560, 768], P('section'), may hold values from -0.125 to 0.125
- cores: bfloat16 [4, 8, 768, 768], P('section', 'expert'), may hold values from -0.21875 to 0.21875
Outputs:
- factor_grad: float32 [4, 2560, 768], P('section', 'expert')
- core_grad: bfloat16 [4, 8, 768, 768], P('section', 'expert')
The draws below stay inside these ranges and needn't reach their ends.
Inputs may be any that keep to these rules, and one draw needn't show every extreme that they name: Within each layer, micro-batch and aligned block of 64 tokens (those of one device), no two tokens share both route and slot, so an expert takes at most 16 tokens of a block; in every block some expert takes exactly 16.
All inputs are finite; a program needn't handle non-finite values.
Results may differ from the reference program's by a relative error of at most 0.012.
Values may be sent and summed in bfloat16 or wider, within the bound.
No kernel may reach another device: no remote copies, remote signals or barrier semaphores. Data moves between devices by JAX's collectives and lax.ppermute only.
A program may use at most 128 MiB of HBM per device.

```python
import jax
import jax.numpy as jnp

D = 2560
RANK = 768
MICRO = 2
TOK_DEV = 64
SECTIONS = 4
EXPERTS = 8
CAP = 16
TOKENS = 512
N_EXPERT = 8


def routing_places(key):
    total = EXPERTS * CAP
    blocks_count = SECTIONS * MICRO * N_EXPERT
    block_keys = jax.random.split(jax.random.fold_in(key, 7), blocks_count)

    def single(block_key):
        first_key, second_key = jax.random.split(block_key)
        ordering = jax.random.permutation(first_key, total).astype(jnp.int32)
        positions = jnp.argsort(ordering).astype(jnp.int32)
        chosen_expert = ordering[0] // CAP
        labels = jnp.arange(total, dtype=jnp.int32)
        scores = jnp.where(labels // CAP == chosen_expert, -1, positions)
        picked = jnp.argsort(scores, stable=True)[:TOK_DEV].astype(jnp.int32)
        shuffle = jax.random.permutation(second_key, TOK_DEV)
        return picked[shuffle].astype(jnp.int32)
    places = jax.vmap(single)(block_keys)
    return places.reshape(SECTIONS, MICRO, N_EXPERT * TOK_DEV)


def draw_route(key, part):
    return (routing_places(key) // CAP).astype(jnp.int32)


def draw_slot(key, part):
    return (routing_places(key) % CAP).astype(jnp.int32)


def levels(key, dims, shards, smallest, high):
    loudness, own = 1.0, jax.random.fold_in(key, 6)
    for axis_at, shards_of in shards:
        steps = jnp.exp(jax.random.uniform(jax.random.fold_in(own, axis_at), (shards_of,), jnp.float32, smallest / len(shards), high / len(shards)))
        loudness = loudness * jnp.repeat(steps, dims[axis_at] // shards_of).reshape([-1 if axis == axis_at else 1 for axis in range(len(dims))])
    return loudness


def scatter_about(stream_key, extent, spread, limit, pieces=(), kind=jnp.bfloat16):
    array = jax.random.normal(stream_key, extent, jnp.float32) * spread
    if len(pieces) > 0:
        array = levels(stream_key, extent, pieces, -0.22, 0.18) * array
    return jnp.clip(array, min=-limit, max=limit).astype(kind)


def setup_inputs(seed: int = 0) -> dict:
    seeds = jax.random.split(jax.random.key(seed), 8)
    return {
        "inputs": scatter_about(seeds[0], (SECTIONS, MICRO, TOKENS, D), 1.0, 6.0, ((0, 4), (2, 8))),
        "teacher": scatter_about(seeds[1], (SECTIONS, MICRO, TOKENS, D), 1.0, 6.0, ((0, 4), (2, 8))),
        "gate": jnp.clip(0.2 + 0.8 * jax.random.uniform(seeds[2], (SECTIONS, MICRO, TOKENS), jnp.float32) ** levels(seeds[2], (SECTIONS, MICRO, TOKENS), ((0, 4), (2, 8)), -0.2, 0.2), 0.2, 1.0),
        "route": draw_route(jax.random.fold_in(seeds[7], 71), 0),
        "slot": draw_slot(jax.random.fold_in(seeds[7], 71), 0),
        "factor": scatter_about(seeds[5], (SECTIONS, D, RANK), D ** -0.5, 0.125, ((0, 4),)),
        "cores": scatter_about(seeds[6], (SECTIONS, EXPERTS, RANK, RANK), RANK ** -0.5, 0.21875, ((0, 4), (1, 8))),
    }


def silu_slope(values):
    sigmoid = jax.nn.sigmoid(values)
    return sigmoid * (1.0 + values * (1.0 - sigmoid))


def to_experts(rows, places):
    columns = rows.shape[-1]
    sources = rows.reshape(N_EXPERT, TOK_DEV, columns)
    targets = places.reshape(N_EXPERT, TOK_DEV)
    owners = jnp.arange(N_EXPERT, dtype=jnp.int32)[:, None]
    buffer = jnp.zeros((N_EXPERT, EXPERTS * CAP, columns), rows.dtype).at[owners, targets].set(sources)
    buffer = buffer.reshape(N_EXPERT, EXPERTS, CAP, columns).transpose(1, 0, 2, 3)
    return buffer.reshape(EXPERTS, N_EXPERT * CAP, columns)


def to_tokens(buffer, places):
    columns = buffer.shape[-1]
    regrouped = buffer.reshape(EXPERTS, N_EXPERT, CAP, columns).transpose(1, 0, 2, 3)
    regrouped = regrouped.reshape(N_EXPERT, EXPERTS * CAP, columns)
    targets = places.reshape(N_EXPERT, TOK_DEV)
    picked = jnp.take_along_axis(regrouped, targets[:, :, None], axis=1)
    return picked.reshape(N_EXPERT * TOK_DEV, columns)


def reference(inputs, teacher, gate, route, slot, factor, cores):
    places_all = (route * CAP + slot).astype(jnp.int32)
    incoming = jnp.zeros((MICRO, TOKENS, D), jnp.float32)
    factor_list = []
    core_list = []
    for section_index in reversed(range(SECTIONS)):
        shared = factor[section_index]
        blocks = cores[section_index].astype(jnp.float32)
        factor_total = jnp.zeros((D, RANK), jnp.float32)
        core_total = jnp.zeros((EXPERTS, RANK, RANK), jnp.float32)
        passed = []
        for micro_index in range(MICRO):
            tokens_now = inputs[section_index, micro_index]
            places = places_all[section_index, micro_index]
            weight_now = gate[section_index, micro_index][:, None]
            projected = jnp.dot(tokens_now, shared, preferred_element_type=jnp.float32).astype(jnp.bfloat16)
            routed = to_experts(projected, places)
            pre = jnp.einsum("esr,erk->esk", routed.astype(jnp.float32), blocks)
            active = jax.nn.silu(pre).astype(jnp.bfloat16)
            hidden = to_tokens(active, places)
            mixed = jnp.dot(hidden, shared.T, preferred_element_type=jnp.float32)
            output = tokens_now.astype(jnp.float32) + weight_now * mixed
            grad_out = output - teacher[section_index, micro_index].astype(jnp.float32) + incoming[micro_index]
            grad_mixed = (weight_now * grad_out).astype(jnp.bfloat16)
            grad_hidden = jnp.dot(grad_mixed, shared, preferred_element_type=jnp.float32).astype(jnp.bfloat16)
            routed_grad = to_experts(grad_hidden, places)
            grad_pre = (routed_grad.astype(jnp.float32) * silu_slope(pre)).astype(jnp.bfloat16)
            grad_routed = jnp.einsum("esk,erk->esr", grad_pre.astype(jnp.float32), blocks).astype(jnp.bfloat16)
            grad_proj = to_tokens(grad_routed, places)
            grad_in = (grad_out + jnp.dot(grad_proj, shared.T, preferred_element_type=jnp.float32)).astype(jnp.bfloat16)
            core_total = core_total + jnp.einsum("esr,esk->erk", routed.astype(jnp.float32), grad_pre.astype(jnp.float32))
            factor_total = factor_total + jnp.dot(tokens_now.T, grad_proj, preferred_element_type=jnp.float32)
            factor_total = factor_total + jnp.dot(grad_mixed.T, hidden, preferred_element_type=jnp.float32)
            passed.append(grad_in.astype(jnp.float32))
        incoming = jnp.stack(passed)
        factor_list.append(factor_total)
        core_list.append(core_total.astype(jnp.bfloat16))
    factor_grad = jnp.stack(factor_list[::-1])
    core_grad = jnp.stack(core_list[::-1])
    return (factor_grad, core_grad)
```

```python
import jax
import jax.numpy as jnp
from jax import lax
from jax.experimental import pallas as pl
from jax.experimental.pallas import tpu as pltpu
from jax.sharding import PartitionSpec as P


def from_behind(value, axis, steps):
    count = lax.axis_size(axis)
    leading, last = (max(0, -steps), min(count, count - steps))
    return lax.ppermute(value, axis, [(source, source + steps) for source in range(leading, last)])


def silu_slope(values):
    sigmoid = jax.nn.sigmoid(values)
    return sigmoid * (1.0 + values * (1.0 - sigmoid))


def times_transposed(left, shared):
    return lax.dot_general(
        left, shared, (((1,), (1,)), ((), ())), preferred_element_type=jnp.float32
    )


def factor_terms(tokens_flat, proj_flat, mixed_flat, hidden_flat):

    def factor_rows(start, count):
        first_term = lax.dot_general(
            tokens_flat, proj_flat, (((0,), (0,)), ((), ())), preferred_element_type=jnp.float32
        )
        second_term = lax.dot_general(
            mixed_flat, hidden_flat, (((0,), (0,)), ((), ())), preferred_element_type=jnp.float32
        )
        return first_term + second_term

    return factor_rows


def store_slice(store, fresh, picked, usable):
    former = lax.dynamic_index_in_dim(store, picked, 0, keepdims=False)
    kept = jnp.where(usable, fresh, former)
    return lax.dynamic_update_index_in_dim(store, kept, picked, 0)


def general_plan(inputs, teacher, gate, route, slot, factor, cores):
    tokens_all = inputs[0]
    targets_all = teacher[0]
    weights_all = gate[0]
    shared = factor[0]
    blocks = cores[0]
    micro_count, token_count, channels = tokens_all.shape
    ranks = shared.shape[1]
    local_experts = blocks.shape[0]
    expert_devices = lax.axis_size("expert")
    capacity = max(2, 2 * token_count // (local_experts * expert_devices))
    slot_count = local_experts * expert_devices * capacity
    places_all = route[0] * capacity + slot[0]
    micro_range = jnp.arange(micro_count, dtype=jnp.int32)[:, None]
    token_proj = jnp.dot(
        tokens_all.reshape(-1, channels), shared, preferred_element_type=jnp.float32
    ).astype(jnp.bfloat16)
    token_proj = token_proj.reshape(micro_count, token_count, ranks)
    proj_slots = (
        jnp.zeros((micro_count, slot_count, ranks), jnp.bfloat16)
        .at[micro_range, places_all]
        .set(token_proj)
    )
    projected = lax.all_to_all(proj_slots, "expert", split_axis=1, concat_axis=1, tiled=True)
    projected = projected.reshape(micro_count, expert_devices, local_experts, capacity, ranks)
    pre = jnp.einsum("mnecr,erk->mneck", projected, blocks, preferred_element_type=jnp.float32)
    active = jax.nn.silu(pre).astype(jnp.bfloat16)
    returned = lax.all_to_all(
        active.reshape(micro_count, slot_count, ranks),
        "expert",
        split_axis=1,
        concat_axis=1,
        tiled=True,
    )
    hidden = jnp.take_along_axis(returned, places_all[:, :, None], axis=1)
    mixed = times_transposed(hidden.reshape(-1, ranks), shared).reshape(
        micro_count, token_count, channels
    )
    output = tokens_all.astype(jnp.float32) + weights_all[:, :, None] * mixed
    errors = output - targets_all.astype(jnp.float32)
    section_count = lax.axis_size("section")
    section_here = lax.axis_index("section")
    incoming = jnp.zeros((token_count, channels), jnp.bfloat16)
    mixed_store = jnp.zeros((micro_count, token_count, channels), jnp.bfloat16)
    proj_store = jnp.zeros((micro_count, token_count, ranks), jnp.bfloat16)
    pre_store = jnp.zeros(
        (micro_count, expert_devices, local_experts, capacity, ranks), jnp.bfloat16
    )
    turn_total = micro_count + section_count - 1
    for turn_index in range(turn_total):
        micro_now = turn_index - (section_count - 1 - section_here)
        usable = jnp.logical_and(micro_now >= 0, micro_now < micro_count)
        picked = jnp.clip(micro_now, 0, micro_count - 1)
        grad_out = lax.dynamic_index_in_dim(errors, picked, 0, keepdims=False) + incoming.astype(
            jnp.float32
        )
        weight_now = lax.dynamic_index_in_dim(weights_all, picked, 0, keepdims=False)
        places = lax.dynamic_index_in_dim(places_all, picked, 0, keepdims=False)
        grad_mixed = (weight_now[:, None] * grad_out).astype(jnp.bfloat16)
        grad_hidden = jnp.dot(grad_mixed, shared, preferred_element_type=jnp.float32).astype(
            jnp.bfloat16
        )
        grad_slots = jnp.zeros((slot_count, ranks), jnp.bfloat16).at[places].set(grad_hidden)
        grad_recv = lax.all_to_all(grad_slots, "expert", split_axis=0, concat_axis=0, tiled=True)
        grad_recv = grad_recv.reshape(expert_devices, local_experts, capacity, ranks)
        pre_now = lax.dynamic_index_in_dim(pre, picked, 0, keepdims=False)
        grad_pre = (grad_recv.astype(jnp.float32) * silu_slope(pre_now)).astype(jnp.bfloat16)
        grad_routed = jnp.einsum(
            "neck,erk->necr", grad_pre, blocks, preferred_element_type=jnp.float32
        ).astype(jnp.bfloat16)
        grad_home = lax.all_to_all(
            grad_routed.reshape(slot_count, ranks),
            "expert",
            split_axis=0,
            concat_axis=0,
            tiled=True,
        )
        grad_proj = grad_home[places]
        grad_in = (grad_out + times_transposed(grad_proj, shared)).astype(jnp.bfloat16)
        if turn_index + 1 < turn_total:
            incoming = from_behind(grad_in, "section", -1)
        mixed_store = store_slice(mixed_store, grad_mixed, picked, usable)
        proj_store = store_slice(proj_store, grad_proj, picked, usable)
        pre_store = store_slice(pre_store, grad_pre, picked, usable)
    core_total = jnp.einsum(
        "mnecr,mneck->erk", projected, pre_store, preferred_element_type=jnp.float32
    )
    all_rows = factor_terms(
        tokens_all.reshape(-1, channels),
        proj_store.reshape(-1, ranks),
        mixed_store.reshape(-1, channels),
        hidden.reshape(-1, ranks),
    )
    factor_share = lax.psum_scatter(
        all_rows(jnp.int32(0), channels // expert_devices * lax.axis_size("expert")),
        "expert",
        scatter_dimension=0,
        tiled=True,
    )
    return (factor_share[None], core_total.astype(jnp.bfloat16)[None])


CORES = 2
CHIPS = 4
LAYERS = 4


def dot(left, right):
    return jnp.dot(left, right, preferred_element_type=jnp.float32)


def dot_first(left, right):
    return lax.dot_general(
        left, right, (((0,), (0,)), ((), ())), preferred_element_type=jnp.float32
    )


def on_chips(value, pairs):
    perm = [
        (CORES * source + core, CORES * target + core)
        for source, target in pairs
        for core in range(CORES)
    ]
    return lax.ppermute(value, "expert", perm)


def swap_cores(value):
    count = lax.axis_size("expert")
    return lax.ppermute(value, "expert", [(index, index ^ 1) for index in range(count)])


def between_layers(value, pairs):
    return lax.ppermute(value, "section", pairs)


def gather_cores(core, middle):
    beside = on_chips(core, [(0, 1), (1, 0), (2, 3), (3, 2)])
    across = on_chips(core, [(1, 2), (2, 1)])
    far_across = on_chips(beside, [(1, 2), (2, 1)])
    outward = on_chips(across, [(1, 0), (2, 3)])
    far_outward = on_chips(far_across, [(1, 0), (2, 3)])
    second = jnp.where(middle, across, outward)
    third = jnp.where(middle, far_across, far_outward)
    held = [core, beside, second, third]
    return held + [swap_cores(piece) for piece in held]


def held_chips(chip, middle):
    near, far = chip ^ 3, chip ^ 2
    return [chip, chip ^ 1, jnp.where(middle, near, far), jnp.where(middle, far, near)]


def gather_rows(rows):
    held = [rows]
    for step in range(1, CHIPS):
        held.append(on_chips(rows, [(chip, chip ^ step) for chip in range(CHIPS)]))
    return held + [swap_cores(piece) for piece in held]


def expert_ids(chips, core):
    return jnp.stack(
        [CORES * chip + core for chip in chips] + [CORES * chip + 1 - core for chip in chips]
    ).astype(jnp.int32)


def routed_product(rows, route, ids_ref, core_refs, transposed):
    dims = (((1,), (1 if transposed else 0,)), ((), ()))
    total = None
    for place, core_ref in enumerate(core_refs):
        chosen = jnp.where(route == ids_ref[place], rows, jnp.zeros_like(rows))
        term = lax.dot_general(
            chosen, core_ref[...], dims, preferred_element_type=jnp.float32
        )
        total = term if total is None else total + term
    return total


def backward_rows(score, weight, slope, route, ids_ref, core_refs):
    grad_hidden = (weight * score).astype(jnp.bfloat16)
    grad_pre = (grad_hidden.astype(jnp.float32) * slope).astype(jnp.bfloat16)
    grad_proj = routed_product(grad_pre, route, ids_ref, core_refs, True)
    return grad_pre, grad_proj.astype(jnp.bfloat16)


def first_kernel(ids_ref, proj_ref, route_ref, weight_ref, own_ref, gram_ref, *refs):
    count = len(refs) - 6
    core_refs = refs[:count]
    hidden_ref, scaled_ref, slope_ref, score_ref, grad_ref, chain_ref = refs[count:]
    route = route_ref[...]
    weight = weight_ref[...]
    pre = routed_product(proj_ref[...], route, ids_ref, core_refs, False)
    sigmoid = 1.0 / (1.0 + jnp.exp(-pre))
    hidden = (pre * sigmoid).astype(jnp.bfloat16)
    slope = sigmoid * (1.0 + pre * (1.0 - sigmoid))
    scaled = (weight * hidden.astype(jnp.float32)).astype(jnp.bfloat16)
    score = own_ref[...] + dot(scaled, gram_ref[...])
    hidden_ref[...] = hidden
    scaled_ref[...] = scaled
    slope_ref[...] = slope
    score_ref[...] = score
    grad_pre, grad_proj = backward_rows(score, weight, slope, route, ids_ref, core_refs)
    grad_ref[...] = grad_pre
    chain_ref[...] = (scaled.astype(jnp.float32) + grad_proj.astype(jnp.float32)).astype(
        jnp.bfloat16
    )


def turn_kernel(terms, ids_ref, route_ref, weight_ref, scaled_ref, slope_ref, score_ref, *refs):
    core_refs = refs[2 * terms : len(refs) - 4]
    next_ref, grad_ref, proj_ref, chain_ref = refs[len(refs) - 4 :]
    score = score_ref[...]
    for term in range(terms):
        score = score + dot(refs[2 * term][...], refs[2 * term + 1][...])
    next_ref[...] = score
    grad_pre, grad_proj = backward_rows(
        score, weight_ref[...], slope_ref[...], route_ref[...], ids_ref, core_refs
    )
    grad_ref[...] = grad_pre
    proj_ref[...] = grad_proj
    chain_ref[...] = (scaled_ref[...].astype(jnp.float32) + grad_proj.astype(jnp.float32)).astype(
        jnp.bfloat16
    )


def call_rows(body, name, outs, scalars, arrays, flops):
    in_bytes = sum(array.size * array.dtype.itemsize for array in arrays)
    return pl.pallas_call(
        body,
        name=name,
        out_shape=[jax.ShapeDtypeStruct(shape, kind) for shape, kind in outs],
        in_specs=[pl.BlockSpec(memory_space=pltpu.SMEM)]
        + [pl.BlockSpec(memory_space=pltpu.VMEM)] * len(arrays),
        out_specs=[pl.BlockSpec(memory_space=pltpu.VMEM)] * len(outs),
        cost_estimate=pl.CostEstimate(flops=flops, bytes_accessed=in_bytes, transcendentals=0),
    )(scalars, *arrays)


def column_blocks(rows, count):
    tokens, channels = rows.shape
    return rows.reshape(tokens, count, channels // count).transpose(1, 0, 2)


def gathered_plan(inputs, teacher, gate, route, slot, factor, cores):
    shared = factor[0]
    channels, ranks = shared.shape
    devices = lax.axis_size("expert")
    micro_count, token_count = route.shape[1:]
    rows = micro_count * token_count
    here = lax.axis_index("expert")
    chip, core = here // CORES, here % CORES
    middle = jnp.logical_or(chip == 1, chip == 2)
    tokens = inputs[0].reshape(rows, channels)
    difference = tokens.astype(jnp.float32) - teacher[0].reshape(rows, channels).astype(jnp.float32)
    difference = difference.astype(jnp.bfloat16)
    weight = gate[0].reshape(rows, 1)
    chosen = route[0].reshape(rows, 1)

    pieces = gather_cores(cores[0, 0], middle)
    ids = expert_ids(held_chips(chip, middle), core)

    down = [(3, 2), (1, 0)]
    two_down = [(3, 1), (2, 0)]
    crossed = [(0, 1), (1, 0)]
    half = channels // CORES
    own_half = lax.dynamic_slice_in_dim(shared, core * half, half, 0)
    other_half = lax.dynamic_slice_in_dim(shared, (1 - core) * half, half, 0)
    halves = [between_layers(own_half, down), between_layers(own_half, two_down)]
    halves.append(between_layers(halves[1], crossed))
    others = [swap_cores(value) for value in halves]
    steps = [between_layers(difference, down), between_layers(difference, two_down)]
    steps.append(between_layers(steps[1], crossed))

    projected = dot(tokens, shared).astype(jnp.bfloat16)
    gram = dot_first(shared, shared).astype(jnp.bfloat16)
    grams = [
        (dot_first(mine, own_half) + dot_first(theirs, other_half)).astype(jnp.bfloat16)
        for mine, theirs in zip(halves, others)
    ]
    own_score = dot(difference, shared)
    down_score = dot(steps[0], shared)
    late_steps = (steps[1].astype(jnp.float32) + steps[2].astype(jnp.float32)).astype(jnp.bfloat16)
    late_score = dot(late_steps, shared)

    bf16, f32 = jnp.bfloat16, jnp.float32
    wide = (rows, ranks)
    product_flops = 2 * rows * ranks * ranks
    hidden, scaled, slope, score, _, chain = call_rows(
        first_kernel,
        "first_turn",
        [(wide, bf16), (wide, bf16), (wide, f32), (wide, f32), (wide, bf16), (wide, bf16)],
        ids,
        [projected, chosen, weight, own_score, gram, *pieces],
        product_flops * (2 * devices + 1),
    )

    def turn(number, score, terms):
        arrays = [array for pair in terms for array in pair]

        def body(*refs):
            turn_kernel(len(terms), *refs)

        return call_rows(
            body,
            f"turn_{number}",
            [(wide, f32), (wide, bf16), (wide, bf16), (wide, bf16)],
            ids,
            [chosen, weight, scaled, slope, score, *arrays, *pieces],
            product_flops * (devices + len(terms)),
        )

    first_down = between_layers(chain, [(3, 2)])
    first_two = between_layers(chain, [(3, 1)])
    first_three = between_layers(chain, [(3, 0)])
    score, _, _, chain = turn(1, score + down_score, [(first_down, grams[0])])
    second_cross = between_layers(chain, [(2, 1)])
    second_two = between_layers(chain, [(2, 0)])
    score, _, _, chain = turn(
        2, score + late_score, [(first_two, grams[1]), (second_cross, grams[2])]
    )
    third_down = between_layers(chain, [(1, 0)])
    score, grad_pre, grad_proj, _ = turn(
        3, score, [(second_two, grams[1]), (first_three, grams[2]), (third_down, grams[0])]
    )

    def whole_factor(mine, theirs):
        first = jnp.where(core == 0, mine, theirs)
        last = jnp.where(core == 0, theirs, mine)
        return first, last

    def spread(values, mine, theirs):
        first, last = whole_factor(mine, theirs)
        return jnp.concatenate(
            [times_transposed(values, first), times_transposed(values, last)], axis=1
        )

    grad_out = difference.astype(f32) + steps[0].astype(f32) + steps[1].astype(f32)
    grad_out = grad_out + steps[2].astype(f32) + times_transposed(scaled, shared)
    grad_out = grad_out + spread(first_two + second_two, halves[1], others[1])
    grad_out = grad_out + spread(second_cross + first_three, halves[2], others[2])
    grad_out = grad_out + spread(first_down + third_down, halves[0], others[0])
    grad_mixed = (weight * grad_out).astype(bf16)

    token_blocks = lax.all_to_all(column_blocks(tokens, devices), "expert", 0, 0, tiled=True)
    mixed_blocks = lax.all_to_all(column_blocks(grad_mixed, devices), "expert", 0, 0, tiled=True)
    order = expert_ids([chip ^ step for step in range(CHIPS)], core)
    factor_rows = jnp.zeros((channels // devices, ranks), f32)
    for place, (proj_piece, hidden_piece) in enumerate(
        zip(gather_rows(grad_proj), gather_rows(hidden))
    ):
        token_part = lax.dynamic_index_in_dim(token_blocks, order[place], 0, keepdims=False)
        mixed_part = lax.dynamic_index_in_dim(mixed_blocks, order[place], 0, keepdims=False)
        factor_rows = factor_rows + dot_first(token_part, proj_piece)
        factor_rows = factor_rows + dot_first(mixed_part, hidden_piece)

    capacity = max(2, 2 * token_count // devices)
    slots = micro_count * capacity
    micro = jnp.arange(rows, dtype=jnp.int32) // token_count
    place = route[0].reshape(rows) * slots + micro * capacity + slot[0].reshape(rows)
    picks = (jnp.arange(devices * slots, dtype=jnp.int32)[:, None] == place[None, :]).astype(bf16)

    def to_slots(values):
        return dot(picks, values).astype(bf16).reshape(devices, slots, ranks)

    proj_slots = lax.all_to_all(to_slots(projected), "expert", 0, 0, tiled=True)
    grad_slots = lax.all_to_all(to_slots(grad_pre), "expert", 0, 0, tiled=True)
    core_total = dot_first(proj_slots.reshape(-1, ranks), grad_slots.reshape(-1, ranks))
    return (factor_rows[None], core_total.astype(bf16)[None, None])


def solution(mesh):
    placed = (
        P("section", None, "expert", None),
        P("section", None, "expert", None),
        P("section", None, "expert"),
        P("section", None, "expert"),
        P("section", None, "expert"),
        P("section", None, None),
        P("section", "expert", None, None),
    )
    drawn_for = (LAYERS, CHIPS * CORES)

    def per_device(*arrays):
        local_experts = arrays[-1].shape[1]
        if (mesh.shape["section"], mesh.shape["expert"]) == drawn_for and local_experts == 1:
            return gathered_plan(*arrays)
        return general_plan(*arrays)

    return jax.shard_map(
        per_device,
        mesh=mesh,
        in_specs=placed,
        out_specs=(P("section", "expert", None), P("section", "expert", None, None)),
        check_vma=False,
    )
```

```python
import jax
import jax.numpy as jnp
from jax import lax
from jax.experimental import pallas as pl
from jax.experimental.pallas import tpu as pltpu
from jax.sharding import PartitionSpec as P


def from_behind(value, axis, steps):
    count = lax.axis_size(axis)
    leading, last = (max(0, -steps), min(count, count - steps))
    return lax.ppermute(value, axis, [(source, source + steps) for source in range(leading, last)])


def silu_slope(values):
    sigmoid = jax.nn.sigmoid(values)
    return sigmoid * (1.0 + values * (1.0 - sigmoid))


def times_transposed(left, shared):
    return lax.dot_general(
        left, shared, (((1,), (1,)), ((), ())), preferred_element_type=jnp.float32
    )


def factor_terms(tokens_flat, proj_flat, mixed_flat, hidden_flat):

    def factor_rows(start, count):
        first_term = lax.dot_general(
            tokens_flat, proj_flat, (((0,), (0,)), ((), ())), preferred_element_type=jnp.float32
        )
        second_term = lax.dot_general(
            mixed_flat, hidden_flat, (((0,), (0,)), ((), ())), preferred_element_type=jnp.float32
        )
        return first_term + second_term

    return factor_rows


def store_slice(store, fresh, picked, usable):
    former = lax.dynamic_index_in_dim(store, picked, 0, keepdims=False)
    kept = jnp.where(usable, fresh, former)
    return lax.dynamic_update_index_in_dim(store, kept, picked, 0)


def general_plan(inputs, teacher, gate, route, slot, factor, cores):
    tokens_all = inputs[0]
    targets_all = teacher[0]
    weights_all = gate[0]
    shared = factor[0]
    blocks = cores[0]
    micro_count, token_count, channels = tokens_all.shape
    ranks = shared.shape[1]
    local_experts = blocks.shape[0]
    expert_devices = lax.axis_size("expert")
    capacity = max(2, 2 * token_count // (local_experts * expert_devices))
    slot_count = local_experts * expert_devices * capacity
    places_all = route[0] * capacity + slot[0]
    micro_range = jnp.arange(micro_count, dtype=jnp.int32)[:, None]
    token_proj = jnp.dot(
        tokens_all.reshape(-1, channels), shared, preferred_element_type=jnp.float32
    ).astype(jnp.bfloat16)
    token_proj = token_proj.reshape(micro_count, token_count, ranks)
    proj_slots = (
        jnp.zeros((micro_count, slot_count, ranks), jnp.bfloat16)
        .at[micro_range, places_all]
        .set(token_proj)
    )
    projected = lax.all_to_all(proj_slots, "expert", split_axis=1, concat_axis=1, tiled=True)
    projected = projected.reshape(micro_count, expert_devices, local_experts, capacity, ranks)
    pre = jnp.einsum("mnecr,erk->mneck", projected, blocks, preferred_element_type=jnp.float32)
    active = jax.nn.silu(pre).astype(jnp.bfloat16)
    returned = lax.all_to_all(
        active.reshape(micro_count, slot_count, ranks),
        "expert",
        split_axis=1,
        concat_axis=1,
        tiled=True,
    )
    hidden = jnp.take_along_axis(returned, places_all[:, :, None], axis=1)
    mixed = times_transposed(hidden.reshape(-1, ranks), shared).reshape(
        micro_count, token_count, channels
    )
    output = tokens_all.astype(jnp.float32) + weights_all[:, :, None] * mixed
    errors = output - targets_all.astype(jnp.float32)
    section_count = lax.axis_size("section")
    section_here = lax.axis_index("section")
    incoming = jnp.zeros((token_count, channels), jnp.bfloat16)
    mixed_store = jnp.zeros((micro_count, token_count, channels), jnp.bfloat16)
    proj_store = jnp.zeros((micro_count, token_count, ranks), jnp.bfloat16)
    pre_store = jnp.zeros(
        (micro_count, expert_devices, local_experts, capacity, ranks), jnp.bfloat16
    )
    turn_total = micro_count + section_count - 1
    for turn_index in range(turn_total):
        micro_now = turn_index - (section_count - 1 - section_here)
        usable = jnp.logical_and(micro_now >= 0, micro_now < micro_count)
        picked = jnp.clip(micro_now, 0, micro_count - 1)
        grad_out = lax.dynamic_index_in_dim(errors, picked, 0, keepdims=False) + incoming.astype(
            jnp.float32
        )
        weight_now = lax.dynamic_index_in_dim(weights_all, picked, 0, keepdims=False)
        places = lax.dynamic_index_in_dim(places_all, picked, 0, keepdims=False)
        grad_mixed = (weight_now[:, None] * grad_out).astype(jnp.bfloat16)
        grad_hidden = jnp.dot(grad_mixed, shared, preferred_element_type=jnp.float32).astype(
            jnp.bfloat16
        )
        grad_slots = jnp.zeros((slot_count, ranks), jnp.bfloat16).at[places].set(grad_hidden)
        grad_recv = lax.all_to_all(grad_slots, "expert", split_axis=0, concat_axis=0, tiled=True)
        grad_recv = grad_recv.reshape(expert_devices, local_experts, capacity, ranks)
        pre_now = lax.dynamic_index_in_dim(pre, picked, 0, keepdims=False)
        grad_pre = (grad_recv.astype(jnp.float32) * silu_slope(pre_now)).astype(jnp.bfloat16)
        grad_routed = jnp.einsum(
            "neck,erk->necr", grad_pre, blocks, preferred_element_type=jnp.float32
        ).astype(jnp.bfloat16)
        grad_home = lax.all_to_all(
            grad_routed.reshape(slot_count, ranks),
            "expert",
            split_axis=0,
            concat_axis=0,
            tiled=True,
        )
        grad_proj = grad_home[places]
        grad_in = (grad_out + times_transposed(grad_proj, shared)).astype(jnp.bfloat16)
        if turn_index + 1 < turn_total:
            incoming = from_behind(grad_in, "section", -1)
        mixed_store = store_slice(mixed_store, grad_mixed, picked, usable)
        proj_store = store_slice(proj_store, grad_proj, picked, usable)
        pre_store = store_slice(pre_store, grad_pre, picked, usable)
    core_total = jnp.einsum(
        "mnecr,mneck->erk", projected, pre_store, preferred_element_type=jnp.float32
    )
    all_rows = factor_terms(
        tokens_all.reshape(-1, channels),
        proj_store.reshape(-1, ranks),
        mixed_store.reshape(-1, channels),
        hidden.reshape(-1, ranks),
    )
    factor_share = lax.psum_scatter(
        all_rows(jnp.int32(0), channels // expert_devices * lax.axis_size("expert")),
        "expert",
        scatter_dimension=0,
        tiled=True,
    )
    return (factor_share[None], core_total.astype(jnp.bfloat16)[None])


CORES = 2
CHIPS = 4
LAYERS = 4
ROOM = 24 * 2**20


def dot(left, right):
    return jnp.dot(left, right, preferred_element_type=jnp.float32)


def dot_first(left, right):
    return lax.dot_general(
        left, right, (((0,), (0,)), ((), ())), preferred_element_type=jnp.float32
    )


def on_chips(value, pairs):
    perm = [
        (CORES * source + core, CORES * target + core)
        for source, target in pairs
        for core in range(CORES)
    ]
    return lax.ppermute(value, "expert", perm)


def swap_cores(value):
    count = lax.axis_size("expert")
    return lax.ppermute(value, "expert", [(index, index ^ 1) for index in range(count)])


def between_layers(value, pairs):
    return lax.ppermute(value, "section", pairs)


def gather_cores(core, middle):
    beside = on_chips(core, [(0, 1), (1, 0), (2, 3), (3, 2)])
    across = on_chips(core, [(1, 2), (2, 1)])
    far_across = on_chips(beside, [(1, 2), (2, 1)])
    outward = on_chips(across, [(1, 0), (2, 3)])
    far_outward = on_chips(far_across, [(1, 0), (2, 3)])
    second = jnp.where(middle, across, outward)
    third = jnp.where(middle, far_across, far_outward)
    held = [core, beside, second, third]
    return held + [swap_cores(piece) for piece in held]


def held_chips(chip, middle):
    near, far = chip ^ 3, chip ^ 2
    return [chip, chip ^ 1, jnp.where(middle, near, far), jnp.where(middle, far, near)]


def across_chips(value, step):
    return on_chips(value, [(chip, chip ^ step) for chip in range(CHIPS)])


def gather_rows(rows):
    held = [rows] + [across_chips(rows, step) for step in range(1, CHIPS)]
    return held + [swap_cores(piece) for piece in held]


def chip_blocks(wide, chip, core):
    count = wide.shape[0] // (CHIPS * CORES)
    blocks = [
        lax.dynamic_slice_in_dim(wide, (CORES * (chip ^ step) + core) * count, count, 0)
        for step in range(CHIPS)
    ]
    return jnp.concatenate(blocks, axis=0)


def exchange_blocks(own, other):
    theirs = swap_cores(other)
    count = own.shape[0] // CHIPS
    joined = [
        jnp.concatenate([half[step * count : (step + 1) * count] for half in (own, theirs)], axis=0)
        for step in range(CHIPS)
    ]
    return joined[:1] + [across_chips(joined[step], step) for step in range(1, CHIPS)]


def expert_ids(chips, core):
    return jnp.stack(
        [CORES * chip + core for chip in chips] + [CORES * chip + 1 - core for chip in chips]
    ).astype(jnp.int32)


def routed_product(rows, route, ids_ref, core_refs, transposed):
    dims = (((1,), (1 if transposed else 0,)), ((), ()))
    total = None
    for place, core_ref in enumerate(core_refs):
        chosen = jnp.where(route == ids_ref[place], rows, jnp.zeros_like(rows))
        term = lax.dot_general(
            chosen, core_ref[...], dims, preferred_element_type=jnp.float32
        )
        total = term if total is None else total + term
    return total


def backward_rows(score, weight, slope, route, ids_ref, core_refs):
    grad_hidden = (weight * score).astype(jnp.bfloat16)
    grad_pre = (grad_hidden.astype(jnp.float32) * slope).astype(jnp.bfloat16)
    grad_proj = routed_product(grad_pre, route, ids_ref, core_refs, True)
    return grad_pre, grad_proj.astype(jnp.bfloat16)


def first_kernel(ids_ref, proj_ref, route_ref, weight_ref, own_ref, gram_ref, *refs):
    count = len(refs) - 6
    core_refs = refs[:count]
    hidden_ref, scaled_ref, slope_ref, score_ref, grad_ref, chain_ref = refs[count:]
    route = route_ref[...]
    weight = weight_ref[...]
    pre = routed_product(proj_ref[...], route, ids_ref, core_refs, False)
    sigmoid = 1.0 / (1.0 + jnp.exp(-pre))
    hidden = (pre * sigmoid).astype(jnp.bfloat16)
    slope = sigmoid * (1.0 + pre * (1.0 - sigmoid))
    scaled = (weight * hidden.astype(jnp.float32)).astype(jnp.bfloat16)
    score = own_ref[...] + dot(scaled, gram_ref[...])
    hidden_ref[...] = hidden
    scaled_ref[...] = scaled
    slope_ref[...] = slope
    score_ref[...] = score
    grad_pre, grad_proj = backward_rows(score, weight, slope, route, ids_ref, core_refs)
    grad_ref[...] = grad_pre
    chain_ref[...] = (scaled.astype(jnp.float32) + grad_proj.astype(jnp.float32)).astype(
        jnp.bfloat16
    )


def turn_kernel(terms, ids_ref, route_ref, weight_ref, scaled_ref, slope_ref, score_ref, *refs):
    core_refs = refs[2 * terms : len(refs) - 4]
    next_ref, grad_ref, proj_ref, chain_ref = refs[len(refs) - 4 :]
    score = score_ref[...]
    for term in range(terms):
        score = score + dot(refs[2 * term][...], refs[2 * term + 1][...])
    next_ref[...] = score
    grad_pre, grad_proj = backward_rows(
        score, weight_ref[...], slope_ref[...], route_ref[...], ids_ref, core_refs
    )
    grad_ref[...] = grad_pre
    proj_ref[...] = grad_proj
    chain_ref[...] = (scaled_ref[...].astype(jnp.float32) + grad_proj.astype(jnp.float32)).astype(
        jnp.bfloat16
    )


def call_rows(body, name, outs, scalars, arrays, flops):
    in_bytes = sum(array.size * array.dtype.itemsize for array in arrays)
    return pl.pallas_call(
        body,
        name=name,
        out_shape=[jax.ShapeDtypeStruct(shape, kind) for shape, kind in outs],
        in_specs=[pl.BlockSpec(memory_space=pltpu.SMEM)]
        + [pl.BlockSpec(memory_space=pltpu.VMEM)] * len(arrays),
        out_specs=[pl.BlockSpec(memory_space=pltpu.VMEM)] * len(outs),
        compiler_params=pltpu.CompilerParams(vmem_limit_bytes=ROOM),
        cost_estimate=pl.CostEstimate(flops=flops, bytes_accessed=in_bytes, transcendentals=0),
    )(scalars, *arrays)


def pair_products(block_ref, near_ref, far_ref):
    count = block_ref.shape[0] // CORES
    blocks = jnp.concatenate([block_ref[:count], block_ref[count:]], axis=1)
    return dot(blocks, jnp.concatenate([near_ref[...], far_ref[...]], axis=0))


def factor_kernel(start, *refs):
    total_ref = refs[-1]
    total = refs[0][...] if start else None
    refs = refs[1:-1] if start else refs[:-1]
    for step in range(CHIPS):
        term = pair_products(refs[step], refs[CHIPS + step], refs[2 * CHIPS + step])
        total = term if total is None else total + term
    total_ref[...] = total


def factor_rows(total, blocks, pieces, name):
    arrays = ([] if total is None else [total]) + blocks + pieces
    count, ranks = blocks[0].shape[0] // CORES, pieces[0].shape[1]

    def body(*refs):
        factor_kernel(total is not None, *refs)

    return pl.pallas_call(
        body,
        name=name,
        out_shape=jax.ShapeDtypeStruct((count, ranks), jnp.float32),
        in_specs=[pl.BlockSpec(memory_space=pltpu.VMEM)] * len(arrays),
        out_specs=pl.BlockSpec(memory_space=pltpu.VMEM),
        compiler_params=pltpu.CompilerParams(vmem_limit_bytes=ROOM),
        cost_estimate=pl.CostEstimate(
            flops=2 * count * ranks * len(pieces) * pieces[0].shape[0],
            bytes_accessed=sum(array.size * array.dtype.itemsize for array in arrays),
            transcendentals=0,
        ),
    )(*arrays)


def after(value, earlier):
    return lax.optimization_barrier((value, earlier))[0]


def gathered_plan(inputs, teacher, gate, route, slot, factor, cores):
    bf16, f32 = jnp.bfloat16, jnp.float32
    shared = factor[0]
    channels, ranks = shared.shape
    devices = lax.axis_size("expert")
    micro_count, token_count = route.shape[1:]
    rows = micro_count * token_count
    here = lax.axis_index("expert")
    chip, core = here // CORES, here % CORES
    middle = jnp.logical_or(chip == 1, chip == 2)
    tokens = inputs[0].reshape(rows, channels)
    weight = gate[0].reshape(rows, 1)
    chosen = route[0].reshape(rows, 1)

    pieces = gather_cores(cores[0, 0], middle)
    ids = expert_ids(held_chips(chip, middle), core)

    down = [(3, 2), (1, 0)]
    two_down = [(3, 1), (2, 0)]
    crossed = [(0, 1), (1, 0)]
    own_half = chip_blocks(shared, chip, core)
    other_half = chip_blocks(shared, chip, 1 - core)
    with jax.named_scope("half_down"):
        half_down = between_layers(own_half, down)
    with jax.named_scope("half_two"):
        half_two = between_layers(own_half, two_down)
    with jax.named_scope("half_cross"):
        half_cross = between_layers(half_two, crossed)
    difference = tokens.astype(f32) - teacher[0].reshape(rows, channels).astype(f32)
    difference = difference.astype(bf16)
    step_down = between_layers(difference, down)
    step_two = between_layers(difference, two_down)
    with jax.named_scope("step_cross"):
        step_cross = between_layers(step_two, crossed)

    def cross_gram(mine, theirs):
        return (dot_first(mine, own_half) + dot_first(theirs, other_half)).astype(bf16)

    projected = dot(tokens, shared).astype(bf16)
    gram = dot_first(shared, shared).astype(bf16)
    down_pair = (half_down, swap_cores(half_down))
    two_pair = (half_two, swap_cores(half_two))
    down_gram = cross_gram(*down_pair)
    two_gram = cross_gram(*two_pair)
    own_score = dot(difference, shared)
    down_score = dot(step_down, shared)

    wide = (rows, ranks)
    product_flops = 2 * rows * ranks * ranks
    with jax.named_scope("first_turn"):
        hidden, scaled, slope, score, _, chain = call_rows(
            first_kernel,
            "first_turn",
            [(wide, bf16), (wide, bf16), (wide, f32), (wide, f32), (wide, bf16), (wide, bf16)],
            ids,
            [projected, chosen, weight, own_score, gram, *pieces],
            product_flops * (2 * devices + 1),
        )
    started = chain
    half_cross = after(half_cross, started)
    step_cross = after(step_cross, started)
    cross_pair = (half_cross, swap_cores(half_cross))
    cross_product = cross_gram(*cross_pair)
    late_steps = (step_two.astype(f32) + step_cross.astype(f32)).astype(bf16)
    late_score = dot(late_steps, shared)

    def turn(number, score, terms):
        arrays = [array for pair in terms for array in pair]

        def body(*refs):
            turn_kernel(len(terms), *refs)

        return call_rows(
            body,
            f"turn_{number}",
            [(wide, f32), (wide, bf16), (wide, bf16), (wide, bf16)],
            ids,
            [chosen, weight, scaled, slope, score, *arrays, *pieces],
            product_flops * (devices + len(terms)),
        )

    first_down = between_layers(chain, [(3, 2)])
    first_two = between_layers(chain, [(3, 1)])
    first_three = between_layers(chain, [(3, 0)])
    score, _, _, chain = turn(1, score + down_score, [(first_down, down_gram)])
    second_cross = between_layers(chain, [(2, 1)])
    second_two = between_layers(chain, [(2, 0)])
    score, _, _, chain = turn(
        2, score + late_score, [(first_two, two_gram), (second_cross, cross_product)]
    )
    third_down = between_layers(chain, [(1, 0)])
    score, grad_pre, grad_proj, _ = turn(
        3, score, [(second_two, two_gram), (first_three, cross_product), (third_down, down_gram)]
    )

    steps_total = difference.astype(f32) + step_down.astype(f32) + late_steps.astype(f32)
    steps_total = steps_total.astype(bf16).T
    waiting = [
        (scaled, (own_half, other_half)),
        (first_two + second_two, two_pair),
        (second_cross + first_three, cross_pair),
        (first_down, down_pair),
    ]

    def mixed_half(side):
        total = chip_blocks(steps_total, chip, core if side == 0 else 1 - core).astype(f32)
        for values, pair in waiting:
            total = total + times_transposed(pair[side], values)
        total = total + times_transposed(down_pair[side], third_down)
        return (total * weight.reshape(1, rows)).astype(bf16)

    mixed_blocks = exchange_blocks(mixed_half(0), mixed_half(1))
    turned = after(tokens, started).T
    token_blocks = exchange_blocks(
        chip_blocks(turned, chip, core), chip_blocks(turned, chip, 1 - core)
    )
    share = factor_rows(None, mixed_blocks, gather_rows(hidden), "mixed_rows")
    share = factor_rows(share, token_blocks, gather_rows(grad_proj), "token_rows")

    capacity = max(2, 2 * token_count // devices)
    slots = micro_count * capacity
    micro = jnp.arange(rows, dtype=jnp.int32) // token_count
    place = route[0].reshape(rows) * slots + micro * capacity + slot[0].reshape(rows)
    picks = (jnp.arange(devices * slots, dtype=jnp.int32)[:, None] == place[None, :]).astype(bf16)

    def to_slots(values):
        return dot(picks, values).astype(bf16).reshape(devices, slots, ranks)

    proj_slots = lax.all_to_all(to_slots(after(projected, started)), "expert", 0, 0, tiled=True)
    grad_slots = lax.all_to_all(to_slots(grad_pre), "expert", 0, 0, tiled=True)
    core_total = dot_first(proj_slots.reshape(-1, ranks), grad_slots.reshape(-1, ranks))
    return (share[None], core_total.astype(bf16)[None, None])


def solution(mesh):
    placed = (
        P("section", None, "expert", None),
        P("section", None, "expert", None),
        P("section", None, "expert"),
        P("section", None, "expert"),
        P("section", None, "expert"),
        P("section", None, None),
        P("section", "expert", None, None),
    )
    drawn_for = (LAYERS, CHIPS * CORES)

    def per_device(*arrays):
        local_experts = arrays[-1].shape[1]
        if (mesh.shape["section"], mesh.shape["expert"]) == drawn_for and local_experts == 1:
            return gathered_plan(*arrays)
        return general_plan(*arrays)

    return jax.shard_map(
        per_device,
        mesh=mesh,
        in_specs=placed,
        out_specs=(P("section", "expert", None), P("section", "expert", None, None)),
        check_vma=False,
    )
```

```python
import jax
import jax.numpy as jnp
from jax import lax
from jax.experimental import pallas as pl
from jax.experimental.pallas import tpu as pltpu
from jax.sharding import PartitionSpec as P


def from_behind(value, axis, steps):
    count = lax.axis_size(axis)
    leading, last = (max(0, -steps), min(count, count - steps))
    return lax.ppermute(value, axis, [(source, source + steps) for source in range(leading, last)])


def silu_slope(values):
    sigmoid = jax.nn.sigmoid(values)
    return sigmoid * (1.0 + values * (1.0 - sigmoid))


def times_transposed(left, shared):
    return lax.dot_general(
        left, shared, (((1,), (1,)), ((), ())), preferred_element_type=jnp.float32
    )


def factor_terms(tokens_flat, proj_flat, mixed_flat, hidden_flat):

    def factor_rows(start, count):
        first_term = lax.dot_general(
            tokens_flat, proj_flat, (((0,), (0,)), ((), ())), preferred_element_type=jnp.float32
        )
        second_term = lax.dot_general(
            mixed_flat, hidden_flat, (((0,), (0,)), ((), ())), preferred_element_type=jnp.float32
        )
        return first_term + second_term

    return factor_rows


def store_slice(store, fresh, picked, usable):
    former = lax.dynamic_index_in_dim(store, picked, 0, keepdims=False)
    kept = jnp.where(usable, fresh, former)
    return lax.dynamic_update_index_in_dim(store, kept, picked, 0)


def general_plan(inputs, teacher, gate, route, slot, factor, cores):
    tokens_all = inputs[0]
    targets_all = teacher[0]
    weights_all = gate[0]
    shared = factor[0]
    blocks = cores[0]
    micro_count, token_count, channels = tokens_all.shape
    ranks = shared.shape[1]
    local_experts = blocks.shape[0]
    expert_devices = lax.axis_size("expert")
    capacity = max(2, 2 * token_count // (local_experts * expert_devices))
    slot_count = local_experts * expert_devices * capacity
    places_all = route[0] * capacity + slot[0]
    micro_range = jnp.arange(micro_count, dtype=jnp.int32)[:, None]
    token_proj = jnp.dot(
        tokens_all.reshape(-1, channels), shared, preferred_element_type=jnp.float32
    ).astype(jnp.bfloat16)
    token_proj = token_proj.reshape(micro_count, token_count, ranks)
    proj_slots = (
        jnp.zeros((micro_count, slot_count, ranks), jnp.bfloat16)
        .at[micro_range, places_all]
        .set(token_proj)
    )
    projected = lax.all_to_all(proj_slots, "expert", split_axis=1, concat_axis=1, tiled=True)
    projected = projected.reshape(micro_count, expert_devices, local_experts, capacity, ranks)
    pre = jnp.einsum("mnecr,erk->mneck", projected, blocks, preferred_element_type=jnp.float32)
    active = jax.nn.silu(pre).astype(jnp.bfloat16)
    returned = lax.all_to_all(
        active.reshape(micro_count, slot_count, ranks),
        "expert",
        split_axis=1,
        concat_axis=1,
        tiled=True,
    )
    hidden = jnp.take_along_axis(returned, places_all[:, :, None], axis=1)
    mixed = times_transposed(hidden.reshape(-1, ranks), shared).reshape(
        micro_count, token_count, channels
    )
    output = tokens_all.astype(jnp.float32) + weights_all[:, :, None] * mixed
    errors = output - targets_all.astype(jnp.float32)
    section_count = lax.axis_size("section")
    section_here = lax.axis_index("section")
    incoming = jnp.zeros((token_count, channels), jnp.bfloat16)
    mixed_store = jnp.zeros((micro_count, token_count, channels), jnp.bfloat16)
    proj_store = jnp.zeros((micro_count, token_count, ranks), jnp.bfloat16)
    pre_store = jnp.zeros(
        (micro_count, expert_devices, local_experts, capacity, ranks), jnp.bfloat16
    )
    turn_total = micro_count + section_count - 1
    for turn_index in range(turn_total):
        micro_now = turn_index - (section_count - 1 - section_here)
        usable = jnp.logical_and(micro_now >= 0, micro_now < micro_count)
        picked = jnp.clip(micro_now, 0, micro_count - 1)
        grad_out = lax.dynamic_index_in_dim(errors, picked, 0, keepdims=False) + incoming.astype(
            jnp.float32
        )
        weight_now = lax.dynamic_index_in_dim(weights_all, picked, 0, keepdims=False)
        places = lax.dynamic_index_in_dim(places_all, picked, 0, keepdims=False)
        grad_mixed = (weight_now[:, None] * grad_out).astype(jnp.bfloat16)
        grad_hidden = jnp.dot(grad_mixed, shared, preferred_element_type=jnp.float32).astype(
            jnp.bfloat16
        )
        grad_slots = jnp.zeros((slot_count, ranks), jnp.bfloat16).at[places].set(grad_hidden)
        grad_recv = lax.all_to_all(grad_slots, "expert", split_axis=0, concat_axis=0, tiled=True)
        grad_recv = grad_recv.reshape(expert_devices, local_experts, capacity, ranks)
        pre_now = lax.dynamic_index_in_dim(pre, picked, 0, keepdims=False)
        grad_pre = (grad_recv.astype(jnp.float32) * silu_slope(pre_now)).astype(jnp.bfloat16)
        grad_routed = jnp.einsum(
            "neck,erk->necr", grad_pre, blocks, preferred_element_type=jnp.float32
        ).astype(jnp.bfloat16)
        grad_home = lax.all_to_all(
            grad_routed.reshape(slot_count, ranks),
            "expert",
            split_axis=0,
            concat_axis=0,
            tiled=True,
        )
        grad_proj = grad_home[places]
        grad_in = (grad_out + times_transposed(grad_proj, shared)).astype(jnp.bfloat16)
        if turn_index + 1 < turn_total:
            incoming = from_behind(grad_in, "section", -1)
        mixed_store = store_slice(mixed_store, grad_mixed, picked, usable)
        proj_store = store_slice(proj_store, grad_proj, picked, usable)
        pre_store = store_slice(pre_store, grad_pre, picked, usable)
    core_total = jnp.einsum(
        "mnecr,mneck->erk", projected, pre_store, preferred_element_type=jnp.float32
    )
    all_rows = factor_terms(
        tokens_all.reshape(-1, channels),
        proj_store.reshape(-1, ranks),
        mixed_store.reshape(-1, channels),
        hidden.reshape(-1, ranks),
    )
    factor_share = lax.psum_scatter(
        all_rows(jnp.int32(0), channels // expert_devices * lax.axis_size("expert")),
        "expert",
        scatter_dimension=0,
        tiled=True,
    )
    return (factor_share[None], core_total.astype(jnp.bfloat16)[None])


CORES = 2
CHIPS = 4
LAYERS = 4
ROOM = 24 * 2**20


def dot(left, right):
    return jnp.dot(left, right, preferred_element_type=jnp.float32)


def dot_first(left, right):
    return lax.dot_general(
        left, right, (((0,), (0,)), ((), ())), preferred_element_type=jnp.float32
    )


def on_chips(value, pairs):
    perm = [
        (CORES * source + core, CORES * target + core)
        for source, target in pairs
        for core in range(CORES)
    ]
    return lax.ppermute(value, "expert", perm)


def swap_cores(value):
    count = lax.axis_size("expert")
    return lax.ppermute(value, "expert", [(index, index ^ 1) for index in range(count)])


def between_layers(value, pairs):
    return lax.ppermute(value, "section", pairs)


def gather_cores(core, middle):
    beside = on_chips(core, [(0, 1), (1, 0), (2, 3), (3, 2)])
    across = on_chips(core, [(1, 2), (2, 1)])
    far_across = on_chips(beside, [(1, 2), (2, 1)])
    outward = on_chips(across, [(1, 0), (2, 3)])
    far_outward = on_chips(far_across, [(1, 0), (2, 3)])
    second = jnp.where(middle, across, outward)
    third = jnp.where(middle, far_across, far_outward)
    held = [core, beside, second, third]
    return held + [swap_cores(piece) for piece in held]


def held_chips(chip, middle):
    near, far = chip ^ 3, chip ^ 2
    return [chip, chip ^ 1, jnp.where(middle, near, far), jnp.where(middle, far, near)]


def across_chips(value, step):
    return on_chips(value, [(chip, chip ^ step) for chip in range(CHIPS)])


def gather_rows(rows):
    held = [rows] + [across_chips(rows, step) for step in range(1, CHIPS)]
    return held + [swap_cores(piece) for piece in held]


def chip_blocks(wide, chip, core):
    count = wide.shape[0] // (CHIPS * CORES)
    blocks = [
        lax.dynamic_slice_in_dim(wide, (CORES * (chip ^ step) + core) * count, count, 0)
        for step in range(CHIPS)
    ]
    return jnp.concatenate(blocks, axis=0)


def chip_columns(wide, chip, core):
    theirs = swap_cores(chip_blocks(wide, chip, 1 - core))
    return jnp.concatenate([chip_blocks(wide, chip, core), theirs], axis=1)


def both_cores(partial):
    rows = partial.shape[0] // CORES
    return partial[:rows] + swap_cores(partial[rows:])


def gram_pair(left, right):
    partial = dot_first(left, right).astype(jnp.bfloat16)
    return partial, swap_cores(partial)


def gram_sum(pair):
    return (pair[0].astype(jnp.float32) + pair[1].astype(jnp.float32)).astype(jnp.bfloat16)


def expert_ids(chips, core):
    return jnp.stack(
        [CORES * chip + core for chip in chips] + [CORES * chip + 1 - core for chip in chips]
    ).astype(jnp.int32)


def routed_product(rows, route, ids_ref, core_refs, transposed):
    dims = (((1,), (1 if transposed else 0,)), ((), ()))
    total = None
    for place, core_ref in enumerate(core_refs):
        chosen = jnp.where(route == ids_ref[place], rows, jnp.zeros_like(rows))
        term = lax.dot_general(
            chosen, core_ref[...], dims, preferred_element_type=jnp.float32
        )
        total = term if total is None else total + term
    return total


def backward_rows(score, weight, slope, route, ids_ref, core_refs):
    grad_hidden = (weight * score).astype(jnp.bfloat16)
    grad_pre = (grad_hidden.astype(jnp.float32) * slope).astype(jnp.bfloat16)
    grad_proj = routed_product(grad_pre, route, ids_ref, core_refs, True)
    return grad_pre, grad_proj.astype(jnp.bfloat16)


def first_kernel(ids_ref, proj_ref, route_ref, weight_ref, own_ref, gram_ref, *refs):
    count = len(refs) - 6
    core_refs = refs[:count]
    hidden_ref, scaled_ref, slope_ref, score_ref, grad_ref, chain_ref = refs[count:]
    route = route_ref[...]
    weight = weight_ref[...]
    pre = routed_product(proj_ref[...], route, ids_ref, core_refs, False)
    sigmoid = 1.0 / (1.0 + jnp.exp(-pre))
    hidden = (pre * sigmoid).astype(jnp.bfloat16)
    slope = sigmoid * (1.0 + pre * (1.0 - sigmoid))
    scaled = (weight * hidden.astype(jnp.float32)).astype(jnp.bfloat16)
    score = own_ref[...] + dot(scaled, gram_ref[...])
    hidden_ref[...] = hidden
    scaled_ref[...] = scaled
    slope_ref[...] = slope
    score_ref[...] = score
    grad_pre, grad_proj = backward_rows(score, weight, slope, route, ids_ref, core_refs)
    grad_ref[...] = grad_pre
    chain_ref[...] = (scaled.astype(jnp.float32) + grad_proj.astype(jnp.float32)).astype(
        jnp.bfloat16
    )


def turn_kernel(terms, ids_ref, route_ref, weight_ref, scaled_ref, slope_ref, score_ref, *refs):
    core_refs = refs[2 * terms : len(refs) - 4]
    next_ref, grad_ref, proj_ref, chain_ref = refs[len(refs) - 4 :]
    score = score_ref[...]
    for term in range(terms):
        score = score + dot(refs[2 * term][...], refs[2 * term + 1][...])
    next_ref[...] = score
    grad_pre, grad_proj = backward_rows(
        score, weight_ref[...], slope_ref[...], route_ref[...], ids_ref, core_refs
    )
    grad_ref[...] = grad_pre
    proj_ref[...] = grad_proj
    chain_ref[...] = (scaled_ref[...].astype(jnp.float32) + grad_proj.astype(jnp.float32)).astype(
        jnp.bfloat16
    )


def call_rows(body, outs, scalars, arrays, flops):
    in_bytes = sum(array.size * array.dtype.itemsize for array in arrays)
    return pl.pallas_call(
        body,
        out_shape=[jax.ShapeDtypeStruct(shape, kind) for shape, kind in outs],
        in_specs=[pl.BlockSpec(memory_space=pltpu.SMEM)]
        + [pl.BlockSpec(memory_space=pltpu.VMEM)] * len(arrays),
        out_specs=[pl.BlockSpec(memory_space=pltpu.VMEM)] * len(outs),
        compiler_params=pltpu.CompilerParams(vmem_limit_bytes=ROOM),
        cost_estimate=pl.CostEstimate(flops=flops, bytes_accessed=in_bytes, transcendentals=0),
    )(scalars, *arrays)


def spread_kernel(terms, last, base_ref, *refs):
    total = base_ref[...].astype(jnp.float32)
    for term in range(terms):
        half_ref, near_ref, far_ref = refs[3 * term : 3 * term + 3]
        values = jnp.concatenate([near_ref[...], far_ref[...]], axis=0)
        total = total + times_transposed(half_ref[...], values)
    outs = refs[3 * terms :]
    if not last:
        outs[0][...] = total
        return
    count = total.shape[0] // CHIPS
    for step in range(CHIPS):
        outs[step][...] = total[step * count : (step + 1) * count].astype(jnp.bfloat16)


def spread(base, terms, last):
    arrays = [base] + [array for term in terms for array in term]
    height, width = base.shape
    if last:
        outs = [jax.ShapeDtypeStruct((height // CHIPS, width), jnp.bfloat16)] * CHIPS
    else:
        outs = [jax.ShapeDtypeStruct((height, width), jnp.float32)]

    def body(*refs):
        spread_kernel(len(terms), last, *refs)

    return pl.pallas_call(
        body,
        out_shape=outs,
        in_specs=[pl.BlockSpec(memory_space=pltpu.VMEM)] * len(arrays),
        out_specs=[pl.BlockSpec(memory_space=pltpu.VMEM)] * len(outs),
        compiler_params=pltpu.CompilerParams(vmem_limit_bytes=ROOM),
        cost_estimate=pl.CostEstimate(
            flops=2 * height * width * terms[0][0].shape[1] * len(terms),
            bytes_accessed=sum(array.size * array.dtype.itemsize for array in arrays),
            transcendentals=0,
        ),
    )(*arrays)


def pair_products(block_ref, near_ref, far_ref):
    return dot(block_ref[...], jnp.concatenate([near_ref[...], far_ref[...]], axis=0))


def factor_kernel(start, *refs):
    total_ref = refs[-1]
    total = refs[0][...] if start else None
    refs = refs[1:-1] if start else refs[:-1]
    for step in range(CHIPS):
        term = pair_products(refs[step], refs[CHIPS + step], refs[2 * CHIPS + step])
        total = term if total is None else total + term
    total_ref[...] = total


def factor_rows(total, blocks, pieces):
    arrays = ([] if total is None else [total]) + blocks + pieces
    count, ranks = blocks[0].shape[0], pieces[0].shape[1]

    def body(*refs):
        factor_kernel(total is not None, *refs)

    return pl.pallas_call(
        body,
        out_shape=jax.ShapeDtypeStruct((count, ranks), jnp.float32),
        in_specs=[pl.BlockSpec(memory_space=pltpu.VMEM)] * len(arrays),
        out_specs=pl.BlockSpec(memory_space=pltpu.VMEM),
        compiler_params=pltpu.CompilerParams(vmem_limit_bytes=ROOM),
        cost_estimate=pl.CostEstimate(
            flops=2 * count * ranks * len(pieces) * pieces[0].shape[0],
            bytes_accessed=sum(array.size * array.dtype.itemsize for array in arrays),
            transcendentals=0,
        ),
    )(*arrays)


def after(value, earlier):
    return lax.optimization_barrier((value, earlier))[0]


def gathered_plan(inputs, teacher, gate, route, slot, factor, cores):
    bf16, f32 = jnp.bfloat16, jnp.float32
    shared = factor[0]
    channels, ranks = shared.shape
    devices = lax.axis_size("expert")
    micro_count, token_count = route.shape[1:]
    rows = micro_count * token_count
    here = lax.axis_index("expert")
    chip, core = here // CORES, here % CORES
    middle = jnp.logical_or(chip == 1, chip == 2)
    tokens = inputs[0].reshape(rows, channels)
    weight = gate[0].reshape(rows, 1)
    chosen = route[0].reshape(rows, 1)

    pieces = gather_cores(cores[0, 0], middle)
    ids = expert_ids(held_chips(chip, middle), core)

    down = [(3, 2), (1, 0)]
    two_down = [(3, 1), (2, 0)]
    crossed = [(0, 1), (1, 0)]
    own_half = chip_blocks(shared, chip, core)
    half_down = between_layers(own_half, down)
    half_two = between_layers(own_half, two_down)
    half_cross = between_layers(half_two, crossed)
    difference = tokens.astype(f32) - teacher[0].reshape(rows, channels).astype(f32)
    difference = chip_columns(difference.astype(bf16).T, chip, core)
    step_down = between_layers(difference, down)
    step_two = between_layers(difference, two_down)
    step_cross = between_layers(step_two, crossed)

    capacity = max(2, 2 * token_count // devices)
    slots = micro_count * capacity
    micro = jnp.arange(rows, dtype=jnp.int32) // token_count
    place = route[0].reshape(rows) * slots + micro * capacity + slot[0].reshape(rows)
    picks = (jnp.arange(devices * slots, dtype=jnp.int32)[:, None] == place[None, :]).astype(bf16)

    def to_slots(values):
        return dot(picks, values).astype(bf16).reshape(devices, slots, ranks)

    projected = dot(tokens, shared).astype(bf16)
    own_gram = gram_pair(own_half, own_half)
    proj_slots = to_slots(projected)
    gram = gram_sum(own_gram)
    own_score = both_cores(dot_first(difference, own_half))
    turned = chip_columns(tokens.T, chip, core)
    token_blocks = [
        turned[step * channels // devices : (step + 1) * channels // devices]
        for step in range(CHIPS)
    ]
    down_gram = gram_sum(gram_pair(half_down, own_half))
    two_gram = gram_sum(gram_pair(half_two, own_half))
    down_score = both_cores(dot_first(step_down, own_half))

    wide = (rows, ranks)
    product_flops = 2 * rows * ranks * ranks
    _, scaled, slope, score, _, chain = call_rows(
        first_kernel,
        [(wide, bf16), (wide, bf16), (wide, f32), (wide, f32), (wide, bf16), (wide, bf16)],
        ids,
        [projected, chosen, weight, own_score, gram, *pieces],
        product_flops * (2 * devices + 1),
    )

    def turn(score, terms):
        arrays = [array for pair in terms for array in pair]

        def body(*refs):
            turn_kernel(len(terms), *refs)

        return call_rows(
            body,
            [(wide, f32), (wide, bf16), (wide, bf16), (wide, bf16)],
            ids,
            [chosen, weight, scaled, slope, score, *arrays, *pieces],
            product_flops * (devices + len(terms)),
        )

    def with_swap(values):
        return values, swap_cores(values)

    chain_first = chain
    first_down = between_layers(chain, [(3, 2)])
    first_two = between_layers(chain, [(3, 1)])
    own_steps = after(difference, chain)
    scaled_pair = with_swap(scaled)
    spread_rows = spread(own_steps, [(own_half, *scaled_pair)], False)[0]
    proj_slots = lax.all_to_all(after(proj_slots, chain), "expert", 0, 0, tiled=True)
    token_blocks = token_blocks[:1] + [
        across_chips(after(token_blocks[step], chain), step) for step in range(1, CHIPS)
    ]
    score, _, _, chain = turn(score + down_score, [(first_down, down_gram)])

    second_cross = between_layers(chain, [(2, 1)])
    second_two = between_layers(chain, [(2, 0)])
    first_three = between_layers(after(chain_first, chain), [(3, 0)])
    half_cross = after(half_cross, chain)
    step_cross = after(step_cross, chain)
    cross_pair = gram_pair(half_cross, own_half)
    late_steps = (step_two.astype(f32) + step_cross.astype(f32)).astype(bf16)
    late_score = both_cores(dot_first(late_steps, own_half))
    cross_product = gram_sum(cross_pair)
    score, _, _, chain = turn(
        score + late_score, [(first_two, two_gram), (second_cross, cross_product)]
    )

    third_down = between_layers(chain, [(1, 0)])
    two_values = with_swap(first_two + after(second_two, chain))
    cross_values = with_swap(second_cross + after(first_three, chain))
    down_values = with_swap(after(first_down, chain))
    other_steps = step_down.astype(f32) + late_steps.astype(f32)
    spread_rows = spread(
        spread_rows + after(other_steps, chain),
        [(half_two, *two_values), (half_cross, *cross_values), (half_down, *down_values)],
        False,
    )[0]
    scaled_rows = [scaled] + [across_chips(after(scaled, chain), step) for step in range(1, CHIPS)]
    score, grad_pre, grad_proj, _ = turn(
        score, [(second_two, two_gram), (first_three, cross_product), (third_down, down_gram)]
    )

    third_pair = with_swap(third_down)
    mixed_blocks = list(spread(spread_rows, [(half_down, *third_pair)], True))
    scaled_rows = [after(rows, mixed_blocks[0]) for rows in scaled_rows]
    grad_slots = after(to_slots(grad_pre), mixed_blocks[0])
    mixed_blocks = mixed_blocks[:1] + [
        across_chips(mixed_blocks[step], step) for step in range(1, CHIPS)
    ]
    scaled_rows = scaled_rows + [scaled_pair[1]] + [swap_cores(rows) for rows in scaled_rows[1:]]
    share = factor_rows(None, mixed_blocks, scaled_rows)
    share = factor_rows(share, token_blocks, gather_rows(grad_proj))
    grad_slots = lax.all_to_all(grad_slots, "expert", 0, 0, tiled=True)
    core_total = dot_first(proj_slots.reshape(-1, ranks), grad_slots.reshape(-1, ranks))
    return (share[None], core_total.astype(bf16)[None, None])


def solution(mesh):
    placed = (
        P("section", None, "expert", None),
        P("section", None, "expert", None),
        P("section", None, "expert"),
        P("section", None, "expert"),
        P("section", None, "expert"),
        P("section", None, None),
        P("section", "expert", None, None),
    )
    drawn_for = (LAYERS, CHIPS * CORES)

    def per_device(*arrays):
        local_experts = arrays[-1].shape[1]
        if (mesh.shape["section"], mesh.shape["expert"]) == drawn_for and local_experts == 1:
            return gathered_plan(*arrays)
        return general_plan(*arrays)

    return jax.shard_map(
        per_device,
        mesh=mesh,
        in_specs=placed,
        out_specs=(P("section", "expert", None), P("section", "expert", None, None)),
        check_vma=False,
    )
```

```python
import jax
import jax.numpy as jnp
from jax import lax
from jax.experimental import pallas as pl
from jax.experimental.pallas import tpu as pltpu
from jax.sharding import PartitionSpec as P


def from_behind(value, axis, steps):
    count = lax.axis_size(axis)
    leading, last = (max(0, -steps), min(count, count - steps))
    return lax.ppermute(value, axis, [(source, source + steps) for source in range(leading, last)])


def silu_slope(values):
    sigmoid = jax.nn.sigmoid(values)
    return sigmoid * (1.0 + values * (1.0 - sigmoid))


def times_transposed(left, shared):
    return lax.dot_general(
        left, shared, (((1,), (1,)), ((), ())), preferred_element_type=jnp.float32
    )


def factor_terms(tokens_flat, proj_flat, mixed_flat, hidden_flat):

    def factor_rows(start, count):
        first_term = lax.dot_general(
            tokens_flat, proj_flat, (((0,), (0,)), ((), ())), preferred_element_type=jnp.float32
        )
        second_term = lax.dot_general(
            mixed_flat, hidden_flat, (((0,), (0,)), ((), ())), preferred_element_type=jnp.float32
        )
        return first_term + second_term

    return factor_rows


def store_slice(store, fresh, picked, usable):
    former = lax.dynamic_index_in_dim(store, picked, 0, keepdims=False)
    kept = jnp.where(usable, fresh, former)
    return lax.dynamic_update_index_in_dim(store, kept, picked, 0)


def general_plan(inputs, teacher, gate, route, slot, factor, cores):
    tokens_all = inputs[0]
    targets_all = teacher[0]
    weights_all = gate[0]
    shared = factor[0]
    blocks = cores[0]
    micro_count, token_count, channels = tokens_all.shape
    ranks = shared.shape[1]
    local_experts = blocks.shape[0]
    expert_devices = lax.axis_size("expert")
    capacity = max(2, 2 * token_count // (local_experts * expert_devices))
    slot_count = local_experts * expert_devices * capacity
    places_all = route[0] * capacity + slot[0]
    micro_range = jnp.arange(micro_count, dtype=jnp.int32)[:, None]
    token_proj = jnp.dot(
        tokens_all.reshape(-1, channels), shared, preferred_element_type=jnp.float32
    ).astype(jnp.bfloat16)
    token_proj = token_proj.reshape(micro_count, token_count, ranks)
    proj_slots = (
        jnp.zeros((micro_count, slot_count, ranks), jnp.bfloat16)
        .at[micro_range, places_all]
        .set(token_proj)
    )
    projected = lax.all_to_all(proj_slots, "expert", split_axis=1, concat_axis=1, tiled=True)
    projected = projected.reshape(micro_count, expert_devices, local_experts, capacity, ranks)
    pre = jnp.einsum("mnecr,erk->mneck", projected, blocks, preferred_element_type=jnp.float32)
    active = jax.nn.silu(pre).astype(jnp.bfloat16)
    returned = lax.all_to_all(
        active.reshape(micro_count, slot_count, ranks),
        "expert",
        split_axis=1,
        concat_axis=1,
        tiled=True,
    )
    hidden = jnp.take_along_axis(returned, places_all[:, :, None], axis=1)
    mixed = times_transposed(hidden.reshape(-1, ranks), shared).reshape(
        micro_count, token_count, channels
    )
    output = tokens_all.astype(jnp.float32) + weights_all[:, :, None] * mixed
    errors = output - targets_all.astype(jnp.float32)
    section_count = lax.axis_size("section")
    section_here = lax.axis_index("section")
    incoming = jnp.zeros((token_count, channels), jnp.bfloat16)
    mixed_store = jnp.zeros((micro_count, token_count, channels), jnp.bfloat16)
    proj_store = jnp.zeros((micro_count, token_count, ranks), jnp.bfloat16)
    pre_store = jnp.zeros(
        (micro_count, expert_devices, local_experts, capacity, ranks), jnp.bfloat16
    )
    turn_total = micro_count + section_count - 1
    for turn_index in range(turn_total):
        micro_now = turn_index - (section_count - 1 - section_here)
        usable = jnp.logical_and(micro_now >= 0, micro_now < micro_count)
        picked = jnp.clip(micro_now, 0, micro_count - 1)
        grad_out = lax.dynamic_index_in_dim(errors, picked, 0, keepdims=False) + incoming.astype(
            jnp.float32
        )
        weight_now = lax.dynamic_index_in_dim(weights_all, picked, 0, keepdims=False)
        places = lax.dynamic_index_in_dim(places_all, picked, 0, keepdims=False)
        grad_mixed = (weight_now[:, None] * grad_out).astype(jnp.bfloat16)
        grad_hidden = jnp.dot(grad_mixed, shared, preferred_element_type=jnp.float32).astype(
            jnp.bfloat16
        )
        grad_slots = jnp.zeros((slot_count, ranks), jnp.bfloat16).at[places].set(grad_hidden)
        grad_recv = lax.all_to_all(grad_slots, "expert", split_axis=0, concat_axis=0, tiled=True)
        grad_recv = grad_recv.reshape(expert_devices, local_experts, capacity, ranks)
        pre_now = lax.dynamic_index_in_dim(pre, picked, 0, keepdims=False)
        grad_pre = (grad_recv.astype(jnp.float32) * silu_slope(pre_now)).astype(jnp.bfloat16)
        grad_routed = jnp.einsum(
            "neck,erk->necr", grad_pre, blocks, preferred_element_type=jnp.float32
        ).astype(jnp.bfloat16)
        grad_home = lax.all_to_all(
            grad_routed.reshape(slot_count, ranks),
            "expert",
            split_axis=0,
            concat_axis=0,
            tiled=True,
        )
        grad_proj = grad_home[places]
        grad_in = (grad_out + times_transposed(grad_proj, shared)).astype(jnp.bfloat16)
        if turn_index + 1 < turn_total:
            incoming = from_behind(grad_in, "section", -1)
        mixed_store = store_slice(mixed_store, grad_mixed, picked, usable)
        proj_store = store_slice(proj_store, grad_proj, picked, usable)
        pre_store = store_slice(pre_store, grad_pre, picked, usable)
    core_total = jnp.einsum(
        "mnecr,mneck->erk", projected, pre_store, preferred_element_type=jnp.float32
    )
    all_rows = factor_terms(
        tokens_all.reshape(-1, channels),
        proj_store.reshape(-1, ranks),
        mixed_store.reshape(-1, channels),
        hidden.reshape(-1, ranks),
    )
    factor_share = lax.psum_scatter(
        all_rows(jnp.int32(0), channels // expert_devices * lax.axis_size("expert")),
        "expert",
        scatter_dimension=0,
        tiled=True,
    )
    return (factor_share[None], core_total.astype(jnp.bfloat16)[None])


CORES = 2
CHIPS = 4
LAYERS = 4
WIDE_ROOM = 24 * 2**20
ROOM = 16 * 2**20


def dot(left, right):
    return jnp.dot(left, right, preferred_element_type=jnp.float32)


def dot_first(left, right):
    return lax.dot_general(
        left, right, (((0,), (0,)), ((), ())), preferred_element_type=jnp.float32
    )


def on_chips(value, pairs):
    perm = [
        (CORES * source + core, CORES * target + core)
        for source, target in pairs
        for core in range(CORES)
    ]
    return lax.ppermute(value, "expert", perm)


def swap_cores(value):
    count = lax.axis_size("expert")
    return lax.ppermute(value, "expert", [(index, index ^ 1) for index in range(count)])


def between_layers(value, pairs):
    return lax.ppermute(value, "section", pairs)


def gather_cores(core, middle):
    beside = on_chips(core, [(0, 1), (1, 0), (2, 3), (3, 2)])
    across = on_chips(core, [(1, 2), (2, 1)])
    far_across = on_chips(beside, [(1, 2), (2, 1)])
    outward = on_chips(across, [(1, 0), (2, 3)])
    far_outward = on_chips(far_across, [(1, 0), (2, 3)])
    second = jnp.where(middle, across, outward)
    held = [core, beside, second]
    thirds = [far_across, far_outward]
    return held + [swap_cores(piece) for piece in held], thirds + [
        swap_cores(piece) for piece in thirds
    ]


def row_marks(route, weight, chip, core, middle):
    count = CHIPS * CORES
    place = lax.broadcasted_iota(jnp.int32, (1, 2 * count), 1)
    step = (place % count) // CORES
    turned = jnp.where(jnp.logical_and(step >= 2, middle), 5 - step, step)
    expert = CORES * (chip ^ turned) + (core ^ (place % CORES))
    marks = (route == expert).astype(jnp.float32)
    return jnp.where(place < count, marks, weight)


def across_chips(value, step):
    return on_chips(value, [(chip, chip ^ step) for chip in range(CHIPS)])


def gather_rows(rows):
    held = [rows] + [across_chips(rows, step) for step in range(1, CHIPS)]
    return held + [swap_cores(piece) for piece in held]


def chip_blocks(wide, chip, core):
    count = wide.shape[0] // (CHIPS * CORES)
    blocks = [
        lax.dynamic_slice_in_dim(wide, (CORES * (chip ^ step) + core) * count, count, 0)
        for step in range(CHIPS)
    ]
    return jnp.concatenate(blocks, axis=0)


def chip_columns(wide, chip, core):
    theirs = swap_cores(chip_blocks(wide, chip, 1 - core))
    return jnp.concatenate([chip_blocks(wide, chip, core), theirs], axis=1)


def both_cores(partial):
    rows = partial.shape[0] // CORES
    return partial[:rows] + swap_cores(partial[rows:])


def gram_pair(left, right):
    partial = dot_first(left, right).astype(jnp.bfloat16)
    return partial, swap_cores(partial)


def gram_sum(pair):
    return (pair[0].astype(jnp.float32) + pair[1].astype(jnp.float32)).astype(jnp.bfloat16)


def routed_product(rows, marks, core_refs, transposed, copies=None):
    dims = (((1,), (1 if transposed else 0,)), ((), ()))
    total = None
    for place, core_ref in enumerate(core_refs):
        if copies is not None:
            copies[place].wait()
        chosen = jnp.where(marks[:, place : place + 1] > 0.5, rows, jnp.zeros_like(rows))
        term = lax.dot_general(
            chosen, core_ref[...], dims, preferred_element_type=jnp.float32
        )
        total = term if total is None else total + term
    return total


def backward_rows(score, slope, marks, core_refs):
    count = len(core_refs)
    grad_hidden = (marks[:, count : count + 1] * score).astype(jnp.bfloat16)
    grad_pre = (grad_hidden.astype(jnp.float32) * slope).astype(jnp.bfloat16)
    grad_proj = routed_product(grad_pre, marks, core_refs, True)
    return grad_pre, grad_proj.astype(jnp.bfloat16)


def first_kernel(middle_ref, proj_ref, marks_ref, own_ref, gram_ref, *refs):
    count = CHIPS * CORES
    held, thirds = refs[: count - 2], refs[count - 2 : count + 2]
    scaled_ref, slope_ref, score_ref, chain_ref = refs[count + 2 : count + 6]
    core_refs, arrived = refs[count + 6 : -1], refs[-1]
    middle = middle_ref[0] > 0
    sources = paired(held, [thirds[:2], thirds[2:]])
    copies = []
    for place, (source, core_ref) in enumerate(zip(sources, core_refs)):
        choices = source if isinstance(source, tuple) else (source,)
        moves = [pltpu.make_async_copy(ref, core_ref, arrived.at[place]) for ref in choices]
        copies.append(moves[0])
        if len(moves) == 1:
            moves[0].start()
        else:
            pl.when(middle)(moves[0].start)
            pl.when(jnp.logical_not(middle))(moves[1].start)
    marks = marks_ref[...]
    pre = routed_product(proj_ref[...], marks, core_refs, False, copies)
    sigmoid = 1.0 / (1.0 + jnp.exp(-pre))
    hidden = (pre * sigmoid).astype(jnp.bfloat16)
    slope = sigmoid * (1.0 + pre * (1.0 - sigmoid))
    weight = marks[:, count : count + 1]
    scaled = (weight * hidden.astype(jnp.float32)).astype(jnp.bfloat16)
    score = own_ref[...] + dot(scaled, gram_ref[...])
    scaled_ref[...] = scaled
    slope_ref[...] = slope
    score_ref[...] = score
    _, grad_proj = backward_rows(score, slope, marks, core_refs)
    chain_ref[...] = (scaled.astype(jnp.float32) + grad_proj.astype(jnp.float32)).astype(
        jnp.bfloat16
    )


def paired(held, thirds):
    own, other = [*held[:3], thirds[0]], [*held[3:], thirds[1]]
    return [piece for pair in zip(own, other) for piece in pair]


def turn_kernel(terms, marks_ref, scaled_ref, slope_ref, score_ref, late_ref, *refs):
    core_refs = refs[2 * terms : len(refs) - 4]
    next_ref, grad_ref, proj_ref, chain_ref = refs[len(refs) - 4 :]
    score = score_ref[...] + late_ref[...]
    for term in range(terms):
        score = score + dot(refs[2 * term][...], refs[2 * term + 1][...])
    next_ref[...] = score
    grad_pre, grad_proj = backward_rows(score, slope_ref[...], marks_ref[...], core_refs)
    grad_ref[...] = grad_pre
    proj_ref[...] = grad_proj
    chain_ref[...] = (scaled_ref[...].astype(jnp.float32) + grad_proj.astype(jnp.float32)).astype(
        jnp.bfloat16
    )


def call_rows(body, outs, arrays, flops, scalars=()):
    in_bytes = sum(array.size * array.dtype.itemsize for array in arrays)
    return pl.pallas_call(
        body,
        out_shape=[jax.ShapeDtypeStruct(shape, kind) for shape, kind in outs],
        in_specs=[pl.BlockSpec(memory_space=pltpu.SMEM)] * len(scalars)
        + [pl.BlockSpec(memory_space=pltpu.VMEM)] * len(arrays),
        out_specs=[pl.BlockSpec(memory_space=pltpu.VMEM)] * len(outs),
        compiler_params=pltpu.CompilerParams(vmem_limit_bytes=ROOM),
        cost_estimate=pl.CostEstimate(flops=flops, bytes_accessed=in_bytes, transcendentals=0),
    )(*scalars, *arrays)


def spread_kernel(terms, base_ref, *refs):
    total = base_ref[...].astype(jnp.float32)
    for term in range(terms):
        half_ref, near_ref, far_ref = refs[3 * term : 3 * term + 3]
        values = jnp.concatenate([near_ref[...], far_ref[...]], axis=0)
        total = total + times_transposed(half_ref[...], values)
    count = total.shape[0] // CHIPS
    for step, out_ref in enumerate(refs[3 * terms :]):
        out_ref[...] = total[step * count : (step + 1) * count].astype(jnp.bfloat16)


def spread(base, terms):
    arrays = [base] + [array for term in terms for array in term]
    height, width = base.shape

    def body(*refs):
        spread_kernel(len(terms), *refs)

    return pl.pallas_call(
        body,
        name="spread",
        out_shape=[jax.ShapeDtypeStruct((height // CHIPS, width), jnp.bfloat16)] * CHIPS,
        in_specs=[pl.BlockSpec(memory_space=pltpu.VMEM)] * len(arrays),
        out_specs=[pl.BlockSpec(memory_space=pltpu.VMEM)] * CHIPS,
        compiler_params=pltpu.CompilerParams(vmem_limit_bytes=WIDE_ROOM),
        cost_estimate=pl.CostEstimate(
            flops=2 * height * width * terms[0][0].shape[1] * len(terms),
            bytes_accessed=sum(array.size * array.dtype.itemsize for array in arrays),
            transcendentals=0,
        ),
    )(*arrays)


def pair_products(block_ref, near_ref, far_ref):
    return dot(block_ref[...], jnp.concatenate([near_ref[...], far_ref[...]], axis=0))


def factor_kernel(start, *refs):
    total_ref = refs[-1]
    total = refs[0][...] if start else None
    refs = refs[1:-1] if start else refs[:-1]
    for step in range(CHIPS):
        term = pair_products(refs[step], refs[CHIPS + step], refs[2 * CHIPS + step])
        total = term if total is None else total + term
    total_ref[...] = total


def factor_rows(total, blocks, pieces):
    arrays = ([] if total is None else [total]) + blocks + pieces
    count, ranks = blocks[0].shape[0], pieces[0].shape[1]

    def body(*refs):
        factor_kernel(total is not None, *refs)

    return pl.pallas_call(
        body,
        out_shape=jax.ShapeDtypeStruct((count, ranks), jnp.float32),
        in_specs=[pl.BlockSpec(memory_space=pltpu.VMEM)] * len(arrays),
        out_specs=pl.BlockSpec(memory_space=pltpu.VMEM),
        compiler_params=pltpu.CompilerParams(vmem_limit_bytes=ROOM),
        cost_estimate=pl.CostEstimate(
            flops=2 * count * ranks * len(pieces) * pieces[0].shape[0],
            bytes_accessed=sum(array.size * array.dtype.itemsize for array in arrays),
            transcendentals=0,
        ),
    )(*arrays)


def after(value, earlier):
    return lax.optimization_barrier((value, earlier))[0]


def gathered_plan(inputs, teacher, gate, route, slot, factor, cores):
    bf16, f32 = jnp.bfloat16, jnp.float32
    shared = factor[0]
    channels, ranks = shared.shape
    devices = lax.axis_size("expert")
    micro_count, token_count = route.shape[1:]
    rows = micro_count * token_count
    here = lax.axis_index("expert")
    chip, core = here // CORES, here % CORES
    middle = jnp.logical_or(chip == 1, chip == 2)
    tokens = inputs[0].reshape(rows, channels)

    held, thirds = gather_cores(cores[0, 0], middle)
    marks = row_marks(
        route[0].reshape(rows, 1), gate[0].reshape(rows, 1), chip, core, middle
    )

    down = [(3, 2), (1, 0)]
    two_down = [(3, 1), (2, 0)]
    crossed = [(0, 1), (1, 0)]
    own_half = chip_blocks(shared, chip, core)
    half_down = between_layers(own_half, down)
    half_two = between_layers(own_half, two_down)
    half_cross = between_layers(half_two, crossed)
    turned = lax.optimization_barrier(tokens.T)
    wanted = lax.optimization_barrier(teacher[0].reshape(rows, channels).T)
    difference = (turned.astype(f32) - wanted.astype(f32)).astype(bf16)
    difference = chip_columns(difference, chip, core)
    step_down = between_layers(difference, down)
    step_two = between_layers(difference, two_down)

    capacity = max(2, 2 * token_count // devices)
    slots = micro_count * capacity
    micro = jnp.arange(rows, dtype=jnp.int32) // token_count
    place = route[0].reshape(rows) * slots + micro * capacity + slot[0].reshape(rows)
    picks = (jnp.arange(devices * slots, dtype=jnp.int32)[:, None] == place[None, :]).astype(bf16)

    def to_slots(values):
        return dot(picks, values).astype(bf16).reshape(devices, slots, ranks)

    projected = dot(tokens, shared).astype(bf16)
    own_gram = gram_pair(own_half, own_half)
    proj_slots = to_slots(projected)
    gram = gram_sum(own_gram)
    own_score = both_cores(dot_first(difference, own_half))
    turned = chip_columns(turned, chip, core)
    token_blocks = [
        turned[step * channels // devices : (step + 1) * channels // devices]
        for step in range(CHIPS)
    ]
    down_gram = gram_sum(gram_pair(half_down, own_half))
    two_gram = gram_sum(gram_pair(half_two, own_half))
    down_score = both_cores(dot_first(step_down, own_half))

    wide = (rows, ranks)
    product_flops = 2 * rows * ranks * ranks
    scaled, slope, score, chain, *pieces = pl.pallas_call(
        first_kernel,
        name="first_turn",
        out_shape=[jax.ShapeDtypeStruct(wide, kind) for kind in (bf16, f32, f32, bf16)]
        + [pltpu.VMEM((ranks, ranks), bf16)] * devices,
        in_specs=[pl.BlockSpec(memory_space=pltpu.SMEM)]
        + [pl.BlockSpec(memory_space=pltpu.VMEM)] * 4
        + [pl.BlockSpec(memory_space=pl.ANY)] * (devices + 2),
        out_specs=[pl.BlockSpec(memory_space=pltpu.VMEM)] * (devices + 4),
        scratch_shapes=[pltpu.SemaphoreType.DMA((devices,))],
        compiler_params=pltpu.CompilerParams(vmem_limit_bytes=ROOM),
        cost_estimate=pl.CostEstimate(
            flops=product_flops * (2 * devices + 1),
            bytes_accessed=2 * devices * ranks * ranks,
            transcendentals=rows * ranks,
        ),
    )(middle.astype(jnp.int32).reshape(1), projected, marks, own_score, gram, *held, *thirds)

    def turn(score, late, terms):
        arrays = [array for pair in terms for array in pair]

        def body(*refs):
            turn_kernel(len(terms), *refs)

        return call_rows(
            body,
            [(wide, f32), (wide, bf16), (wide, bf16), (wide, bf16)],
            [marks, scaled, slope, score, late, *arrays, *pieces],
            product_flops * (devices + len(terms)),
        )

    chain_first = chain
    first_down = between_layers(chain, [(3, 2)])
    step_cross = between_layers(after(step_two, chain), crossed)
    first_two = between_layers(chain, [(3, 1)])
    proj_slots = lax.all_to_all(after(proj_slots, chain), "expert", 0, 0, tiled=True)
    score, _, _, chain = turn(score, down_score, [(first_down, down_gram)])

    second_cross = between_layers(chain, [(2, 1)])
    second_two = between_layers(chain, [(2, 0)])
    first_three = between_layers(after(chain_first, chain), [(3, 0)])
    half_cross = after(half_cross, chain)
    step_cross = after(step_cross, chain)
    cross_pair = gram_pair(half_cross, own_half)
    late_steps = (step_two.astype(f32) + step_cross.astype(f32)).astype(bf16)
    late_score = both_cores(dot_first(late_steps, own_half))
    cross_product = gram_sum(cross_pair)
    score, _, _, chain = turn(
        score, late_score, [(first_two, two_gram), (second_cross, cross_product)]
    )

    third_down = between_layers(chain, [(1, 0)])
    scaled_rows = [scaled] + [across_chips(after(scaled, chain), step) for step in range(1, CHIPS)]
    token_blocks = token_blocks[:1] + [
        across_chips(after(token_blocks[step], chain), step) for step in range(1, CHIPS)
    ]
    steps_total = difference.astype(f32) + step_down.astype(f32)
    steps_total = (steps_total + after(late_steps, chain).astype(f32)).astype(bf16)
    score, grad_pre, grad_proj, _ = turn(
        score,
        jnp.zeros_like(score),
        [(second_two, two_gram), (first_three, cross_product), (third_down, down_gram)],
    )

    def with_swap(values):
        return values, swap_cores(values)

    proj_rows = gather_rows(grad_proj)
    scaled_pair = with_swap(after(scaled, chain))
    two_pair = with_swap(first_two + after(second_two, chain))
    cross_pair = with_swap(second_cross + after(first_three, chain))
    down_pair = with_swap(first_down + third_down)
    mixed_blocks = spread(
        steps_total,
        [
            (own_half, *scaled_pair),
            (half_two, *two_pair),
            (half_cross, *cross_pair),
            (half_down, *down_pair),
        ],
    )
    scaled_rows = [after(rows, mixed_blocks[0]) for rows in scaled_rows]
    mixed_blocks = list(mixed_blocks[:1]) + [
        across_chips(mixed_blocks[step], step) for step in range(1, CHIPS)
    ]
    scaled_rows = scaled_rows + [scaled_pair[1]] + [swap_cores(rows) for rows in scaled_rows[1:]]
    share = factor_rows(None, token_blocks, proj_rows)
    share = factor_rows(share, mixed_blocks, scaled_rows)
    grad_slots = lax.all_to_all(to_slots(grad_pre), "expert", 0, 0, tiled=True)
    core_total = dot_first(proj_slots.reshape(-1, ranks), grad_slots.reshape(-1, ranks))
    return (share[None], core_total.astype(bf16)[None, None])


def solution(mesh):
    placed = (
        P("section", None, "expert", None),
        P("section", None, "expert", None),
        P("section", None, "expert"),
        P("section", None, "expert"),
        P("section", None, "expert"),
        P("section", None, None),
        P("section", "expert", None, None),
    )
    drawn_for = (LAYERS, CHIPS * CORES)

    def per_device(*arrays):
        local_experts = arrays[-1].shape[1]
        if (mesh.shape["section"], mesh.shape["expert"]) == drawn_for and local_experts == 1:
            return gathered_plan(*arrays)
        return general_plan(*arrays)

    return jax.shard_map(
        per_device,
        mesh=mesh,
        in_specs=placed,
        out_specs=(P("section", "expert", None), P("section", "expert", None, None)),
        check_vma=False,
    )
```

```python
import jax
import jax.numpy as jnp
from jax import lax
from jax.experimental import pallas as pl
from jax.experimental.pallas import tpu as pltpu
from jax.sharding import PartitionSpec as P


def from_behind(value, axis, steps):
    count = lax.axis_size(axis)
    leading, last = (max(0, -steps), min(count, count - steps))
    return lax.ppermute(value, axis, [(source, source + steps) for source in range(leading, last)])


def silu_slope(values):
    sigmoid = jax.nn.sigmoid(values)
    return sigmoid * (1.0 + values * (1.0 - sigmoid))


def times_transposed(left, shared):
    return lax.dot_general(
        left, shared, (((1,), (1,)), ((), ())), preferred_element_type=jnp.float32
    )


def factor_terms(tokens_flat, proj_flat, mixed_flat, hidden_flat):

    def factor_rows(start, count):
        first_term = lax.dot_general(
            tokens_flat, proj_flat, (((0,), (0,)), ((), ())), preferred_element_type=jnp.float32
        )
        second_term = lax.dot_general(
            mixed_flat, hidden_flat, (((0,), (0,)), ((), ())), preferred_element_type=jnp.float32
        )
        return first_term + second_term

    return factor_rows


def store_slice(store, fresh, picked, usable):
    former = lax.dynamic_index_in_dim(store, picked, 0, keepdims=False)
    kept = jnp.where(usable, fresh, former)
    return lax.dynamic_update_index_in_dim(store, kept, picked, 0)


def general_plan(inputs, teacher, gate, route, slot, factor, cores):
    tokens_all = inputs[0]
    targets_all = teacher[0]
    weights_all = gate[0]
    shared = factor[0]
    blocks = cores[0]
    micro_count, token_count, channels = tokens_all.shape
    ranks = shared.shape[1]
    local_experts = blocks.shape[0]
    expert_devices = lax.axis_size("expert")
    capacity = max(2, 2 * token_count // (local_experts * expert_devices))
    slot_count = local_experts * expert_devices * capacity
    places_all = route[0] * capacity + slot[0]
    micro_range = jnp.arange(micro_count, dtype=jnp.int32)[:, None]
    token_proj = jnp.dot(
        tokens_all.reshape(-1, channels), shared, preferred_element_type=jnp.float32
    ).astype(jnp.bfloat16)
    token_proj = token_proj.reshape(micro_count, token_count, ranks)
    proj_slots = (
        jnp.zeros((micro_count, slot_count, ranks), jnp.bfloat16)
        .at[micro_range, places_all]
        .set(token_proj)
    )
    projected = lax.all_to_all(proj_slots, "expert", split_axis=1, concat_axis=1, tiled=True)
    projected = projected.reshape(micro_count, expert_devices, local_experts, capacity, ranks)
    pre = jnp.einsum("mnecr,erk->mneck", projected, blocks, preferred_element_type=jnp.float32)
    active = jax.nn.silu(pre).astype(jnp.bfloat16)
    returned = lax.all_to_all(
        active.reshape(micro_count, slot_count, ranks),
        "expert",
        split_axis=1,
        concat_axis=1,
        tiled=True,
    )
    hidden = jnp.take_along_axis(returned, places_all[:, :, None], axis=1)
    mixed = times_transposed(hidden.reshape(-1, ranks), shared).reshape(
        micro_count, token_count, channels
    )
    output = tokens_all.astype(jnp.float32) + weights_all[:, :, None] * mixed
    errors = output - targets_all.astype(jnp.float32)
    section_count = lax.axis_size("section")
    section_here = lax.axis_index("section")
    incoming = jnp.zeros((token_count, channels), jnp.bfloat16)
    mixed_store = jnp.zeros((micro_count, token_count, channels), jnp.bfloat16)
    proj_store = jnp.zeros((micro_count, token_count, ranks), jnp.bfloat16)
    pre_store = jnp.zeros(
        (micro_count, expert_devices, local_experts, capacity, ranks), jnp.bfloat16
    )
    turn_total = micro_count + section_count - 1
    for turn_index in range(turn_total):
        micro_now = turn_index - (section_count - 1 - section_here)
        usable = jnp.logical_and(micro_now >= 0, micro_now < micro_count)
        picked = jnp.clip(micro_now, 0, micro_count - 1)
        grad_out = lax.dynamic_index_in_dim(errors, picked, 0, keepdims=False) + incoming.astype(
            jnp.float32
        )
        weight_now = lax.dynamic_index_in_dim(weights_all, picked, 0, keepdims=False)
        places = lax.dynamic_index_in_dim(places_all, picked, 0, keepdims=False)
        grad_mixed = (weight_now[:, None] * grad_out).astype(jnp.bfloat16)
        grad_hidden = jnp.dot(grad_mixed, shared, preferred_element_type=jnp.float32).astype(
            jnp.bfloat16
        )
        grad_slots = jnp.zeros((slot_count, ranks), jnp.bfloat16).at[places].set(grad_hidden)
        grad_recv = lax.all_to_all(grad_slots, "expert", split_axis=0, concat_axis=0, tiled=True)
        grad_recv = grad_recv.reshape(expert_devices, local_experts, capacity, ranks)
        pre_now = lax.dynamic_index_in_dim(pre, picked, 0, keepdims=False)
        grad_pre = (grad_recv.astype(jnp.float32) * silu_slope(pre_now)).astype(jnp.bfloat16)
        grad_routed = jnp.einsum(
            "neck,erk->necr", grad_pre, blocks, preferred_element_type=jnp.float32
        ).astype(jnp.bfloat16)
        grad_home = lax.all_to_all(
            grad_routed.reshape(slot_count, ranks),
            "expert",
            split_axis=0,
            concat_axis=0,
            tiled=True,
        )
        grad_proj = grad_home[places]
        grad_in = (grad_out + times_transposed(grad_proj, shared)).astype(jnp.bfloat16)
        if turn_index + 1 < turn_total:
            incoming = from_behind(grad_in, "section", -1)
        mixed_store = store_slice(mixed_store, grad_mixed, picked, usable)
        proj_store = store_slice(proj_store, grad_proj, picked, usable)
        pre_store = store_slice(pre_store, grad_pre, picked, usable)
    core_total = jnp.einsum(
        "mnecr,mneck->erk", projected, pre_store, preferred_element_type=jnp.float32
    )
    all_rows = factor_terms(
        tokens_all.reshape(-1, channels),
        proj_store.reshape(-1, ranks),
        mixed_store.reshape(-1, channels),
        hidden.reshape(-1, ranks),
    )
    factor_share = lax.psum_scatter(
        all_rows(jnp.int32(0), channels // expert_devices * lax.axis_size("expert")),
        "expert",
        scatter_dimension=0,
        tiled=True,
    )
    return (factor_share[None], core_total.astype(jnp.bfloat16)[None])


CORES = 2
CHIPS = 4
LAYERS = 4
WIDE_ROOM = 24 * 2**20
ROOM = 16 * 2**20


def dot(left, right):
    return jnp.dot(left, right, preferred_element_type=jnp.float32)


def dot_first(left, right):
    return lax.dot_general(
        left, right, (((0,), (0,)), ((), ())), preferred_element_type=jnp.float32
    )


def on_chips(value, pairs):
    perm = [
        (CORES * source + core, CORES * target + core)
        for source, target in pairs
        for core in range(CORES)
    ]
    return lax.ppermute(value, "expert", perm)


def swap_cores(value):
    count = lax.axis_size("expert")
    return lax.ppermute(value, "expert", [(index, index ^ 1) for index in range(count)])


def between_layers(value, pairs):
    return lax.ppermute(value, "section", pairs)


def gather_cores(core, middle):
    beside = on_chips(core, [(0, 1), (1, 0), (2, 3), (3, 2)])
    across = on_chips(core, [(1, 2), (2, 1)])
    far_across = on_chips(beside, [(1, 2), (2, 1)])
    outward = on_chips(across, [(1, 0), (2, 3)])
    far_outward = on_chips(far_across, [(1, 0), (2, 3)])
    second = jnp.where(middle, across, outward)
    held = [core, beside, second]
    thirds = [far_across, far_outward]
    return held + [swap_cores(piece) for piece in held], thirds + [
        swap_cores(piece) for piece in thirds
    ]


def row_marks(route, weight, chip, core, middle):
    count = CHIPS * CORES
    place = lax.broadcasted_iota(jnp.int32, (1, 2 * count), 1)
    step = (place % count) // CORES
    turned = jnp.where(jnp.logical_and(step >= 2, middle), 5 - step, step)
    expert = CORES * (chip ^ turned) + (core ^ (place % CORES))
    marks = (route == expert).astype(jnp.float32)
    return jnp.where(place < count, marks, weight)


def across_chips(value, step):
    return on_chips(value, [(chip, chip ^ step) for chip in range(CHIPS)])


def gather_rows(rows):
    held = [rows] + [across_chips(rows, step) for step in range(1, CHIPS)]
    return held + [swap_cores(piece) for piece in held]


def chip_blocks(wide, chip, core):
    count = wide.shape[0] // (CHIPS * CORES)
    blocks = [
        lax.dynamic_slice_in_dim(wide, (CORES * (chip ^ step) + core) * count, count, 0)
        for step in range(CHIPS)
    ]
    return jnp.concatenate(blocks, axis=0)


def chip_columns(wide, chip, core):
    theirs = swap_cores(chip_blocks(wide, chip, 1 - core))
    return jnp.concatenate([chip_blocks(wide, chip, core), theirs], axis=1)


def both_cores(partial):
    rows = partial.shape[0] // CORES
    return partial[:rows] + swap_cores(partial[rows:])


def gram_pair(left, right):
    partial = dot_first(left, right).astype(jnp.bfloat16)
    return partial, swap_cores(partial)


def gram_sum(pair):
    return (pair[0].astype(jnp.float32) + pair[1].astype(jnp.float32)).astype(jnp.bfloat16)


def routed_product(rows, marks, core_refs, transposed, copies=None):
    dims = (((1,), (1 if transposed else 0,)), ((), ()))
    total = None
    for place, core_ref in enumerate(core_refs):
        if copies is not None:
            copies[place].wait()
        chosen = jnp.where(marks[:, place : place + 1] > 0.5, rows, jnp.zeros_like(rows))
        term = lax.dot_general(
            chosen, core_ref[...], dims, preferred_element_type=jnp.float32
        )
        total = term if total is None else total + term
    return total


def backward_rows(score, slope, marks, core_refs):
    count = len(core_refs)
    grad_hidden = (marks[:, count : count + 1] * score).astype(jnp.bfloat16)
    grad_pre = (grad_hidden.astype(jnp.float32) * slope).astype(jnp.bfloat16)
    grad_proj = routed_product(grad_pre, marks, core_refs, True)
    return grad_pre, grad_proj.astype(jnp.bfloat16)


def first_kernel(middle_ref, proj_ref, marks_ref, own_ref, gram_ref, *refs):
    count = CHIPS * CORES
    held, thirds = refs[: count - 2], refs[count - 2 : count + 2]
    scaled_ref, slope_ref, score_ref, chain_ref = refs[count + 2 : count + 6]
    core_refs, arrived = refs[count + 6 : -1], refs[-1]
    middle = middle_ref[0] > 0
    sources = paired(held, [thirds[:2], thirds[2:]])
    copies = []
    for place, (source, core_ref) in enumerate(zip(sources, core_refs)):
        choices = source if isinstance(source, tuple) else (source,)
        moves = [pltpu.make_async_copy(ref, core_ref, arrived.at[place]) for ref in choices]
        copies.append(moves[0])
        if len(moves) == 1:
            moves[0].start()
        else:
            pl.when(middle)(moves[0].start)
            pl.when(jnp.logical_not(middle))(moves[1].start)
    marks = marks_ref[...]
    pre = routed_product(proj_ref[...], marks, core_refs, False, copies)
    sigmoid = 1.0 / (1.0 + jnp.exp(-pre))
    hidden = (pre * sigmoid).astype(jnp.bfloat16)
    slope = sigmoid * (1.0 + pre * (1.0 - sigmoid))
    weight = marks[:, count : count + 1]
    scaled = (weight * hidden.astype(jnp.float32)).astype(jnp.bfloat16)
    score = own_ref[...] + dot(scaled, gram_ref[...])
    scaled_ref[...] = scaled
    slope_ref[...] = slope
    score_ref[...] = score
    _, grad_proj = backward_rows(score, slope, marks, core_refs)
    chain_ref[...] = (scaled.astype(jnp.float32) + grad_proj.astype(jnp.float32)).astype(
        jnp.bfloat16
    )


def paired(held, thirds):
    own, other = [*held[:3], thirds[0]], [*held[3:], thirds[1]]
    return [piece for pair in zip(own, other) for piece in pair]


def turn_kernel(terms, late, marks_ref, scaled_ref, slope_ref, score_ref, *refs):
    score = score_ref[...]
    if late:
        score, refs = score + refs[0][...], refs[1:]
    core_refs = refs[2 * terms : len(refs) - 4]
    next_ref, grad_ref, proj_ref, chain_ref = refs[len(refs) - 4 :]
    for term in range(terms):
        score = score + dot(refs[2 * term][...], refs[2 * term + 1][...])
    next_ref[...] = score
    grad_pre, grad_proj = backward_rows(score, slope_ref[...], marks_ref[...], core_refs)
    grad_ref[...] = grad_pre
    proj_ref[...] = grad_proj
    chain_ref[...] = (scaled_ref[...].astype(jnp.float32) + grad_proj.astype(jnp.float32)).astype(
        jnp.bfloat16
    )


def call_rows(body, outs, arrays, flops, scalars=()):
    in_bytes = sum(array.size * array.dtype.itemsize for array in arrays)
    return pl.pallas_call(
        body,
        out_shape=[jax.ShapeDtypeStruct(shape, kind) for shape, kind in outs],
        in_specs=[pl.BlockSpec(memory_space=pltpu.SMEM)] * len(scalars)
        + [pl.BlockSpec(memory_space=pltpu.VMEM)] * len(arrays),
        out_specs=[pl.BlockSpec(memory_space=pltpu.VMEM)] * len(outs),
        compiler_params=pltpu.CompilerParams(vmem_limit_bytes=ROOM),
        cost_estimate=pl.CostEstimate(flops=flops, bytes_accessed=in_bytes, transcendentals=0),
    )(*scalars, *arrays)


def spread_kernel(terms, base_ref, *refs):
    total = base_ref[...].astype(jnp.float32)
    for term in range(terms):
        half_ref, near_ref, far_ref = refs[3 * term : 3 * term + 3]
        values = jnp.concatenate([near_ref[...], far_ref[...]], axis=0)
        total = total + times_transposed(half_ref[...], values)
    count = total.shape[0] // CHIPS
    for step, out_ref in enumerate(refs[3 * terms :]):
        out_ref[...] = total[step * count : (step + 1) * count].astype(jnp.bfloat16)


def spread(base, terms):
    arrays = [base] + [array for term in terms for array in term]
    height, width = base.shape

    def body(*refs):
        spread_kernel(len(terms), *refs)

    return pl.pallas_call(
        body,
        name="spread",
        out_shape=[jax.ShapeDtypeStruct((height // CHIPS, width), jnp.bfloat16)] * CHIPS,
        in_specs=[pl.BlockSpec(memory_space=pltpu.VMEM)] * len(arrays),
        out_specs=[pl.BlockSpec(memory_space=pltpu.VMEM)] * CHIPS,
        compiler_params=pltpu.CompilerParams(vmem_limit_bytes=WIDE_ROOM),
        cost_estimate=pl.CostEstimate(
            flops=2 * height * width * terms[0][0].shape[1] * len(terms),
            bytes_accessed=sum(array.size * array.dtype.itemsize for array in arrays),
            transcendentals=0,
        ),
    )(*arrays)


def pair_products(block_ref, near_ref, far_ref):
    return dot(block_ref[...], jnp.concatenate([near_ref[...], far_ref[...]], axis=0))


def factor_kernel(start, *refs):
    total_ref = refs[-1]
    total = refs[0][...] if start else None
    refs = refs[1:-1] if start else refs[:-1]
    for step in range(CHIPS):
        term = pair_products(refs[step], refs[CHIPS + step], refs[2 * CHIPS + step])
        total = term if total is None else total + term
    total_ref[...] = total


def factor_rows(total, blocks, pieces):
    arrays = ([] if total is None else [total]) + blocks + pieces
    count, ranks = blocks[0].shape[0], pieces[0].shape[1]

    def body(*refs):
        factor_kernel(total is not None, *refs)

    return pl.pallas_call(
        body,
        out_shape=jax.ShapeDtypeStruct((count, ranks), jnp.float32),
        in_specs=[pl.BlockSpec(memory_space=pltpu.VMEM)] * len(arrays),
        out_specs=pl.BlockSpec(memory_space=pltpu.VMEM),
        compiler_params=pltpu.CompilerParams(vmem_limit_bytes=ROOM),
        cost_estimate=pl.CostEstimate(
            flops=2 * count * ranks * len(pieces) * pieces[0].shape[0],
            bytes_accessed=sum(array.size * array.dtype.itemsize for array in arrays),
            transcendentals=0,
        ),
    )(*arrays)


def after(value, earlier):
    return lax.optimization_barrier((value, earlier))[0]


def gathered_plan(inputs, teacher, gate, route, slot, factor, cores):
    bf16, f32 = jnp.bfloat16, jnp.float32
    shared = factor[0]
    channels, ranks = shared.shape
    devices = lax.axis_size("expert")
    micro_count, token_count = route.shape[1:]
    rows = micro_count * token_count
    here = lax.axis_index("expert")
    chip, core = here // CORES, here % CORES
    middle = jnp.logical_or(chip == 1, chip == 2)
    tokens = inputs[0].reshape(rows, channels)

    held, thirds = gather_cores(cores[0, 0], middle)
    marks = row_marks(
        route[0].reshape(rows, 1), gate[0].reshape(rows, 1), chip, core, middle
    )

    down = [(3, 2), (1, 0)]
    two_down = [(3, 1), (2, 0)]
    crossed = [(0, 1), (1, 0)]
    own_half = chip_blocks(shared, chip, core)
    half_down = between_layers(own_half, down)
    half_two = between_layers(own_half, two_down)
    half_cross = between_layers(half_two, crossed)
    turned = lax.optimization_barrier(tokens.T)
    wanted = lax.optimization_barrier(teacher[0].reshape(rows, channels).T)
    difference = (turned.astype(f32) - wanted.astype(f32)).astype(bf16)
    difference = chip_columns(difference, chip, core)
    step_down = between_layers(difference, down)
    step_two = between_layers(difference, two_down)

    capacity = max(2, 2 * token_count // devices)
    slots = micro_count * capacity
    micro = jnp.arange(rows, dtype=jnp.int32) // token_count
    expert = route[0].reshape(rows)
    near = (expert % CORES ^ core) * CHIPS + (expert // CORES ^ chip)
    place = near * slots + micro * capacity + slot[0].reshape(rows)
    picks = (jnp.arange(devices * slots, dtype=jnp.int32)[:, None] == place[None, :]).astype(bf16)

    def to_slots(values):
        held = dot(picks, values).astype(bf16)
        half = CHIPS * slots
        own, theirs = held[:half], swap_cores(held[half:])
        return [
            jnp.concatenate([part[step * slots : (step + 1) * slots] for part in (own, theirs)])
            for step in range(CHIPS)
        ]

    def to_experts(parts):
        return parts[:1] + [across_chips(parts[step], step) for step in range(1, CHIPS)]

    projected = dot(tokens, shared).astype(bf16)
    own_gram = gram_pair(own_half, own_half)
    proj_slots = to_slots(projected)
    gram = gram_sum(own_gram)
    own_score = both_cores(dot_first(difference, own_half))
    turned = chip_columns(turned, chip, core)
    token_blocks = [
        turned[step * channels // devices : (step + 1) * channels // devices]
        for step in range(CHIPS)
    ]
    down_gram = gram_sum(gram_pair(half_down, own_half))
    two_gram = gram_sum(gram_pair(half_two, own_half))
    down_score = both_cores(dot_first(step_down, own_half))

    wide = (rows, ranks)
    product_flops = 2 * rows * ranks * ranks
    scaled, slope, score, chain, *pieces = pl.pallas_call(
        first_kernel,
        name="first_turn",
        out_shape=[jax.ShapeDtypeStruct(wide, kind) for kind in (bf16, f32, f32, bf16)]
        + [pltpu.VMEM((ranks, ranks), bf16)] * devices,
        in_specs=[pl.BlockSpec(memory_space=pltpu.SMEM)]
        + [pl.BlockSpec(memory_space=pltpu.VMEM)] * 4
        + [pl.BlockSpec(memory_space=pl.ANY)] * (devices + 2),
        out_specs=[pl.BlockSpec(memory_space=pltpu.VMEM)] * (devices + 4),
        scratch_shapes=[pltpu.SemaphoreType.DMA((devices,))],
        compiler_params=pltpu.CompilerParams(vmem_limit_bytes=ROOM),
        cost_estimate=pl.CostEstimate(
            flops=product_flops * (2 * devices + 1),
            bytes_accessed=2 * devices * ranks * ranks,
            transcendentals=rows * ranks,
        ),
    )(middle.astype(jnp.int32).reshape(1), projected, marks, own_score, gram, *held, *thirds)

    def turn(score, late, terms):
        arrays = [array for pair in terms for array in pair]

        def body(*refs):
            turn_kernel(len(terms), bool(late), *refs)

        return call_rows(
            body,
            [(wide, f32), (wide, bf16), (wide, bf16), (wide, bf16)],
            [marks, scaled, slope, score, *late, *arrays, *pieces],
            product_flops * (devices + len(terms)),
        )

    chain_first = chain
    first_down = between_layers(chain, [(3, 2)])
    step_cross = between_layers(after(step_two, chain), crossed)
    first_two = between_layers(chain, [(3, 1)])
    proj_slots = to_experts([after(part, chain) for part in proj_slots])
    score, _, _, chain = turn(score, [down_score], [(first_down, down_gram)])

    second_cross = between_layers(chain, [(2, 1)])
    second_two = between_layers(chain, [(2, 0)])
    first_three = between_layers(after(chain_first, chain), [(3, 0)])
    half_cross = after(half_cross, chain)
    step_cross = after(step_cross, chain)
    cross_pair = gram_pair(half_cross, own_half)
    late_steps = (step_two.astype(f32) + step_cross.astype(f32)).astype(bf16)
    late_score = both_cores(dot_first(late_steps, own_half))
    cross_product = gram_sum(cross_pair)
    score, _, _, chain = turn(
        score, [late_score], [(first_two, two_gram), (second_cross, cross_product)]
    )

    third_down = between_layers(chain, [(1, 0)])
    scaled_rows = [scaled] + [across_chips(after(scaled, chain), step) for step in range(1, CHIPS)]
    token_blocks = token_blocks[:1] + [
        across_chips(after(token_blocks[step], chain), step) for step in range(1, CHIPS)
    ]
    steps_total = difference.astype(f32) + step_down.astype(f32)
    steps_total = (steps_total + after(late_steps, chain).astype(f32)).astype(bf16)
    score, grad_pre, grad_proj, _ = turn(
        score, [], [(second_two, two_gram), (first_three, cross_product), (third_down, down_gram)]
    )

    def with_swap(values):
        return values, swap_cores(values)

    proj_rows = gather_rows(grad_proj)
    grad_slots = to_slots(grad_pre)
    grad_slots = to_experts(grad_slots)
    scaled_pair = with_swap(after(scaled, grad_proj))
    two_pair = with_swap(first_two + after(second_two, grad_proj))
    cross_pair = with_swap(second_cross + after(first_three, grad_proj))
    down_pair = with_swap(first_down + third_down)
    mixed_blocks = spread(
        steps_total,
        [
            (own_half, *scaled_pair),
            (half_two, *two_pair),
            (half_cross, *cross_pair),
            (half_down, *down_pair),
        ],
    )
    scaled_rows = [after(rows, mixed_blocks[0]) for rows in scaled_rows]
    mixed_blocks = list(mixed_blocks[:1]) + [
        across_chips(mixed_blocks[step], step) for step in range(1, CHIPS)
    ]
    scaled_rows = scaled_rows + [scaled_pair[1]] + [swap_cores(rows) for rows in scaled_rows[1:]]
    share = factor_rows(None, token_blocks, proj_rows)
    core_total = dot_first(jnp.concatenate(proj_slots), jnp.concatenate(grad_slots)).astype(bf16)
    share = factor_rows(after(share, core_total), mixed_blocks, scaled_rows)
    return (share[None], core_total[None, None])


def solution(mesh):
    placed = (
        P("section", None, "expert", None),
        P("section", None, "expert", None),
        P("section", None, "expert"),
        P("section", None, "expert"),
        P("section", None, "expert"),
        P("section", None, None),
        P("section", "expert", None, None),
    )
    drawn_for = (LAYERS, CHIPS * CORES)

    def per_device(*arrays):
        local_experts = arrays[-1].shape[1]
        if (mesh.shape["section"], mesh.shape["expert"]) == drawn_for and local_experts == 1:
            return gathered_plan(*arrays)
        return general_plan(*arrays)

    return jax.shard_map(
        per_device,
        mesh=mesh,
        in_specs=placed,
        out_specs=(P("section", "expert", None), P("section", "expert", None, None)),
        check_vma=False,
    )
```

```python
import jax
import jax.numpy as jnp
from jax import lax
from jax.experimental import pallas as pl
from jax.experimental.pallas import tpu as pltpu
from jax.sharding import PartitionSpec as P


def from_behind(value, axis, steps):
    count = lax.axis_size(axis)
    leading, last = (max(0, -steps), min(count, count - steps))
    return lax.ppermute(value, axis, [(source, source + steps) for source in range(leading, last)])


def silu_slope(values):
    sigmoid = jax.nn.sigmoid(values)
    return sigmoid * (1.0 + values * (1.0 - sigmoid))


def times_transposed(left, shared):
    return lax.dot_general(
        left, shared, (((1,), (1,)), ((), ())), preferred_element_type=jnp.float32
    )


def factor_terms(tokens_flat, proj_flat, mixed_flat, hidden_flat):

    def factor_rows(start, count):
        first_term = lax.dot_general(
            tokens_flat, proj_flat, (((0,), (0,)), ((), ())), preferred_element_type=jnp.float32
        )
        second_term = lax.dot_general(
            mixed_flat, hidden_flat, (((0,), (0,)), ((), ())), preferred_element_type=jnp.float32
        )
        return first_term + second_term

    return factor_rows


def store_slice(store, fresh, picked, usable):
    former = lax.dynamic_index_in_dim(store, picked, 0, keepdims=False)
    kept = jnp.where(usable, fresh, former)
    return lax.dynamic_update_index_in_dim(store, kept, picked, 0)


def general_plan(inputs, teacher, gate, route, slot, factor, cores):
    tokens_all = inputs[0]
    targets_all = teacher[0]
    weights_all = gate[0]
    shared = factor[0]
    blocks = cores[0]
    micro_count, token_count, channels = tokens_all.shape
    ranks = shared.shape[1]
    local_experts = blocks.shape[0]
    expert_devices = lax.axis_size("expert")
    capacity = max(2, 2 * token_count // (local_experts * expert_devices))
    slot_count = local_experts * expert_devices * capacity
    places_all = route[0] * capacity + slot[0]
    micro_range = jnp.arange(micro_count, dtype=jnp.int32)[:, None]
    token_proj = jnp.dot(
        tokens_all.reshape(-1, channels), shared, preferred_element_type=jnp.float32
    ).astype(jnp.bfloat16)
    token_proj = token_proj.reshape(micro_count, token_count, ranks)
    proj_slots = (
        jnp.zeros((micro_count, slot_count, ranks), jnp.bfloat16)
        .at[micro_range, places_all]
        .set(token_proj)
    )
    projected = lax.all_to_all(proj_slots, "expert", split_axis=1, concat_axis=1, tiled=True)
    projected = projected.reshape(micro_count, expert_devices, local_experts, capacity, ranks)
    pre = jnp.einsum("mnecr,erk->mneck", projected, blocks, preferred_element_type=jnp.float32)
    active = jax.nn.silu(pre).astype(jnp.bfloat16)
    returned = lax.all_to_all(
        active.reshape(micro_count, slot_count, ranks),
        "expert",
        split_axis=1,
        concat_axis=1,
        tiled=True,
    )
    hidden = jnp.take_along_axis(returned, places_all[:, :, None], axis=1)
    mixed = times_transposed(hidden.reshape(-1, ranks), shared).reshape(
        micro_count, token_count, channels
    )
    output = tokens_all.astype(jnp.float32) + weights_all[:, :, None] * mixed
    errors = output - targets_all.astype(jnp.float32)
    section_count = lax.axis_size("section")
    section_here = lax.axis_index("section")
    incoming = jnp.zeros((token_count, channels), jnp.bfloat16)
    mixed_store = jnp.zeros((micro_count, token_count, channels), jnp.bfloat16)
    proj_store = jnp.zeros((micro_count, token_count, ranks), jnp.bfloat16)
    pre_store = jnp.zeros(
        (micro_count, expert_devices, local_experts, capacity, ranks), jnp.bfloat16
    )
    turn_total = micro_count + section_count - 1
    for turn_index in range(turn_total):
        micro_now = turn_index - (section_count - 1 - section_here)
        usable = jnp.logical_and(micro_now >= 0, micro_now < micro_count)
        picked = jnp.clip(micro_now, 0, micro_count - 1)
        grad_out = lax.dynamic_index_in_dim(errors, picked, 0, keepdims=False) + incoming.astype(
            jnp.float32
        )
        weight_now = lax.dynamic_index_in_dim(weights_all, picked, 0, keepdims=False)
        places = lax.dynamic_index_in_dim(places_all, picked, 0, keepdims=False)
        grad_mixed = (weight_now[:, None] * grad_out).astype(jnp.bfloat16)
        grad_hidden = jnp.dot(grad_mixed, shared, preferred_element_type=jnp.float32).astype(
            jnp.bfloat16
        )
        grad_slots = jnp.zeros((slot_count, ranks), jnp.bfloat16).at[places].set(grad_hidden)
        grad_recv = lax.all_to_all(grad_slots, "expert", split_axis=0, concat_axis=0, tiled=True)
        grad_recv = grad_recv.reshape(expert_devices, local_experts, capacity, ranks)
        pre_now = lax.dynamic_index_in_dim(pre, picked, 0, keepdims=False)
        grad_pre = (grad_recv.astype(jnp.float32) * silu_slope(pre_now)).astype(jnp.bfloat16)
        grad_routed = jnp.einsum(
            "neck,erk->necr", grad_pre, blocks, preferred_element_type=jnp.float32
        ).astype(jnp.bfloat16)
        grad_home = lax.all_to_all(
            grad_routed.reshape(slot_count, ranks),
            "expert",
            split_axis=0,
            concat_axis=0,
            tiled=True,
        )
        grad_proj = grad_home[places]
        grad_in = (grad_out + times_transposed(grad_proj, shared)).astype(jnp.bfloat16)
        if turn_index + 1 < turn_total:
            incoming = from_behind(grad_in, "section", -1)
        mixed_store = store_slice(mixed_store, grad_mixed, picked, usable)
        proj_store = store_slice(proj_store, grad_proj, picked, usable)
        pre_store = store_slice(pre_store, grad_pre, picked, usable)
    core_total = jnp.einsum(
        "mnecr,mneck->erk", projected, pre_store, preferred_element_type=jnp.float32
    )
    all_rows = factor_terms(
        tokens_all.reshape(-1, channels),
        proj_store.reshape(-1, ranks),
        mixed_store.reshape(-1, channels),
        hidden.reshape(-1, ranks),
    )
    factor_share = lax.psum_scatter(
        all_rows(jnp.int32(0), channels // expert_devices * lax.axis_size("expert")),
        "expert",
        scatter_dimension=0,
        tiled=True,
    )
    return (factor_share[None], core_total.astype(jnp.bfloat16)[None])


CORES = 2
CHIPS = 4
LAYERS = 4
WIDE_ROOM = 24 * 2**20
ROOM = 16 * 2**20


def dot(left, right):
    return jnp.dot(left, right, preferred_element_type=jnp.float32)


def dot_first(left, right):
    return lax.dot_general(
        left, right, (((0,), (0,)), ((), ())), preferred_element_type=jnp.float32
    )


def on_chips(value, pairs):
    perm = [
        (CORES * source + core, CORES * target + core)
        for source, target in pairs
        for core in range(CORES)
    ]
    return lax.ppermute(value, "expert", perm)


def swap_cores(value):
    count = lax.axis_size("expert")
    return lax.ppermute(value, "expert", [(index, index ^ 1) for index in range(count)])


def between_layers(value, pairs):
    return lax.ppermute(value, "section", pairs)


def gather_cores(core):
    beside = on_chips(core, [(0, 1), (1, 0), (2, 3), (3, 2)])
    across = on_chips(core, [(1, 2), (2, 1)])
    far_across = on_chips(beside, [(1, 2), (2, 1)])
    outward = on_chips(across, [(1, 0), (2, 3)])
    far_outward = on_chips(far_across, [(1, 0), (2, 3)])
    held, swapped = [core, beside], [swap_cores(piece) for piece in (core, beside)]
    near = [(across, outward), (far_across, far_outward)]
    far = [tuple(swap_cores(piece) for piece in pair) for pair in near]
    return [piece for both in zip(held + near, swapped + far) for piece in both]


def row_marks(route, weight, chip, core, middle):
    count = CHIPS * CORES
    place = lax.broadcasted_iota(jnp.int32, (1, 2 * count), 1)
    step = (place % count) // CORES
    turned = jnp.where(jnp.logical_and(step >= 2, middle), 5 - step, step)
    expert = CORES * (chip ^ turned) + (core ^ (place % CORES))
    marks = (route == expert).astype(jnp.float32)
    return jnp.where(place < count, marks, weight)


def across_chips(value, step):
    return on_chips(value, [(chip, chip ^ step) for chip in range(CHIPS)])


def gather_rows(rows):
    held = [rows] + [across_chips(rows, step) for step in range(1, CHIPS)]
    return held + [swap_cores(piece) for piece in held]


def chip_blocks(wide, chip, core):
    count = wide.shape[0] // (CHIPS * CORES)
    blocks = [
        lax.dynamic_slice_in_dim(wide, (CORES * (chip ^ step) + core) * count, count, 0)
        for step in range(CHIPS)
    ]
    return jnp.concatenate(blocks, axis=0)


def chip_columns(wide, chip, core):
    theirs = swap_cores(chip_blocks(wide, chip, 1 - core))
    return jnp.concatenate([chip_blocks(wide, chip, core), theirs], axis=1)


def both_cores(partial):
    rows = partial.shape[0] // CORES
    return partial[:rows] + swap_cores(partial[rows:])


def gram_pair(left, right):
    partial = dot_first(left, right).astype(jnp.bfloat16)
    return partial, swap_cores(partial)


def gram_sum(pair):
    return (pair[0].astype(jnp.float32) + pair[1].astype(jnp.float32)).astype(jnp.bfloat16)


def routed_product(rows, marks, start, core_refs, transposed, copies=None):
    dims = (((1,), (1 if transposed else 0,)), ((), ()))
    total = None
    for place, core_ref in enumerate(core_refs):
        if copies is not None:
            copies[place].wait()
        mark = marks[:, start + place : start + place + 1]
        chosen = jnp.where(mark > 0.5, rows, jnp.zeros_like(rows))
        term = lax.dot_general(
            chosen, core_ref[...], dims, preferred_element_type=jnp.float32
        )
        total = term if total is None else total + term
    return total


def backward_rows(score, slope, marks, core_refs):
    count = len(core_refs)
    grad_hidden = (marks[:, count : count + 1] * score).astype(jnp.bfloat16)
    grad_pre = (grad_hidden.astype(jnp.float32) * slope).astype(jnp.bfloat16)
    grad_proj = routed_product(grad_pre, marks, 0, core_refs, True)
    return grad_pre, grad_proj.astype(jnp.bfloat16)


def fetch(middle, sources, targets, arrived):
    copies = []
    for place, (source, target) in enumerate(zip(sources, targets)):
        choices = source if isinstance(source, tuple) else (source,)
        moves = [pltpu.make_async_copy(ref, target, arrived.at[place]) for ref in choices]
        copies.append(moves[0])
        if len(moves) == 1:
            moves[0].start()
        else:
            pl.when(middle)(moves[0].start)
            pl.when(jnp.logical_not(middle))(moves[1].start)
    return copies


def early_kernel(middle_ref, proj_ref, marks_ref, *refs):
    sources = [*refs[:4], (refs[4], refs[5]), (refs[6], refs[7])]
    part_ref, core_refs, arrived = refs[8], refs[9:-1], refs[-1]
    copies = fetch(middle_ref[0] > 0, sources, core_refs, arrived)
    part_ref[...] = routed_product(proj_ref[...], marks_ref[...], 0, core_refs, False, copies)


def first_kernel(middle_ref, proj_ref, marks_ref, part_ref, *refs):
    early = CHIPS * CORES - 2
    held, refs = refs[:early], refs[early:]
    sources = [(refs[0], refs[1]), (refs[2], refs[3]), refs[4], refs[5]]
    scaled_ref, slope_ref, score_ref, chain_ref, near_ref, far_ref = refs[6:12]
    own_ref, gram_ref, arrived = refs[12:]
    last = [near_ref, far_ref]
    copies = fetch(middle_ref[0] > 0, sources, [*last, own_ref, gram_ref], arrived)
    core_refs, count = [*held, *last], early + 2
    marks = marks_ref[...]
    pre = part_ref[...] + routed_product(proj_ref[...], marks, early, last, False, copies)
    sigmoid = 1.0 / (1.0 + jnp.exp(-pre))
    hidden = (pre * sigmoid).astype(jnp.bfloat16)
    slope = sigmoid * (1.0 + pre * (1.0 - sigmoid))
    weight = marks[:, count : count + 1]
    scaled = (weight * hidden.astype(jnp.float32)).astype(jnp.bfloat16)
    copies[2].wait()
    copies[3].wait()
    score = own_ref[...] + dot(scaled, gram_ref[...])
    scaled_ref[...] = scaled
    slope_ref[...] = slope
    score_ref[...] = score
    _, grad_proj = backward_rows(score, slope, marks, core_refs)
    chain_ref[...] = (scaled.astype(jnp.float32) + grad_proj.astype(jnp.float32)).astype(
        jnp.bfloat16
    )


def turn_kernel(terms, late, marks_ref, scaled_ref, slope_ref, score_ref, *refs):
    score = score_ref[...]
    if late:
        score, refs = score + refs[0][...], refs[1:]
    core_refs = refs[2 * terms : len(refs) - 4]
    next_ref, grad_ref, proj_ref, chain_ref = refs[len(refs) - 4 :]
    for term in range(terms):
        score = score + dot(refs[2 * term][...], refs[2 * term + 1][...])
    next_ref[...] = score
    grad_pre, grad_proj = backward_rows(score, slope_ref[...], marks_ref[...], core_refs)
    grad_ref[...] = grad_pre
    proj_ref[...] = grad_proj
    chain_ref[...] = (scaled_ref[...].astype(jnp.float32) + grad_proj.astype(jnp.float32)).astype(
        jnp.bfloat16
    )


def call_rows(body, outs, arrays, flops, scalars=()):
    in_bytes = sum(array.size * array.dtype.itemsize for array in arrays)
    return pl.pallas_call(
        body,
        out_shape=[jax.ShapeDtypeStruct(shape, kind) for shape, kind in outs],
        in_specs=[pl.BlockSpec(memory_space=pltpu.SMEM)] * len(scalars)
        + [pl.BlockSpec(memory_space=pltpu.VMEM)] * len(arrays),
        out_specs=[pl.BlockSpec(memory_space=pltpu.VMEM)] * len(outs),
        compiler_params=pltpu.CompilerParams(vmem_limit_bytes=ROOM),
        cost_estimate=pl.CostEstimate(flops=flops, bytes_accessed=in_bytes, transcendentals=0),
    )(*scalars, *arrays)


def spread_kernel(terms, base_ref, *refs):
    total = base_ref[...].astype(jnp.float32)
    for term in range(terms):
        half_ref, near_ref, far_ref = refs[3 * term : 3 * term + 3]
        values = jnp.concatenate([near_ref[...], far_ref[...]], axis=0)
        total = total + times_transposed(half_ref[...], values)
    count = total.shape[0] // CHIPS
    for step, out_ref in enumerate(refs[3 * terms :]):
        out_ref[...] = total[step * count : (step + 1) * count].astype(jnp.bfloat16)


def spread(base, terms):
    arrays = [base] + [array for term in terms for array in term]
    height, width = base.shape

    def body(*refs):
        spread_kernel(len(terms), *refs)

    return pl.pallas_call(
        body,
        name="spread",
        out_shape=[jax.ShapeDtypeStruct((height // CHIPS, width), jnp.bfloat16)] * CHIPS,
        in_specs=[pl.BlockSpec(memory_space=pltpu.VMEM)] * len(arrays),
        out_specs=[pl.BlockSpec(memory_space=pltpu.VMEM)] * CHIPS,
        compiler_params=pltpu.CompilerParams(vmem_limit_bytes=WIDE_ROOM),
        cost_estimate=pl.CostEstimate(
            flops=2 * height * width * terms[0][0].shape[1] * len(terms),
            bytes_accessed=sum(array.size * array.dtype.itemsize for array in arrays),
            transcendentals=0,
        ),
    )(*arrays)


def pair_products(block_ref, near_ref, far_ref):
    return dot(block_ref[...], jnp.concatenate([near_ref[...], far_ref[...]], axis=0))


def factor_kernel(start, *refs):
    total_ref = refs[-1]
    total = refs[0][...] if start else None
    refs = refs[1:-1] if start else refs[:-1]
    for step in range(CHIPS):
        term = pair_products(refs[step], refs[CHIPS + step], refs[2 * CHIPS + step])
        total = term if total is None else total + term
    total_ref[...] = total


def factor_rows(total, blocks, pieces):
    arrays = ([] if total is None else [total]) + blocks + pieces
    count, ranks = blocks[0].shape[0], pieces[0].shape[1]

    def body(*refs):
        factor_kernel(total is not None, *refs)

    return pl.pallas_call(
        body,
        out_shape=jax.ShapeDtypeStruct((count, ranks), jnp.float32),
        in_specs=[pl.BlockSpec(memory_space=pltpu.VMEM)] * len(arrays),
        out_specs=pl.BlockSpec(memory_space=pltpu.VMEM),
        compiler_params=pltpu.CompilerParams(vmem_limit_bytes=ROOM),
        cost_estimate=pl.CostEstimate(
            flops=2 * count * ranks * len(pieces) * pieces[0].shape[0],
            bytes_accessed=sum(array.size * array.dtype.itemsize for array in arrays),
            transcendentals=0,
        ),
    )(*arrays)


def after(value, earlier):
    return lax.optimization_barrier((value, earlier))[0]


def gathered_plan(inputs, teacher, gate, route, slot, factor, cores):
    bf16, f32 = jnp.bfloat16, jnp.float32
    shared = factor[0]
    channels, ranks = shared.shape
    devices = lax.axis_size("expert")
    micro_count, token_count = route.shape[1:]
    rows = micro_count * token_count
    here = lax.axis_index("expert")
    chip, core = here // CORES, here % CORES
    middle = jnp.logical_or(chip == 1, chip == 2)
    tokens = inputs[0].reshape(rows, channels)

    travelled = gather_cores(cores[0, 0])
    marks = row_marks(
        route[0].reshape(rows, 1), gate[0].reshape(rows, 1), chip, core, middle
    )

    down = [(3, 2), (1, 0)]
    two_down = [(3, 1), (2, 0)]
    crossed = [(0, 1), (1, 0)]
    own_half = chip_blocks(shared, chip, core)
    half_down = between_layers(own_half, down)
    half_two = between_layers(own_half, two_down)
    half_cross = between_layers(half_two, crossed)
    turned = lax.optimization_barrier(tokens.T)
    wanted = lax.optimization_barrier(teacher[0].reshape(rows, channels).T)
    difference = (turned.astype(f32) - wanted.astype(f32)).astype(bf16)
    difference = chip_columns(difference, chip, core)
    step_down = between_layers(difference, down)
    step_two = between_layers(difference, two_down)

    capacity = max(2, 2 * token_count // devices)
    slots = micro_count * capacity
    micro = jnp.arange(rows, dtype=jnp.int32) // token_count
    expert = route[0].reshape(rows)
    near = (expert % CORES ^ core) * CHIPS + (expert // CORES ^ chip)
    place = near * slots + micro * capacity + slot[0].reshape(rows)
    picks = (jnp.arange(devices * slots, dtype=jnp.int32)[:, None] == place[None, :]).astype(bf16)

    def to_slots(values):
        held = dot(picks, values).astype(bf16)
        half = CHIPS * slots
        own, theirs = held[:half], swap_cores(held[half:])
        return [
            jnp.concatenate([part[step * slots : (step + 1) * slots] for part in (own, theirs)])
            for step in range(CHIPS)
        ]

    def to_experts(parts):
        return parts[:1] + [across_chips(parts[step], step) for step in range(1, CHIPS)]

    step_cross = between_layers(step_two, crossed)
    projected = dot(tokens, shared).astype(bf16)
    own_gram = gram_pair(own_half, own_half)
    proj_slots = to_slots(projected)
    gram = gram_sum(own_gram)
    own_score = both_cores(dot_first(difference, own_half))
    turned = chip_columns(turned, chip, core)
    token_blocks = [
        turned[step * channels // devices : (step + 1) * channels // devices]
        for step in range(CHIPS)
    ]
    down_gram = gram_sum(gram_pair(half_down, own_half))
    two_gram = gram_sum(gram_pair(half_two, own_half))
    down_score = both_cores(dot_first(step_down, own_half))

    wide = (rows, ranks)
    product_flops = 2 * rows * ranks * ranks
    flag = middle.astype(jnp.int32).reshape(1)
    block = pltpu.VMEM((ranks, ranks), bf16)

    def core_call(body, sources, outs, arrays, scratch, products):
        flat = [ref for source in sources for ref in (source if type(source) is tuple else [source])]
        return pl.pallas_call(
            body,
            out_shape=outs,
            in_specs=[pl.BlockSpec(memory_space=pltpu.SMEM)]
            + [pl.BlockSpec(memory_space=pltpu.VMEM)] * len(arrays)
            + [pl.BlockSpec(memory_space=pl.ANY)] * len(flat),
            out_specs=[pl.BlockSpec(memory_space=pltpu.VMEM)] * len(outs),
            scratch_shapes=scratch + [pltpu.SemaphoreType.DMA((len(sources),))],
            compiler_params=pltpu.CompilerParams(vmem_limit_bytes=ROOM),
            cost_estimate=pl.CostEstimate(
                flops=product_flops * products,
                bytes_accessed=2 * len(sources) * ranks * ranks,
                transcendentals=0,
            ),
        )(flag, *arrays, *flat)

    part, *held = core_call(
        early_kernel,
        travelled[:-2],
        [jax.ShapeDtypeStruct(wide, f32)] + [block] * (devices - 2),
        [projected, marks],
        [],
        devices - 2,
    )
    scaled, slope, score, chain, *last = core_call(
        first_kernel,
        [*travelled[-2:], own_score, gram],
        [jax.ShapeDtypeStruct(wide, kind) for kind in (bf16, f32, f32, bf16)] + [block] * 2,
        [projected, marks, part, *held],
        [pltpu.VMEM(wide, f32), pltpu.VMEM((ranks, ranks), bf16)],
        devices + 3,
    )
    pieces = [*held, *last]

    def turn(score, late, terms):
        arrays = [array for pair in terms for array in pair]

        def body(*refs):
            turn_kernel(len(terms), bool(late), *refs)

        return call_rows(
            body,
            [(wide, f32), (wide, bf16), (wide, bf16), (wide, bf16)],
            [marks, scaled, slope, score, *late, *arrays, *pieces],
            product_flops * (devices + len(terms)),
        )

    chain_first = chain
    first_down = between_layers(chain, [(3, 2)])
    first_two = between_layers(chain, [(3, 1)])
    scaled_rows = [scaled] + [across_chips(after(scaled, chain), step) for step in range(1, CHIPS)]
    token_blocks = token_blocks[:1] + [
        across_chips(after(token_blocks[step], chain), step) for step in range(1, CHIPS)
    ]
    score, _, _, chain = turn(score, [down_score], [(first_down, down_gram)])

    second_cross = between_layers(chain, [(2, 1)])
    second_two = between_layers(chain, [(2, 0)])
    first_three = between_layers(after(chain_first, chain), [(3, 0)])
    proj_slots = to_experts([after(part, chain) for part in proj_slots])
    half_cross = after(half_cross, chain)
    step_cross = after(step_cross, chain)
    cross_pair = gram_pair(half_cross, own_half)
    late_steps = (step_two.astype(f32) + step_cross.astype(f32)).astype(bf16)
    late_score = both_cores(dot_first(late_steps, own_half))
    cross_product = gram_sum(cross_pair)
    score, _, _, chain = turn(
        score, [late_score], [(first_two, two_gram), (second_cross, cross_product)]
    )

    third_down = between_layers(chain, [(1, 0)])
    steps_total = difference.astype(f32) + step_down.astype(f32)
    steps_total = (steps_total + after(late_steps, chain).astype(f32)).astype(bf16)
    score, grad_pre, grad_proj, _ = turn(
        score, [], [(second_two, two_gram), (first_three, cross_product), (third_down, down_gram)]
    )

    def with_swap(values):
        return values, swap_cores(values)

    proj_rows = gather_rows(grad_proj)
    scaled_pair = with_swap(after(scaled, grad_proj))
    two_pair = with_swap(first_two + after(second_two, grad_proj))
    cross_pair = with_swap(second_cross + after(first_three, grad_proj))
    down_pair = with_swap(first_down + third_down)
    mixed_blocks = spread(
        steps_total,
        [
            (own_half, *scaled_pair),
            (half_two, *two_pair),
            (half_cross, *cross_pair),
            (half_down, *down_pair),
        ],
    )
    mixed_first = mixed_blocks[0]
    scaled_rows = [after(rows, mixed_first) for rows in scaled_rows]
    mixed_blocks = list(mixed_blocks[:1]) + [
        across_chips(mixed_blocks[step], step) for step in range(1, CHIPS)
    ]
    grad_slots = to_slots(after(grad_pre, mixed_first))
    grad_slots = to_experts(grad_slots)
    scaled_rows = scaled_rows + [scaled_pair[1]] + [swap_cores(rows) for rows in scaled_rows[1:]]
    share = factor_rows(None, token_blocks, proj_rows)
    core_total = dot_first(jnp.concatenate(proj_slots), jnp.concatenate(grad_slots)).astype(bf16)
    share = factor_rows(after(share, core_total), mixed_blocks, scaled_rows)
    return (share[None], core_total[None, None])


def solution(mesh):
    placed = (
        P("section", None, "expert", None),
        P("section", None, "expert", None),
        P("section", None, "expert"),
        P("section", None, "expert"),
        P("section", None, "expert"),
        P("section", None, None),
        P("section", "expert", None, None),
    )
    drawn_for = (LAYERS, CHIPS * CORES)

    def per_device(*arrays):
        local_experts = arrays[-1].shape[1]
        if (mesh.shape["section"], mesh.shape["expert"]) == drawn_for and local_experts == 1:
            return gathered_plan(*arrays)
        return general_plan(*arrays)

    return jax.shard_map(
        per_device,
        mesh=mesh,
        in_specs=placed,
        out_specs=(P("section", "expert", None), P("section", "expert", None, None)),
        check_vma=False,
    )
```

```python
import jax
import jax.numpy as jnp
from jax import lax
from jax.experimental import pallas as pl
from jax.experimental.pallas import tpu as pltpu
from jax.sharding import PartitionSpec as P


def from_behind(value, axis, steps):
    count = lax.axis_size(axis)
    leading, last = (max(0, -steps), min(count, count - steps))
    return lax.ppermute(value, axis, [(source, source + steps) for source in range(leading, last)])


def silu_slope(values):
    sigmoid = jax.nn.sigmoid(values)
    return sigmoid * (1.0 + values * (1.0 - sigmoid))


def times_transposed(left, shared):
    return lax.dot_general(
        left, shared, (((1,), (1,)), ((), ())), preferred_element_type=jnp.float32
    )


def factor_terms(tokens_flat, proj_flat, mixed_flat, hidden_flat):

    def factor_rows(start, count):
        first_term = lax.dot_general(
            tokens_flat, proj_flat, (((0,), (0,)), ((), ())), preferred_element_type=jnp.float32
        )
        second_term = lax.dot_general(
            mixed_flat, hidden_flat, (((0,), (0,)), ((), ())), preferred_element_type=jnp.float32
        )
        return first_term + second_term

    return factor_rows


def store_slice(store, fresh, picked, usable):
    former = lax.dynamic_index_in_dim(store, picked, 0, keepdims=False)
    kept = jnp.where(usable, fresh, former)
    return lax.dynamic_update_index_in_dim(store, kept, picked, 0)


def general_plan(inputs, teacher, gate, route, slot, factor, cores):
    tokens_all = inputs[0]
    targets_all = teacher[0]
    weights_all = gate[0]
    shared = factor[0]
    blocks = cores[0]
    micro_count, token_count, channels = tokens_all.shape
    ranks = shared.shape[1]
    local_experts = blocks.shape[0]
    expert_devices = lax.axis_size("expert")
    capacity = max(2, 2 * token_count // (local_experts * expert_devices))
    slot_count = local_experts * expert_devices * capacity
    places_all = route[0] * capacity + slot[0]
    micro_range = jnp.arange(micro_count, dtype=jnp.int32)[:, None]
    token_proj = jnp.dot(
        tokens_all.reshape(-1, channels), shared, preferred_element_type=jnp.float32
    ).astype(jnp.bfloat16)
    token_proj = token_proj.reshape(micro_count, token_count, ranks)
    proj_slots = (
        jnp.zeros((micro_count, slot_count, ranks), jnp.bfloat16)
        .at[micro_range, places_all]
        .set(token_proj)
    )
    projected = lax.all_to_all(proj_slots, "expert", split_axis=1, concat_axis=1, tiled=True)
    projected = projected.reshape(micro_count, expert_devices, local_experts, capacity, ranks)
    pre = jnp.einsum("mnecr,erk->mneck", projected, blocks, preferred_element_type=jnp.float32)
    active = jax.nn.silu(pre).astype(jnp.bfloat16)
    returned = lax.all_to_all(
        active.reshape(micro_count, slot_count, ranks),
        "expert",
        split_axis=1,
        concat_axis=1,
        tiled=True,
    )
    hidden = jnp.take_along_axis(returned, places_all[:, :, None], axis=1)
    mixed = times_transposed(hidden.reshape(-1, ranks), shared).reshape(
        micro_count, token_count, channels
    )
    output = tokens_all.astype(jnp.float32) + weights_all[:, :, None] * mixed
    errors = output - targets_all.astype(jnp.float32)
    section_count = lax.axis_size("section")
    section_here = lax.axis_index("section")
    incoming = jnp.zeros((token_count, channels), jnp.bfloat16)
    mixed_store = jnp.zeros((micro_count, token_count, channels), jnp.bfloat16)
    proj_store = jnp.zeros((micro_count, token_count, ranks), jnp.bfloat16)
    pre_store = jnp.zeros(
        (micro_count, expert_devices, local_experts, capacity, ranks), jnp.bfloat16
    )
    turn_total = micro_count + section_count - 1
    for turn_index in range(turn_total):
        micro_now = turn_index - (section_count - 1 - section_here)
        usable = jnp.logical_and(micro_now >= 0, micro_now < micro_count)
        picked = jnp.clip(micro_now, 0, micro_count - 1)
        grad_out = lax.dynamic_index_in_dim(errors, picked, 0, keepdims=False) + incoming.astype(
            jnp.float32
        )
        weight_now = lax.dynamic_index_in_dim(weights_all, picked, 0, keepdims=False)
        places = lax.dynamic_index_in_dim(places_all, picked, 0, keepdims=False)
        grad_mixed = (weight_now[:, None] * grad_out).astype(jnp.bfloat16)
        grad_hidden = jnp.dot(grad_mixed, shared, preferred_element_type=jnp.float32).astype(
            jnp.bfloat16
        )
        grad_slots = jnp.zeros((slot_count, ranks), jnp.bfloat16).at[places].set(grad_hidden)
        grad_recv = lax.all_to_all(grad_slots, "expert", split_axis=0, concat_axis=0, tiled=True)
        grad_recv = grad_recv.reshape(expert_devices, local_experts, capacity, ranks)
        pre_now = lax.dynamic_index_in_dim(pre, picked, 0, keepdims=False)
        grad_pre = (grad_recv.astype(jnp.float32) * silu_slope(pre_now)).astype(jnp.bfloat16)
        grad_routed = jnp.einsum(
            "neck,erk->necr", grad_pre, blocks, preferred_element_type=jnp.float32
        ).astype(jnp.bfloat16)
        grad_home = lax.all_to_all(
            grad_routed.reshape(slot_count, ranks),
            "expert",
            split_axis=0,
            concat_axis=0,
            tiled=True,
        )
        grad_proj = grad_home[places]
        grad_in = (grad_out + times_transposed(grad_proj, shared)).astype(jnp.bfloat16)
        if turn_index + 1 < turn_total:
            incoming = from_behind(grad_in, "section", -1)
        mixed_store = store_slice(mixed_store, grad_mixed, picked, usable)
        proj_store = store_slice(proj_store, grad_proj, picked, usable)
        pre_store = store_slice(pre_store, grad_pre, picked, usable)
    core_total = jnp.einsum(
        "mnecr,mneck->erk", projected, pre_store, preferred_element_type=jnp.float32
    )
    all_rows = factor_terms(
        tokens_all.reshape(-1, channels),
        proj_store.reshape(-1, ranks),
        mixed_store.reshape(-1, channels),
        hidden.reshape(-1, ranks),
    )
    factor_share = lax.psum_scatter(
        all_rows(jnp.int32(0), channels // expert_devices * lax.axis_size("expert")),
        "expert",
        scatter_dimension=0,
        tiled=True,
    )
    return (factor_share[None], core_total.astype(jnp.bfloat16)[None])


CORES = 2
CHIPS = 4
LAYERS = 4
ROOM = 16 * 2**20


def dot(left, right):
    return jnp.dot(left, right, preferred_element_type=jnp.float32)


def dot_first(left, right):
    return lax.dot_general(
        left, right, (((0,), (0,)), ((), ())), preferred_element_type=jnp.float32
    )


def on_chips(value, pairs):
    perm = [
        (CORES * source + core, CORES * target + core)
        for source, target in pairs
        for core in range(CORES)
    ]
    return lax.ppermute(value, "expert", perm)


def swap_cores(value):
    count = lax.axis_size("expert")
    return lax.ppermute(value, "expert", [(index, index ^ 1) for index in range(count)])


def between_layers(value, pairs):
    return lax.ppermute(value, "section", pairs)


def gather_cores(core):
    beside = on_chips(core, [(0, 1), (1, 0), (2, 3), (3, 2)])
    across = on_chips(core, [(1, 2), (2, 1)])
    far_across = on_chips(beside, [(1, 2), (2, 1)])
    outward = on_chips(across, [(1, 0), (2, 3)])
    far_outward = on_chips(far_across, [(1, 0), (2, 3)])
    held, swapped = [core, beside], [swap_cores(piece) for piece in (core, beside)]
    near = [(across, outward), (far_across, far_outward)]
    far = [tuple(swap_cores(piece) for piece in pair) for pair in near]
    return [piece for both in zip(held + near, swapped + far) for piece in both]


def row_marks(route, weight, chip, core, middle):
    count = CHIPS * CORES
    place = lax.broadcasted_iota(jnp.int32, (1, 2 * count), 1)
    step = (place % count) // CORES
    turned = jnp.where(jnp.logical_and(step >= 2, middle), 5 - step, step)
    expert = CORES * (chip ^ turned) + (core ^ (place % CORES))
    marks = (route == expert).astype(jnp.float32)
    return jnp.where(place < count, marks, weight)


def across_chips(value, step):
    return on_chips(value, [(chip, chip ^ step) for chip in range(CHIPS)])


def gather_rows(rows):
    held = [rows] + [across_chips(rows, step) for step in range(1, CHIPS)]
    return held + [swap_cores(piece) for piece in held]


def chip_blocks(wide, chip, core):
    count = wide.shape[0] // (CHIPS * CORES)
    blocks = [
        lax.dynamic_slice_in_dim(wide, (CORES * (chip ^ step) + core) * count, count, 0)
        for step in range(CHIPS)
    ]
    return jnp.concatenate(blocks, axis=0)


def chip_columns(wide, chip, core):
    theirs = swap_cores(chip_blocks(wide, chip, 1 - core))
    return jnp.concatenate([chip_blocks(wide, chip, core), theirs], axis=1)


def both_cores(partial):
    rows = partial.shape[0] // CORES
    return partial[:rows] + swap_cores(partial[rows:])


def gram_pair(left, right):
    partial = dot_first(left, right).astype(jnp.bfloat16)
    return partial, swap_cores(partial)


def gram_sum(pair):
    return (pair[0].astype(jnp.float32) + pair[1].astype(jnp.float32)).astype(jnp.bfloat16)


def routed_product(rows, marks, start, core_refs, transposed, copies=None):
    dims = (((1,), (1 if transposed else 0,)), ((), ()))
    total = None
    for place, core_ref in enumerate(core_refs):
        if copies is not None:
            copies[place].wait()
        mark = marks[:, start + place : start + place + 1]
        chosen = jnp.where(mark > 0.5, rows, jnp.zeros_like(rows))
        term = lax.dot_general(
            chosen, core_ref[...], dims, preferred_element_type=jnp.float32
        )
        total = term if total is None else total + term
    return total


def backward_rows(score, slope, marks, core_refs):
    count = len(core_refs)
    grad_hidden = (marks[:, count : count + 1] * score).astype(jnp.bfloat16)
    grad_pre = (grad_hidden.astype(jnp.float32) * slope).astype(jnp.bfloat16)
    grad_proj = routed_product(grad_pre, marks, 0, core_refs, True)
    return grad_pre, grad_proj.astype(jnp.bfloat16)


def fetch(middle, sources, targets, arrived):
    copies = []
    for place, (source, target) in enumerate(zip(sources, targets)):
        choices = source if isinstance(source, tuple) else (source,)
        moves = [pltpu.make_async_copy(ref, target, arrived.at[place]) for ref in choices]
        copies.append(moves[0])
        if len(moves) == 1:
            moves[0].start()
        else:
            pl.when(middle)(moves[0].start)
            pl.when(jnp.logical_not(middle))(moves[1].start)
    return copies


def early_kernel(middle_ref, proj_ref, marks_ref, *refs):
    sources = [*refs[:4], (refs[4], refs[5]), (refs[6], refs[7])]
    part_ref, core_refs, arrived = refs[8], refs[9:-1], refs[-1]
    copies = fetch(middle_ref[0] > 0, sources, core_refs, arrived)
    part_ref[...] = routed_product(proj_ref[...], marks_ref[...], 0, core_refs, False, copies)


def first_kernel(middle_ref, proj_ref, marks_ref, part_ref, *refs):
    early = CHIPS * CORES - 2
    held, refs = refs[:early], refs[early:]
    sources = [(refs[0], refs[1]), (refs[2], refs[3]), refs[4], refs[5]]
    scaled_ref, slope_ref, score_ref, chain_ref, near_ref, far_ref = refs[6:12]
    own_ref, gram_ref, arrived = refs[12:]
    last = [near_ref, far_ref]
    copies = fetch(middle_ref[0] > 0, sources, [*last, own_ref, gram_ref], arrived)
    core_refs, count = [*held, *last], early + 2
    marks = marks_ref[...]
    pre = part_ref[...] + routed_product(proj_ref[...], marks, early, last, False, copies)
    sigmoid = 1.0 / (1.0 + jnp.exp(-pre))
    hidden = (pre * sigmoid).astype(jnp.bfloat16)
    slope = sigmoid * (1.0 + pre * (1.0 - sigmoid))
    weight = marks[:, count : count + 1]
    scaled = (weight * hidden.astype(jnp.float32)).astype(jnp.bfloat16)
    copies[2].wait()
    copies[3].wait()
    score = own_ref[...] + dot(scaled, gram_ref[...])
    scaled_ref[...] = scaled
    slope_ref[...] = slope
    score_ref[...] = score
    _, grad_proj = backward_rows(score, slope, marks, core_refs)
    chain_ref[...] = (scaled.astype(jnp.float32) + grad_proj.astype(jnp.float32)).astype(
        jnp.bfloat16
    )


def turn_kernel(terms, late, marks_ref, scaled_ref, slope_ref, score_ref, *refs):
    score = score_ref[...]
    if late:
        score, refs = score + refs[0][...], refs[1:]
    core_refs = refs[2 * terms : len(refs) - 4]
    next_ref, grad_ref, proj_ref, chain_ref = refs[len(refs) - 4 :]
    for term in range(terms):
        score = score + dot(refs[2 * term][...], refs[2 * term + 1][...])
    next_ref[...] = score
    grad_pre, grad_proj = backward_rows(score, slope_ref[...], marks_ref[...], core_refs)
    grad_ref[...] = grad_pre
    proj_ref[...] = grad_proj
    chain_ref[...] = (scaled_ref[...].astype(jnp.float32) + grad_proj.astype(jnp.float32)).astype(
        jnp.bfloat16
    )


def call_rows(body, outs, arrays, flops, scalars=()):
    in_bytes = sum(array.size * array.dtype.itemsize for array in arrays)
    return pl.pallas_call(
        body,
        out_shape=[jax.ShapeDtypeStruct(shape, kind) for shape, kind in outs],
        in_specs=[pl.BlockSpec(memory_space=pltpu.SMEM)] * len(scalars)
        + [pl.BlockSpec(memory_space=pltpu.VMEM)] * len(arrays),
        out_specs=[pl.BlockSpec(memory_space=pltpu.VMEM)] * len(outs),
        compiler_params=pltpu.CompilerParams(vmem_limit_bytes=ROOM),
        cost_estimate=pl.CostEstimate(flops=flops, bytes_accessed=in_bytes, transcendentals=0),
    )(*scalars, *arrays)


def spread_kernel(terms, base_ref, *refs):
    total = base_ref[...].astype(jnp.float32)
    for term in range(terms):
        half_ref, near_ref, far_ref = refs[3 * term : 3 * term + 3]
        values = jnp.concatenate([near_ref[...], far_ref[...]], axis=0)
        total = total + times_transposed(half_ref[...], values)
    block = total.astype(jnp.bfloat16)
    for step, out_ref in enumerate(refs[3 * terms :]):

        @pl.when(pl.program_id(0) == step)
        def _():
            out_ref[...] = block


def spread(base, terms):
    arrays = [base] + [array for term in terms for array in term]
    height, width = base.shape
    count = height // CHIPS

    def rows(columns):
        return pl.BlockSpec((count, columns), lambda step: (step, 0))

    def whole(array):
        return pl.BlockSpec(array.shape, lambda step: (0, 0))

    specs = [rows(width)]
    for half, near, far in terms:
        specs += [rows(half.shape[1]), whole(near), whole(far)]

    def body(*refs):
        spread_kernel(len(terms), *refs)

    return pl.pallas_call(
        body,
        name="spread",
        grid=(CHIPS,),
        out_shape=[jax.ShapeDtypeStruct((count, width), jnp.bfloat16)] * CHIPS,
        in_specs=specs,
        out_specs=[pl.BlockSpec((count, width), lambda step: (0, 0))] * CHIPS,
        compiler_params=pltpu.CompilerParams(vmem_limit_bytes=ROOM),
        cost_estimate=pl.CostEstimate(
            flops=2 * height * width * terms[0][0].shape[1] * len(terms),
            bytes_accessed=sum(array.size * array.dtype.itemsize for array in arrays),
            transcendentals=0,
        ),
    )(*arrays)


def pair_products(block_ref, near_ref, far_ref):
    return dot(block_ref[...], jnp.concatenate([near_ref[...], far_ref[...]], axis=0))


def factor_kernel(start, *refs):
    total_ref = refs[-1]
    total = refs[0][...] if start else None
    refs = refs[1:-1] if start else refs[:-1]
    for step in range(CHIPS):
        term = pair_products(refs[step], refs[CHIPS + step], refs[2 * CHIPS + step])
        total = term if total is None else total + term
    total_ref[...] = total


def factor_rows(total, blocks, pieces):
    arrays = ([] if total is None else [total]) + blocks + pieces
    count, ranks = blocks[0].shape[0], pieces[0].shape[1]

    def body(*refs):
        factor_kernel(total is not None, *refs)

    return pl.pallas_call(
        body,
        out_shape=jax.ShapeDtypeStruct((count, ranks), jnp.float32),
        in_specs=[pl.BlockSpec(memory_space=pltpu.VMEM)] * len(arrays),
        out_specs=pl.BlockSpec(memory_space=pltpu.VMEM),
        compiler_params=pltpu.CompilerParams(vmem_limit_bytes=ROOM),
        cost_estimate=pl.CostEstimate(
            flops=2 * count * ranks * len(pieces) * pieces[0].shape[0],
            bytes_accessed=sum(array.size * array.dtype.itemsize for array in arrays),
            transcendentals=0,
        ),
    )(*arrays)


def after(value, earlier):
    return lax.optimization_barrier((value, earlier))[0]


def gathered_plan(inputs, teacher, gate, route, slot, factor, cores):
    bf16, f32 = jnp.bfloat16, jnp.float32
    shared = factor[0]
    channels, ranks = shared.shape
    devices = lax.axis_size("expert")
    micro_count, token_count = route.shape[1:]
    rows = micro_count * token_count
    here = lax.axis_index("expert")
    chip, core = here // CORES, here % CORES
    middle = jnp.logical_or(chip == 1, chip == 2)
    tokens = inputs[0].reshape(rows, channels)

    travelled = gather_cores(cores[0, 0])
    marks = row_marks(
        route[0].reshape(rows, 1), gate[0].reshape(rows, 1), chip, core, middle
    )

    down = [(3, 2), (1, 0)]
    two_down = [(3, 1), (2, 0)]
    two_cross, down_cross = [(0, 1)], [(2, 0)]
    own_half = chip_blocks(shared, chip, core)
    half_down = between_layers(own_half, down)
    half_two = between_layers(own_half, two_down)
    half_cross = between_layers(half_two, two_cross)
    half_late = between_layers(half_down, down_cross)
    turned = lax.optimization_barrier(tokens.T)
    wanted = lax.optimization_barrier(teacher[0].reshape(rows, channels).T)
    difference = (turned.astype(f32) - wanted.astype(f32)).astype(bf16)
    difference = chip_columns(difference, chip, core)
    step_down = between_layers(difference, down)
    step_two = between_layers(difference, two_down)

    capacity = max(2, 2 * token_count // devices)
    slots = micro_count * capacity
    micro = jnp.arange(rows, dtype=jnp.int32) // token_count
    expert = route[0].reshape(rows)
    near = (expert % CORES ^ core) * CHIPS + (expert // CORES ^ chip)
    place = near * slots + micro * capacity + slot[0].reshape(rows)
    picks = (jnp.arange(devices * slots, dtype=jnp.int32)[:, None] == place[None, :]).astype(bf16)

    def to_slots(values):
        held = dot(picks, values).astype(bf16)
        half = CHIPS * slots
        own, theirs = held[:half], swap_cores(held[half:])
        return [
            jnp.concatenate([part[step * slots : (step + 1) * slots] for part in (own, theirs)])
            for step in range(CHIPS)
        ]

    def to_experts(parts):
        return parts[:1] + [across_chips(parts[step], step) for step in range(1, CHIPS)]

    step_cross = between_layers(step_two, two_cross)
    step_late = between_layers(step_down, down_cross)
    projected = dot(tokens, shared).astype(bf16)
    own_gram = gram_pair(own_half, own_half)
    proj_slots = to_slots(projected)
    gram = gram_sum(own_gram)
    own_score = both_cores(dot_first(difference, own_half))
    turned = chip_columns(turned, chip, core)
    token_blocks = [
        turned[step * channels // devices : (step + 1) * channels // devices]
        for step in range(CHIPS)
    ]
    down_gram = gram_sum(gram_pair(half_down, own_half))
    two_gram = gram_sum(gram_pair(half_two, own_half))
    down_score = both_cores(dot_first(step_down, own_half))

    wide = (rows, ranks)
    product_flops = 2 * rows * ranks * ranks
    flag = middle.astype(jnp.int32).reshape(1)
    block = pltpu.VMEM((ranks, ranks), bf16)

    def core_call(body, sources, outs, arrays, scratch, products):
        flat = [ref for source in sources for ref in (source if type(source) is tuple else [source])]
        return pl.pallas_call(
            body,
            out_shape=outs,
            in_specs=[pl.BlockSpec(memory_space=pltpu.SMEM)]
            + [pl.BlockSpec(memory_space=pltpu.VMEM)] * len(arrays)
            + [pl.BlockSpec(memory_space=pl.ANY)] * len(flat),
            out_specs=[pl.BlockSpec(memory_space=pltpu.VMEM)] * len(outs),
            scratch_shapes=scratch + [pltpu.SemaphoreType.DMA((len(sources),))],
            compiler_params=pltpu.CompilerParams(vmem_limit_bytes=ROOM),
            cost_estimate=pl.CostEstimate(
                flops=product_flops * products,
                bytes_accessed=2 * len(sources) * ranks * ranks,
                transcendentals=0,
            ),
        )(flag, *arrays, *flat)

    part, *held = core_call(
        early_kernel,
        travelled[:-2],
        [jax.ShapeDtypeStruct(wide, f32)] + [block] * (devices - 2),
        [projected, marks],
        [],
        devices - 2,
    )
    scaled, slope, score, chain, *last = core_call(
        first_kernel,
        [*travelled[-2:], own_score, gram],
        [jax.ShapeDtypeStruct(wide, kind) for kind in (bf16, f32, f32, bf16)] + [block] * 2,
        [projected, marks, part, *held],
        [pltpu.VMEM(wide, f32), pltpu.VMEM((ranks, ranks), bf16)],
        devices + 3,
    )
    pieces = [*held, *last]

    def turn(score, late, terms):
        arrays = [array for pair in terms for array in pair]

        def body(*refs):
            turn_kernel(len(terms), bool(late), *refs)

        return call_rows(
            body,
            [(wide, f32), (wide, bf16), (wide, bf16), (wide, bf16)],
            [marks, scaled, slope, score, *late, *arrays, *pieces],
            product_flops * (devices + len(terms)),
        )

    chain_first = chain
    first_down = between_layers(chain, [(3, 2)])
    first_two = between_layers(chain, [(3, 1)])
    scaled_rows = [scaled] + [across_chips(after(scaled, chain), step) for step in range(1, CHIPS)]
    token_blocks = token_blocks[:1] + [
        across_chips(after(token_blocks[step], chain), step) for step in range(1, CHIPS)
    ]
    score, _, _, chain = turn(score, [down_score], [(first_down, down_gram)])

    second_cross = between_layers(chain, [(2, 1)])
    second_two = between_layers(chain, [(2, 0)])
    first_three = between_layers(after(chain_first, chain), [(3, 0)])
    proj_slots = to_experts([after(part, chain) for part in proj_slots])
    half_cross = after(half_cross, chain)
    step_cross = after(step_cross, chain)
    cross_pair = gram_pair(half_cross, own_half)
    late_steps = (step_two.astype(f32) + step_cross.astype(f32)).astype(bf16)
    late_score = both_cores(dot_first(late_steps, own_half))
    cross_product = gram_sum(cross_pair)
    score, _, _, chain = turn(
        score, [late_score], [(first_two, two_gram), (second_cross, cross_product)]
    )

    third_down = between_layers(chain, [(1, 0)])
    half_late, step_late = after(half_late, chain), after(step_late, chain)
    late_pair = gram_pair(half_late, own_half)
    last_score = both_cores(dot_first(step_late, own_half))
    steps_total = difference.astype(f32) + step_down.astype(f32)
    steps_total = steps_total + after(late_steps, chain).astype(f32)
    steps_total = (steps_total + step_late.astype(f32)).astype(bf16)
    late_product = gram_sum(late_pair)
    score, grad_pre, grad_proj, _ = turn(
        score,
        [last_score],
        [(second_two, two_gram), (first_three, late_product), (third_down, down_gram)],
    )

    def with_swap(values):
        return values, swap_cores(values)

    proj_rows = gather_rows(grad_proj)
    scaled_pair = with_swap(after(scaled, grad_proj))
    two_pair = with_swap(first_two + after(second_two, grad_proj))
    cross_pair = with_swap(after(second_cross, grad_proj))
    late_pair = with_swap(after(first_three, grad_proj))
    down_pair = with_swap(first_down + third_down)
    mixed_blocks = spread(
        steps_total,
        [
            (own_half, *scaled_pair),
            (half_two, *two_pair),
            (half_cross, *cross_pair),
            (half_late, *late_pair),
            (half_down, *down_pair),
        ],
    )
    mixed_first = mixed_blocks[0]
    scaled_rows = [after(rows, mixed_first) for rows in scaled_rows]
    mixed_blocks = list(mixed_blocks[:1]) + [
        across_chips(mixed_blocks[step], step) for step in range(1, CHIPS)
    ]
    grad_slots = to_slots(after(grad_pre, mixed_first))
    grad_slots = to_experts(grad_slots)
    scaled_rows = scaled_rows + [scaled_pair[1]] + [swap_cores(rows) for rows in scaled_rows[1:]]
    share = factor_rows(None, token_blocks, proj_rows)
    core_total = dot_first(jnp.concatenate(proj_slots), jnp.concatenate(grad_slots)).astype(bf16)
    share = factor_rows(after(share, core_total), mixed_blocks, scaled_rows)
    return (share[None], core_total[None, None])


def solution(mesh):
    placed = (
        P("section", None, "expert", None),
        P("section", None, "expert", None),
        P("section", None, "expert"),
        P("section", None, "expert"),
        P("section", None, "expert"),
        P("section", None, None),
        P("section", "expert", None, None),
    )
    drawn_for = (LAYERS, CHIPS * CORES)

    def per_device(*arrays):
        local_experts = arrays[-1].shape[1]
        if (mesh.shape["section"], mesh.shape["expert"]) == drawn_for and local_experts == 1:
            return gathered_plan(*arrays)
        return general_plan(*arrays)

    return jax.shard_map(
        per_device,
        mesh=mesh,
        in_specs=placed,
        out_specs=(P("section", "expert", None), P("section", "expert", None, None)),
        check_vma=False,
    )
```

```python
import jax
import jax.numpy as jnp
from jax import lax
from jax.experimental import pallas as pl
from jax.experimental.pallas import tpu as pltpu
from jax.sharding import PartitionSpec as P


def from_behind(value, axis, steps):
    count = lax.axis_size(axis)
    leading, last = (max(0, -steps), min(count, count - steps))
    return lax.ppermute(value, axis, [(source, source + steps) for source in range(leading, last)])


def silu_slope(values):
    sigmoid = jax.nn.sigmoid(values)
    return sigmoid * (1.0 + values * (1.0 - sigmoid))


def times_transposed(left, shared):
    return lax.dot_general(
        left, shared, (((1,), (1,)), ((), ())), preferred_element_type=jnp.float32
    )


def factor_terms(tokens_flat, proj_flat, mixed_flat, hidden_flat):

    def factor_rows(start, count):
        first_term = lax.dot_general(
            tokens_flat, proj_flat, (((0,), (0,)), ((), ())), preferred_element_type=jnp.float32
        )
        second_term = lax.dot_general(
            mixed_flat, hidden_flat, (((0,), (0,)), ((), ())), preferred_element_type=jnp.float32
        )
        return first_term + second_term

    return factor_rows


def store_slice(store, fresh, picked, usable):
    former = lax.dynamic_index_in_dim(store, picked, 0, keepdims=False)
    kept = jnp.where(usable, fresh, former)
    return lax.dynamic_update_index_in_dim(store, kept, picked, 0)


def general_plan(inputs, teacher, gate, route, slot, factor, cores):
    tokens_all = inputs[0]
    targets_all = teacher[0]
    weights_all = gate[0]
    shared = factor[0]
    blocks = cores[0]
    micro_count, token_count, channels = tokens_all.shape
    ranks = shared.shape[1]
    local_experts = blocks.shape[0]
    expert_devices = lax.axis_size("expert")
    capacity = max(2, 2 * token_count // (local_experts * expert_devices))
    slot_count = local_experts * expert_devices * capacity
    places_all = route[0] * capacity + slot[0]
    micro_range = jnp.arange(micro_count, dtype=jnp.int32)[:, None]
    token_proj = jnp.dot(
        tokens_all.reshape(-1, channels), shared, preferred_element_type=jnp.float32
    ).astype(jnp.bfloat16)
    token_proj = token_proj.reshape(micro_count, token_count, ranks)
    proj_slots = (
        jnp.zeros((micro_count, slot_count, ranks), jnp.bfloat16)
        .at[micro_range, places_all]
        .set(token_proj)
    )
    projected = lax.all_to_all(proj_slots, "expert", split_axis=1, concat_axis=1, tiled=True)
    projected = projected.reshape(micro_count, expert_devices, local_experts, capacity, ranks)
    pre = jnp.einsum("mnecr,erk->mneck", projected, blocks, preferred_element_type=jnp.float32)
    active = jax.nn.silu(pre).astype(jnp.bfloat16)
    returned = lax.all_to_all(
        active.reshape(micro_count, slot_count, ranks),
        "expert",
        split_axis=1,
        concat_axis=1,
        tiled=True,
    )
    hidden = jnp.take_along_axis(returned, places_all[:, :, None], axis=1)
    mixed = times_transposed(hidden.reshape(-1, ranks), shared).reshape(
        micro_count, token_count, channels
    )
    output = tokens_all.astype(jnp.float32) + weights_all[:, :, None] * mixed
    errors = output - targets_all.astype(jnp.float32)
    section_count = lax.axis_size("section")
    section_here = lax.axis_index("section")
    incoming = jnp.zeros((token_count, channels), jnp.bfloat16)
    mixed_store = jnp.zeros((micro_count, token_count, channels), jnp.bfloat16)
    proj_store = jnp.zeros((micro_count, token_count, ranks), jnp.bfloat16)
    pre_store = jnp.zeros(
        (micro_count, expert_devices, local_experts, capacity, ranks), jnp.bfloat16
    )
    turn_total = micro_count + section_count - 1
    for turn_index in range(turn_total):
        micro_now = turn_index - (section_count - 1 - section_here)
        usable = jnp.logical_and(micro_now >= 0, micro_now < micro_count)
        picked = jnp.clip(micro_now, 0, micro_count - 1)
        grad_out = lax.dynamic_index_in_dim(errors, picked, 0, keepdims=False) + incoming.astype(
            jnp.float32
        )
        weight_now = lax.dynamic_index_in_dim(weights_all, picked, 0, keepdims=False)
        places = lax.dynamic_index_in_dim(places_all, picked, 0, keepdims=False)
        grad_mixed = (weight_now[:, None] * grad_out).astype(jnp.bfloat16)
        grad_hidden = jnp.dot(grad_mixed, shared, preferred_element_type=jnp.float32).astype(
            jnp.bfloat16
        )
        grad_slots = jnp.zeros((slot_count, ranks), jnp.bfloat16).at[places].set(grad_hidden)
        grad_recv = lax.all_to_all(grad_slots, "expert", split_axis=0, concat_axis=0, tiled=True)
        grad_recv = grad_recv.reshape(expert_devices, local_experts, capacity, ranks)
        pre_now = lax.dynamic_index_in_dim(pre, picked, 0, keepdims=False)
        grad_pre = (grad_recv.astype(jnp.float32) * silu_slope(pre_now)).astype(jnp.bfloat16)
        grad_routed = jnp.einsum(
            "neck,erk->necr", grad_pre, blocks, preferred_element_type=jnp.float32
        ).astype(jnp.bfloat16)
        grad_home = lax.all_to_all(
            grad_routed.reshape(slot_count, ranks),
            "expert",
            split_axis=0,
            concat_axis=0,
            tiled=True,
        )
        grad_proj = grad_home[places]
        grad_in = (grad_out + times_transposed(grad_proj, shared)).astype(jnp.bfloat16)
        if turn_index + 1 < turn_total:
            incoming = from_behind(grad_in, "section", -1)
        mixed_store = store_slice(mixed_store, grad_mixed, picked, usable)
        proj_store = store_slice(proj_store, grad_proj, picked, usable)
        pre_store = store_slice(pre_store, grad_pre, picked, usable)
    core_total = jnp.einsum(
        "mnecr,mneck->erk", projected, pre_store, preferred_element_type=jnp.float32
    )
    all_rows = factor_terms(
        tokens_all.reshape(-1, channels),
        proj_store.reshape(-1, ranks),
        mixed_store.reshape(-1, channels),
        hidden.reshape(-1, ranks),
    )
    factor_share = lax.psum_scatter(
        all_rows(jnp.int32(0), channels // expert_devices * lax.axis_size("expert")),
        "expert",
        scatter_dimension=0,
        tiled=True,
    )
    return (factor_share[None], core_total.astype(jnp.bfloat16)[None])


CORES = 2
CHIPS = 4
LAYERS = 4
ROOM = 16 * 2**20


def dot(left, right):
    return jnp.dot(left, right, preferred_element_type=jnp.float32)


def dot_first(left, right):
    return lax.dot_general(
        left, right, (((0,), (0,)), ((), ())), preferred_element_type=jnp.float32
    )


def on_chips(value, pairs):
    perm = [
        (CORES * source + core, CORES * target + core)
        for source, target in pairs
        for core in range(CORES)
    ]
    return lax.ppermute(value, "expert", perm)


def swap_cores(value):
    count = lax.axis_size("expert")
    return lax.ppermute(value, "expert", [(index, index ^ 1) for index in range(count)])


def between_layers(value, pairs):
    return lax.ppermute(value, "section", pairs)


def gather_cores(core):
    beside = on_chips(core, [(0, 1), (1, 0), (2, 3), (3, 2)])
    across = on_chips(core, [(1, 2), (2, 1)])
    far_across = on_chips(beside, [(1, 2), (2, 1)])
    outward = on_chips(across, [(1, 0), (2, 3)])
    far_outward = on_chips(far_across, [(1, 0), (2, 3)])
    held, swapped = [core, beside], [swap_cores(piece) for piece in (core, beside)]
    near = [(across, outward), (far_across, far_outward)]
    far = [tuple(swap_cores(piece) for piece in pair) for pair in near]
    return [piece for both in zip(held + near, swapped + far) for piece in both]


def row_marks(route, weight, chip, core, middle):
    count = CHIPS * CORES
    place = lax.broadcasted_iota(jnp.int32, (1, 2 * count), 1)
    step = (place % count) // CORES
    turned = jnp.where(jnp.logical_and(step >= 2, middle), 5 - step, step)
    expert = CORES * (chip ^ turned) + (core ^ (place % CORES))
    marks = (route == expert).astype(jnp.float32)
    return jnp.where(place < count, marks, weight)


def across_chips(value, step):
    return on_chips(value, [(chip, chip ^ step) for chip in range(CHIPS)])


def gather_rows(rows):
    held = [rows] + [across_chips(rows, step) for step in range(1, CHIPS)]
    return held + [swap_cores(piece) for piece in held]


def chip_blocks(wide, chip, core):
    count = wide.shape[0] // (CHIPS * CORES)
    blocks = [
        lax.dynamic_slice_in_dim(wide, (CORES * (chip ^ step) + core) * count, count, 0)
        for step in range(CHIPS)
    ]
    return jnp.concatenate(blocks, axis=0)


def chip_columns(wide, chip, core):
    theirs = swap_cores(chip_blocks(wide, chip, 1 - core))
    return jnp.concatenate([chip_blocks(wide, chip, core), theirs], axis=1)


def both_cores(partial):
    rows = partial.shape[0] // CORES
    return partial[:rows] + swap_cores(partial[rows:])


def gram_pair(left, right):
    partial = dot_first(left, right).astype(jnp.bfloat16)
    return partial, swap_cores(partial)


def gram_sum(pair):
    return (pair[0].astype(jnp.float32) + pair[1].astype(jnp.float32)).astype(jnp.bfloat16)


def routed_product(rows, marks, start, core_refs, transposed, copies=None):
    dims = (((1,), (1 if transposed else 0,)), ((), ()))
    total = None
    for place, core_ref in enumerate(core_refs):
        if copies is not None:
            copies[place].wait()
        mark = marks[:, start + place : start + place + 1]
        chosen = jnp.where(mark > 0.5, rows, jnp.zeros_like(rows))
        term = lax.dot_general(
            chosen, core_ref[...], dims, preferred_element_type=jnp.float32
        )
        total = term if total is None else total + term
    return total


def backward_rows(score, slope, marks, core_refs):
    count = len(core_refs)
    grad_hidden = (marks[:, count : count + 1] * score).astype(jnp.bfloat16)
    grad_pre = (grad_hidden.astype(jnp.float32) * slope).astype(jnp.bfloat16)
    grad_proj = routed_product(grad_pre, marks, 0, core_refs, True)
    return grad_pre, grad_proj.astype(jnp.bfloat16)


def fetch(middle, sources, targets, arrived):
    copies = []
    for place, (source, target) in enumerate(zip(sources, targets)):
        choices = source if isinstance(source, tuple) else (source,)
        moves = [pltpu.make_async_copy(ref, target, arrived.at[place]) for ref in choices]
        copies.append(moves[0])
        if len(moves) == 1:
            moves[0].start()
        else:
            pl.when(middle)(moves[0].start)
            pl.when(jnp.logical_not(middle))(moves[1].start)
    return copies


def early_kernel(middle_ref, proj_ref, marks_ref, *refs):
    sources = [*refs[:4], (refs[4], refs[5]), (refs[6], refs[7])]
    part_ref, core_refs, arrived = refs[8], refs[9:-1], refs[-1]
    copies = fetch(middle_ref[0] > 0, sources, core_refs, arrived)
    part_ref[...] = routed_product(proj_ref[...], marks_ref[...], 0, core_refs, False, copies)


def first_kernel(middle_ref, proj_ref, marks_ref, part_ref, *refs):
    early = CHIPS * CORES - 2
    held, refs = refs[:early], refs[early:]
    sources = [(refs[0], refs[1]), (refs[2], refs[3]), refs[4], refs[5]]
    scaled_ref, slope_ref, score_ref, chain_ref, near_ref, far_ref = refs[6:12]
    own_ref, gram_ref, arrived = refs[12:]
    last = [near_ref, far_ref]
    copies = fetch(middle_ref[0] > 0, sources, [*last, own_ref, gram_ref], arrived)
    core_refs, count = [*held, *last], early + 2
    marks = marks_ref[...]
    pre = part_ref[...] + routed_product(proj_ref[...], marks, early, last, False, copies)
    sigmoid = 1.0 / (1.0 + jnp.exp(-pre))
    hidden = (pre * sigmoid).astype(jnp.bfloat16)
    slope = sigmoid * (1.0 + pre * (1.0 - sigmoid))
    weight = marks[:, count : count + 1]
    scaled = (weight * hidden.astype(jnp.float32)).astype(jnp.bfloat16)
    copies[2].wait()
    copies[3].wait()
    score = own_ref[...] + dot(scaled, gram_ref[...])
    scaled_ref[...] = scaled
    slope_ref[...] = slope
    score_ref[...] = score
    _, grad_proj = backward_rows(score, slope, marks, core_refs)
    chain_ref[...] = (scaled.astype(jnp.float32) + grad_proj.astype(jnp.float32)).astype(
        jnp.bfloat16
    )


def turn_kernel(terms, late, marks_ref, scaled_ref, slope_ref, score_ref, *refs):
    score = score_ref[...]
    if late:
        score, refs = score + refs[0][...], refs[1:]
    core_refs = refs[2 * terms : len(refs) - 4]
    next_ref, grad_ref, proj_ref, chain_ref = refs[len(refs) - 4 :]
    for term in range(terms):
        score = score + dot(refs[2 * term][...], refs[2 * term + 1][...])
    next_ref[...] = score
    grad_pre, grad_proj = backward_rows(score, slope_ref[...], marks_ref[...], core_refs)
    grad_ref[...] = grad_pre
    proj_ref[...] = grad_proj
    chain_ref[...] = (scaled_ref[...].astype(jnp.float32) + grad_proj.astype(jnp.float32)).astype(
        jnp.bfloat16
    )


def call_rows(body, outs, arrays, flops, scalars=()):
    in_bytes = sum(array.size * array.dtype.itemsize for array in arrays)
    return pl.pallas_call(
        body,
        out_shape=[jax.ShapeDtypeStruct(shape, kind) for shape, kind in outs],
        in_specs=[pl.BlockSpec(memory_space=pltpu.SMEM)] * len(scalars)
        + [pl.BlockSpec(memory_space=pltpu.VMEM)] * len(arrays),
        out_specs=[pl.BlockSpec(memory_space=pltpu.VMEM)] * len(outs),
        compiler_params=pltpu.CompilerParams(vmem_limit_bytes=ROOM),
        cost_estimate=pl.CostEstimate(flops=flops, bytes_accessed=in_bytes, transcendentals=0),
    )(*scalars, *arrays)


def spread_kernel(terms, base_ref, *refs):
    total = base_ref[...].astype(jnp.float32)
    for term in range(terms):
        half_ref, near_ref, far_ref = refs[3 * term : 3 * term + 3]
        values = jnp.concatenate([near_ref[...], far_ref[...]], axis=0)
        total = total + times_transposed(half_ref[...], values)
    block = total.astype(jnp.bfloat16)
    slot_refs, outs = refs[3 * terms : 3 * terms + 2], refs[3 * terms + 2 :]
    count, width = block.shape
    for step, out_ref in enumerate(outs):

        @pl.when(pl.program_id(0) == step)
        def _():
            out_ref[:count, :] = block
            for part, (row, column, slots) in enumerate(slot_tiles(slot_refs[0], width)):
                slot_ref = slot_refs[part % CORES]
                out_ref[pl.ds(count + row, slots), :] = slot_ref[
                    step * slots : (step + 1) * slots, column : column + width
                ]


def slot_tiles(slot_ref, width):
    slots = slot_ref.shape[0] // CHIPS
    groups = slot_ref.shape[1] // width
    return [
        ((CORES * group + side) * slots, group * width, slots)
        for group in range(groups)
        for side in range(CORES)
    ]


def under_block(block, own, theirs, step):
    width = block.shape[1]
    parts = [
        (own, theirs)[part % CORES][step * slots : (step + 1) * slots, column : column + width]
        for part, (_, column, slots) in enumerate(slot_tiles(own, width))
    ]
    return jnp.concatenate([block, *parts], axis=0)


def spread(base, terms, own_slots, their_slots):
    arrays = [base] + [array for term in terms for array in term] + [own_slots, their_slots]
    height, width = base.shape
    count = height // CHIPS
    tall = count + CORES * own_slots.size // (CHIPS * width)

    def rows(columns):
        return pl.BlockSpec((count, columns), lambda step: (step, 0))

    def whole(array):
        return pl.BlockSpec(array.shape, lambda step: (0, 0))

    specs = [rows(width)]
    for half, near, far in terms:
        specs += [rows(half.shape[1]), whole(near), whole(far)]
    specs += [whole(own_slots), whole(their_slots)]

    def body(*refs):
        spread_kernel(len(terms), *refs)

    return pl.pallas_call(
        body,
        name="spread",
        grid=(CHIPS,),
        out_shape=[jax.ShapeDtypeStruct((tall, width), jnp.bfloat16)] * CHIPS,
        in_specs=specs,
        out_specs=[pl.BlockSpec((tall, width), lambda step: (0, 0))] * CHIPS,
        compiler_params=pltpu.CompilerParams(vmem_limit_bytes=ROOM),
        cost_estimate=pl.CostEstimate(
            flops=2 * height * width * terms[0][0].shape[1] * len(terms),
            bytes_accessed=sum(array.size * array.dtype.itemsize for array in arrays),
            transcendentals=0,
        ),
    )(*arrays)


def pair_products(block_ref, count, near_ref, far_ref):
    return dot(block_ref[:count, :], jnp.concatenate([near_ref[...], far_ref[...]], axis=0))


def block_products(count, refs):
    total = None
    for step in range(CHIPS):
        term = pair_products(refs[step], count, refs[CHIPS + step], refs[2 * CHIPS + step])
        total = term if total is None else total + term
    return total


def token_kernel(*refs):
    refs[-1][...] = block_products(refs[-1].shape[0], refs[:-1])


def last_kernel(*refs):
    token_refs, refs = refs[:CHIPS], refs[CHIPS:]
    total_ref, product_refs = refs[0], refs[1:-2]
    share_ref, core_ref = refs[-2:]
    count = share_ref.shape[0]
    share_ref[...] = total_ref[...] + block_products(count, product_refs)
    width = token_refs[0].shape[1]
    slots = (token_refs[0].shape[0] - count) * width // core_ref.shape[0]

    def group(block_refs, column):
        start = count + column * slots
        return jnp.concatenate([ref[start : start + slots, :] for ref in block_refs], axis=0)

    groups = core_ref.shape[0] // width
    for left in range(groups):
        for right in range(groups):
            product = dot_first(group(token_refs, left), group(product_refs[:CHIPS], right))
            core_ref[
                left * width : (left + 1) * width, right * width : (right + 1) * width
            ] = product.astype(jnp.bfloat16)


def block_call(body, outs, arrays, flops):
    return pl.pallas_call(
        body,
        out_shape=outs,
        in_specs=[pl.BlockSpec(memory_space=pltpu.VMEM)] * len(arrays),
        out_specs=[pl.BlockSpec(memory_space=pltpu.VMEM)] * len(outs),
        compiler_params=pltpu.CompilerParams(vmem_limit_bytes=ROOM),
        cost_estimate=pl.CostEstimate(
            flops=flops,
            bytes_accessed=sum(array.size * array.dtype.itemsize for array in arrays),
            transcendentals=0,
        ),
    )(*arrays)


def after(value, earlier):
    return lax.optimization_barrier((value, earlier))[0]


def gathered_plan(inputs, teacher, gate, route, slot, factor, cores):
    bf16, f32 = jnp.bfloat16, jnp.float32
    shared = factor[0]
    channels, ranks = shared.shape
    devices = lax.axis_size("expert")
    micro_count, token_count = route.shape[1:]
    rows = micro_count * token_count
    here = lax.axis_index("expert")
    chip, core = here // CORES, here % CORES
    middle = jnp.logical_or(chip == 1, chip == 2)
    tokens = inputs[0].reshape(rows, channels)

    travelled = gather_cores(cores[0, 0])
    marks = row_marks(
        route[0].reshape(rows, 1), gate[0].reshape(rows, 1), chip, core, middle
    )

    down = [(3, 2), (1, 0)]
    two_down = [(3, 1), (2, 0)]
    two_cross, down_cross = [(0, 1)], [(2, 0)]
    own_half = chip_blocks(shared, chip, core)
    half_down = between_layers(own_half, down)
    half_two = between_layers(own_half, two_down)
    half_cross = between_layers(half_two, two_cross)
    half_late = between_layers(half_down, down_cross)
    turned = lax.optimization_barrier(tokens.T)
    wanted = lax.optimization_barrier(teacher[0].reshape(rows, channels).T)
    difference = (turned.astype(f32) - wanted.astype(f32)).astype(bf16)
    difference = chip_columns(difference, chip, core)
    step_down = between_layers(difference, down)
    step_two = between_layers(difference, two_down)

    capacity = max(2, 2 * token_count // devices)
    slots = micro_count * capacity
    micro = jnp.arange(rows, dtype=jnp.int32) // token_count
    expert = route[0].reshape(rows)
    near = (expert % CORES ^ core) * CHIPS + (expert // CORES ^ chip)
    place = near * slots + micro * capacity + slot[0].reshape(rows)
    picks = (jnp.arange(devices * slots, dtype=jnp.int32)[:, None] == place[None, :]).astype(bf16)

    def to_slots(values):
        held = dot(picks, values).astype(bf16)
        half = CHIPS * slots
        return held[:half], swap_cores(held[half:])

    step_cross = between_layers(step_two, two_cross)
    step_late = between_layers(step_down, down_cross)
    projected = dot(tokens, shared).astype(bf16)
    own_gram = gram_pair(own_half, own_half)
    proj_slots = to_slots(projected)
    gram = gram_sum(own_gram)
    own_score = both_cores(dot_first(difference, own_half))
    turned = chip_columns(turned, chip, core)
    token_blocks = [
        under_block(
            turned[step * channels // devices : (step + 1) * channels // devices],
            *proj_slots,
            step,
        )
        for step in range(CHIPS)
    ]
    down_gram = gram_sum(gram_pair(half_down, own_half))
    two_gram = gram_sum(gram_pair(half_two, own_half))
    down_score = both_cores(dot_first(step_down, own_half))

    wide = (rows, ranks)
    product_flops = 2 * rows * ranks * ranks
    flag = middle.astype(jnp.int32).reshape(1)
    block = pltpu.VMEM((ranks, ranks), bf16)

    def core_call(body, sources, outs, arrays, scratch, products):
        flat = [ref for source in sources for ref in (source if type(source) is tuple else [source])]
        return pl.pallas_call(
            body,
            out_shape=outs,
            in_specs=[pl.BlockSpec(memory_space=pltpu.SMEM)]
            + [pl.BlockSpec(memory_space=pltpu.VMEM)] * len(arrays)
            + [pl.BlockSpec(memory_space=pl.ANY)] * len(flat),
            out_specs=[pl.BlockSpec(memory_space=pltpu.VMEM)] * len(outs),
            scratch_shapes=scratch + [pltpu.SemaphoreType.DMA((len(sources),))],
            compiler_params=pltpu.CompilerParams(vmem_limit_bytes=ROOM),
            cost_estimate=pl.CostEstimate(
                flops=product_flops * products,
                bytes_accessed=2 * len(sources) * ranks * ranks,
                transcendentals=0,
            ),
        )(flag, *arrays, *flat)

    part, *held = core_call(
        early_kernel,
        travelled[:-2],
        [jax.ShapeDtypeStruct(wide, f32)] + [block] * (devices - 2),
        [projected, marks],
        [],
        devices - 2,
    )
    scaled, slope, score, chain, *last = core_call(
        first_kernel,
        [*travelled[-2:], own_score, gram],
        [jax.ShapeDtypeStruct(wide, kind) for kind in (bf16, f32, f32, bf16)] + [block] * 2,
        [projected, marks, part, *held],
        [pltpu.VMEM(wide, f32), pltpu.VMEM((ranks, ranks), bf16)],
        devices + 3,
    )
    pieces = [*held, *last]

    def turn(score, late, terms):
        arrays = [array for pair in terms for array in pair]

        def body(*refs):
            turn_kernel(len(terms), bool(late), *refs)

        return call_rows(
            body,
            [(wide, f32), (wide, bf16), (wide, bf16), (wide, bf16)],
            [marks, scaled, slope, score, *late, *arrays, *pieces],
            product_flops * (devices + len(terms)),
        )

    chain_first = chain
    first_down = between_layers(chain, [(3, 2)])
    first_two = between_layers(chain, [(3, 1)])
    scaled_rows = [scaled] + [across_chips(after(scaled, chain), step) for step in range(1, CHIPS)]
    token_blocks = token_blocks[:1] + [
        across_chips(after(token_blocks[step], chain), step) for step in range(1, CHIPS)
    ]
    score, _, _, chain = turn(score, [down_score], [(first_down, down_gram)])

    second_cross = between_layers(chain, [(2, 1)])
    second_two = between_layers(chain, [(2, 0)])
    first_three = between_layers(after(chain_first, chain), [(3, 0)])
    half_cross = after(half_cross, chain)
    step_cross = after(step_cross, chain)
    cross_pair = gram_pair(half_cross, own_half)
    late_steps = (step_two.astype(f32) + step_cross.astype(f32)).astype(bf16)
    late_score = both_cores(dot_first(late_steps, own_half))
    cross_product = gram_sum(cross_pair)
    score, _, _, chain = turn(
        score, [late_score], [(first_two, two_gram), (second_cross, cross_product)]
    )

    third_down = between_layers(chain, [(1, 0)])
    half_late, step_late = after(half_late, chain), after(step_late, chain)
    late_pair = gram_pair(half_late, own_half)
    last_score = both_cores(dot_first(step_late, own_half))
    steps_total = difference.astype(f32) + step_down.astype(f32)
    steps_total = steps_total + after(late_steps, chain).astype(f32)
    steps_total = (steps_total + step_late.astype(f32)).astype(bf16)
    late_product = gram_sum(late_pair)
    score, grad_pre, grad_proj, _ = turn(
        score,
        [last_score],
        [(second_two, two_gram), (first_three, late_product), (third_down, down_gram)],
    )

    def with_swap(values):
        return values, swap_cores(values)

    proj_rows = gather_rows(grad_proj)
    grad_slots = to_slots(grad_pre)
    scaled_pair = with_swap(after(scaled, grad_proj))
    two_pair = with_swap(first_two + after(second_two, grad_proj))
    cross_pair = with_swap(after(second_cross, grad_proj))
    late_pair = with_swap(after(first_three, grad_proj))
    down_pair = with_swap(first_down + third_down)
    mixed_blocks = spread(
        steps_total,
        [
            (own_half, *scaled_pair),
            (half_two, *two_pair),
            (half_cross, *cross_pair),
            (half_late, *late_pair),
            (half_down, *down_pair),
        ],
        *grad_slots,
    )
    mixed_first = mixed_blocks[0]
    scaled_rows = [after(rows, mixed_first) for rows in scaled_rows]
    mixed_blocks = list(mixed_blocks[:1]) + [
        across_chips(mixed_blocks[step], step) for step in range(1, CHIPS)
    ]
    scaled_rows = scaled_rows + [scaled_pair[1]] + [swap_cores(rows) for rows in scaled_rows[1:]]
    share = jax.ShapeDtypeStruct((channels // devices, ranks), f32)
    share_flops = 2 * channels * rows * ranks
    token_share = block_call(token_kernel, [share], token_blocks + proj_rows, share_flops)
    factor_share, core_total = block_call(
        last_kernel,
        [share, jax.ShapeDtypeStruct((ranks, ranks), bf16)],
        [*token_blocks, *token_share, *mixed_blocks, *scaled_rows],
        share_flops,
    )
    return (factor_share[None], core_total[None, None])


def solution(mesh):
    placed = (
        P("section", None, "expert", None),
        P("section", None, "expert", None),
        P("section", None, "expert"),
        P("section", None, "expert"),
        P("section", None, "expert"),
        P("section", None, None),
        P("section", "expert", None, None),
    )
    drawn_for = (LAYERS, CHIPS * CORES)

    def per_device(*arrays):
        local_experts = arrays[-1].shape[1]
        ranks, width = arrays[-1].shape[-1], CORES * arrays[3].shape[1] * arrays[3].shape[2]
        fits = local_experts == 1 and ranks % width == 0
        if (mesh.shape["section"], mesh.shape["expert"]) == drawn_for and fits:
            return gathered_plan(*arrays)
        return general_plan(*arrays)

    return jax.shard_map(
        per_device,
        mesh=mesh,
        in_specs=placed,
        out_specs=(P("section", "expert", None), P("section", "expert", None, None)),
        check_vma=False,
    )
```

```python
import jax
import jax.numpy as jnp
from jax import lax
from jax.experimental import pallas as pl
from jax.experimental.pallas import tpu as pltpu
from jax.sharding import PartitionSpec as P


def from_behind(value, axis, steps):
    count = lax.axis_size(axis)
    leading, last = (max(0, -steps), min(count, count - steps))
    return lax.ppermute(value, axis, [(source, source + steps) for source in range(leading, last)])


def silu_slope(values):
    sigmoid = jax.nn.sigmoid(values)
    return sigmoid * (1.0 + values * (1.0 - sigmoid))


def times_transposed(left, shared):
    return lax.dot_general(
        left, shared, (((1,), (1,)), ((), ())), preferred_element_type=jnp.float32
    )


def factor_terms(tokens_flat, proj_flat, mixed_flat, hidden_flat):

    def factor_rows(start, count):
        first_term = lax.dot_general(
            tokens_flat, proj_flat, (((0,), (0,)), ((), ())), preferred_element_type=jnp.float32
        )
        second_term = lax.dot_general(
            mixed_flat, hidden_flat, (((0,), (0,)), ((), ())), preferred_element_type=jnp.float32
        )
        return first_term + second_term

    return factor_rows


def store_slice(store, fresh, picked, usable):
    former = lax.dynamic_index_in_dim(store, picked, 0, keepdims=False)
    kept = jnp.where(usable, fresh, former)
    return lax.dynamic_update_index_in_dim(store, kept, picked, 0)


def general_plan(inputs, teacher, gate, route, slot, factor, cores):
    tokens_all = inputs[0]
    targets_all = teacher[0]
    weights_all = gate[0]
    shared = factor[0]
    blocks = cores[0]
    micro_count, token_count, channels = tokens_all.shape
    ranks = shared.shape[1]
    local_experts = blocks.shape[0]
    expert_devices = lax.axis_size("expert")
    capacity = max(2, 2 * token_count // (local_experts * expert_devices))
    slot_count = local_experts * expert_devices * capacity
    places_all = route[0] * capacity + slot[0]
    micro_range = jnp.arange(micro_count, dtype=jnp.int32)[:, None]
    token_proj = jnp.dot(
        tokens_all.reshape(-1, channels), shared, preferred_element_type=jnp.float32
    ).astype(jnp.bfloat16)
    token_proj = token_proj.reshape(micro_count, token_count, ranks)
    proj_slots = (
        jnp.zeros((micro_count, slot_count, ranks), jnp.bfloat16)
        .at[micro_range, places_all]
        .set(token_proj)
    )
    projected = lax.all_to_all(proj_slots, "expert", split_axis=1, concat_axis=1, tiled=True)
    projected = projected.reshape(micro_count, expert_devices, local_experts, capacity, ranks)
    pre = jnp.einsum("mnecr,erk->mneck", projected, blocks, preferred_element_type=jnp.float32)
    active = jax.nn.silu(pre).astype(jnp.bfloat16)
    returned = lax.all_to_all(
        active.reshape(micro_count, slot_count, ranks),
        "expert",
        split_axis=1,
        concat_axis=1,
        tiled=True,
    )
    hidden = jnp.take_along_axis(returned, places_all[:, :, None], axis=1)
    mixed = times_transposed(hidden.reshape(-1, ranks), shared).reshape(
        micro_count, token_count, channels
    )
    output = tokens_all.astype(jnp.float32) + weights_all[:, :, None] * mixed
    errors = output - targets_all.astype(jnp.float32)
    section_count = lax.axis_size("section")
    section_here = lax.axis_index("section")
    incoming = jnp.zeros((token_count, channels), jnp.bfloat16)
    mixed_store = jnp.zeros((micro_count, token_count, channels), jnp.bfloat16)
    proj_store = jnp.zeros((micro_count, token_count, ranks), jnp.bfloat16)
    pre_store = jnp.zeros(
        (micro_count, expert_devices, local_experts, capacity, ranks), jnp.bfloat16
    )
    turn_total = micro_count + section_count - 1
    for turn_index in range(turn_total):
        micro_now = turn_index - (section_count - 1 - section_here)
        usable = jnp.logical_and(micro_now >= 0, micro_now < micro_count)
        picked = jnp.clip(micro_now, 0, micro_count - 1)
        grad_out = lax.dynamic_index_in_dim(errors, picked, 0, keepdims=False) + incoming.astype(
            jnp.float32
        )
        weight_now = lax.dynamic_index_in_dim(weights_all, picked, 0, keepdims=False)
        places = lax.dynamic_index_in_dim(places_all, picked, 0, keepdims=False)
        grad_mixed = (weight_now[:, None] * grad_out).astype(jnp.bfloat16)
        grad_hidden = jnp.dot(grad_mixed, shared, preferred_element_type=jnp.float32).astype(
            jnp.bfloat16
        )
        grad_slots = jnp.zeros((slot_count, ranks), jnp.bfloat16).at[places].set(grad_hidden)
        grad_recv = lax.all_to_all(grad_slots, "expert", split_axis=0, concat_axis=0, tiled=True)
        grad_recv = grad_recv.reshape(expert_devices, local_experts, capacity, ranks)
        pre_now = lax.dynamic_index_in_dim(pre, picked, 0, keepdims=False)
        grad_pre = (grad_recv.astype(jnp.float32) * silu_slope(pre_now)).astype(jnp.bfloat16)
        grad_routed = jnp.einsum(
            "neck,erk->necr", grad_pre, blocks, preferred_element_type=jnp.float32
        ).astype(jnp.bfloat16)
        grad_home = lax.all_to_all(
            grad_routed.reshape(slot_count, ranks),
            "expert",
            split_axis=0,
            concat_axis=0,
            tiled=True,
        )
        grad_proj = grad_home[places]
        grad_in = (grad_out + times_transposed(grad_proj, shared)).astype(jnp.bfloat16)
        if turn_index + 1 < turn_total:
            incoming = from_behind(grad_in, "section", -1)
        mixed_store = store_slice(mixed_store, grad_mixed, picked, usable)
        proj_store = store_slice(proj_store, grad_proj, picked, usable)
        pre_store = store_slice(pre_store, grad_pre, picked, usable)
    core_total = jnp.einsum(
        "mnecr,mneck->erk", projected, pre_store, preferred_element_type=jnp.float32
    )
    all_rows = factor_terms(
        tokens_all.reshape(-1, channels),
        proj_store.reshape(-1, ranks),
        mixed_store.reshape(-1, channels),
        hidden.reshape(-1, ranks),
    )
    factor_share = lax.psum_scatter(
        all_rows(jnp.int32(0), channels // expert_devices * lax.axis_size("expert")),
        "expert",
        scatter_dimension=0,
        tiled=True,
    )
    return (factor_share[None], core_total.astype(jnp.bfloat16)[None])


CORES = 2
CHIPS = 4
LAYERS = 4
ROOM = 16 * 2**20


def dot(left, right):
    return jnp.dot(left, right, preferred_element_type=jnp.float32)


def dot_first(left, right):
    return lax.dot_general(
        left, right, (((0,), (0,)), ((), ())), preferred_element_type=jnp.float32
    )


def on_chips(value, pairs):
    perm = [
        (CORES * source + core, CORES * target + core)
        for source, target in pairs
        for core in range(CORES)
    ]
    return lax.ppermute(value, "expert", perm)


def swap_cores(value):
    count = lax.axis_size("expert")
    return lax.ppermute(value, "expert", [(index, index ^ 1) for index in range(count)])


def between_layers(value, pairs):
    return lax.ppermute(value, "section", pairs)


def gather_cores(core):
    beside = on_chips(core, [(0, 1), (1, 0), (2, 3), (3, 2)])
    across = on_chips(core, [(1, 2), (2, 1)])
    half = core.shape[0] // 2
    far_a = on_chips(beside[:half], [(1, 2), (2, 1)])
    far_b = on_chips(beside[half:], [(1, 2), (2, 1)])
    outward = on_chips(across, [(1, 0), (2, 3)])
    last_a = on_chips(far_a, [(1, 0), (2, 3)])
    last_b = on_chips(far_b, [(1, 0), (2, 3)])
    held, swapped = [core, beside], [swap_cores(piece) for piece in (core, beside)]
    near = [(across, outward), (far_a, last_a, far_b, last_b)]
    far = [tuple(swap_cores(piece) for piece in pair) for pair in near]
    return [piece for both in zip(held + near, swapped + far) for piece in both]


def row_marks(route, weight, chip, core, middle):
    count = CHIPS * CORES
    place = lax.broadcasted_iota(jnp.int32, (1, 2 * count), 1)
    step = (place % count) // CORES
    turned = jnp.where(jnp.logical_and(step >= 2, middle), 5 - step, step)
    expert = CORES * (chip ^ turned) + (core ^ (place % CORES))
    marks = (route == expert).astype(jnp.float32)
    return jnp.where(place < count, marks, weight)


def across_chips(value, step):
    return on_chips(value, [(chip, chip ^ step) for chip in range(CHIPS)])


def gather_rows(rows):
    held = [rows] + [across_chips(rows, step) for step in range(1, CHIPS)]
    return held + [swap_cores(piece) for piece in held]


def chip_blocks(wide, chip, core):
    count = wide.shape[0] // (CHIPS * CORES)
    blocks = [
        lax.dynamic_slice_in_dim(wide, (CORES * (chip ^ step) + core) * count, count, 0)
        for step in range(CHIPS)
    ]
    return jnp.concatenate(blocks, axis=0)


def chip_columns(wide, chip, core):
    theirs = swap_cores(chip_blocks(wide, chip, 1 - core))
    return jnp.concatenate([chip_blocks(wide, chip, core), theirs], axis=1)


def both_cores(partial):
    rows = partial.shape[0] // CORES
    return partial[:rows] + swap_cores(partial[rows:])


def gram_pair(left, right):
    partial = dot_first(left, right).astype(jnp.bfloat16)
    return partial, swap_cores(partial)


def gram_sum(pair):
    return (pair[0].astype(jnp.float32) + pair[1].astype(jnp.float32)).astype(jnp.bfloat16)


def routed_product(rows, marks, start, core_refs, transposed, copies=None):
    dims = (((1,), (1 if transposed else 0,)), ((), ()))
    total = None
    for place, core_ref in enumerate(core_refs):
        if copies is not None:
            for move in copies[place]:
                move.wait()
        mark = marks[:, start + place : start + place + 1]
        chosen = jnp.where(mark > 0.5, rows, jnp.zeros_like(rows))
        term = lax.dot_general(
            chosen, core_ref[...], dims, preferred_element_type=jnp.float32
        )
        total = term if total is None else total + term
    return total


def backward_rows(score, slope, marks, core_refs):
    count = len(core_refs)
    grad_hidden = (marks[:, count : count + 1] * score).astype(jnp.bfloat16)
    grad_pre = (grad_hidden.astype(jnp.float32) * slope).astype(jnp.bfloat16)
    grad_proj = routed_product(grad_pre, marks, 0, core_refs, True)
    return grad_pre, grad_proj.astype(jnp.bfloat16)


def fetch(middle, sources, targets, arrived):
    copies, count = [], 0
    for source, target in zip(sources, targets):
        if not isinstance(source, tuple):
            move = pltpu.make_async_copy(source, target, arrived.at[count])
            move.start()
            copies.append([move])
            count += 1
            continue
        moves = []
        for place in range(0, len(source), 2):
            inner, outer = source[place : place + 2]
            part = target.at[pl.ds(place // 2 * inner.shape[0], inner.shape[0]), :]
            move = pltpu.make_async_copy(inner, part, arrived.at[count])
            pl.when(middle)(move.start)
            pl.when(jnp.logical_not(middle))(
                pltpu.make_async_copy(outer, part, arrived.at[count]).start
            )
            moves.append(move)
            count += 1
        copies.append(moves)
    return copies


def early_kernel(middle_ref, proj_ref, marks_ref, *refs):
    sources = [*refs[:4], (refs[4], refs[5]), (refs[6], refs[7])]
    part_ref, core_refs, arrived = refs[8], refs[9:-1], refs[-1]
    copies = fetch(middle_ref[0] > 0, sources, core_refs, arrived)
    part_ref[...] = routed_product(proj_ref[...], marks_ref[...], 0, core_refs, False, copies)


def first_kernel(middle_ref, proj_ref, marks_ref, part_ref, *refs):
    early = CHIPS * CORES - 2
    held, refs = refs[:early], refs[early:]
    sources = [tuple(refs[:4]), tuple(refs[4:8]), refs[8], refs[9]]
    scaled_ref, slope_ref, score_ref, chain_ref, near_ref, far_ref = refs[10:16]
    own_ref, gram_ref, arrived = refs[16:]
    last = [near_ref, far_ref]
    copies = fetch(middle_ref[0] > 0, sources, [*last, own_ref, gram_ref], arrived)
    core_refs, count = [*held, *last], early + 2
    marks = marks_ref[...]
    pre = part_ref[...] + routed_product(proj_ref[...], marks, early, last, False, copies)
    sigmoid = 1.0 / (1.0 + jnp.exp(-pre))
    hidden = (pre * sigmoid).astype(jnp.bfloat16)
    slope = sigmoid * (1.0 + pre * (1.0 - sigmoid))
    weight = marks[:, count : count + 1]
    scaled = (weight * hidden.astype(jnp.float32)).astype(jnp.bfloat16)
    for move in copies[2] + copies[3]:
        move.wait()
    score = own_ref[...] + dot(scaled, gram_ref[...])
    scaled_ref[...] = scaled
    slope_ref[...] = slope
    score_ref[...] = score
    _, grad_proj = backward_rows(score, slope, marks, core_refs)
    chain_ref[...] = (scaled.astype(jnp.float32) + grad_proj.astype(jnp.float32)).astype(
        jnp.bfloat16
    )


def turn_kernel(terms, late, marks_ref, scaled_ref, slope_ref, score_ref, *refs):
    score = score_ref[...]
    if late:
        score, refs = score + refs[0][...], refs[1:]
    core_refs = refs[2 * terms : len(refs) - 4]
    next_ref, grad_ref, proj_ref, chain_ref = refs[len(refs) - 4 :]
    for term in range(terms):
        score = score + dot(refs[2 * term][...], refs[2 * term + 1][...])
    next_ref[...] = score
    grad_pre, grad_proj = backward_rows(score, slope_ref[...], marks_ref[...], core_refs)
    grad_ref[...] = grad_pre
    proj_ref[...] = grad_proj
    chain_ref[...] = (scaled_ref[...].astype(jnp.float32) + grad_proj.astype(jnp.float32)).astype(
        jnp.bfloat16
    )


def call_rows(body, outs, arrays, flops, scalars=()):
    in_bytes = sum(array.size * array.dtype.itemsize for array in arrays)
    return pl.pallas_call(
        body,
        out_shape=[jax.ShapeDtypeStruct(shape, kind) for shape, kind in outs],
        in_specs=[pl.BlockSpec(memory_space=pltpu.SMEM)] * len(scalars)
        + [pl.BlockSpec(memory_space=pltpu.VMEM)] * len(arrays),
        out_specs=[pl.BlockSpec(memory_space=pltpu.VMEM)] * len(outs),
        compiler_params=pltpu.CompilerParams(vmem_limit_bytes=ROOM),
        cost_estimate=pl.CostEstimate(flops=flops, bytes_accessed=in_bytes, transcendentals=0),
    )(*scalars, *arrays)


def spread_kernel(terms, base_ref, *refs):
    total = base_ref[...].astype(jnp.float32)
    refs, first = list(refs), pl.program_id(0) < CHIPS // 2
    for parts in terms:
        half = refs.pop(0)[...]
        if parts > 1:
            half = jnp.where(first, half, refs.pop(0)[...])
        values = jnp.concatenate([refs.pop(0)[...], refs.pop(0)[...]], axis=0)
        total = total + times_transposed(half, values)
    block = total.astype(jnp.bfloat16)
    slot_refs, outs = refs[:2], refs[2:]
    count, width = block.shape
    for step, out_ref in enumerate(outs):

        @pl.when(pl.program_id(0) == step)
        def _():
            out_ref[:count, :] = block
            for part, (row, column, slots) in enumerate(slot_tiles(slot_refs[0], width)):
                slot_ref = slot_refs[part % CORES]
                out_ref[pl.ds(count + row, slots), :] = slot_ref[
                    step * slots : (step + 1) * slots, column : column + width
                ]


def slot_tiles(slot_ref, width):
    slots = slot_ref.shape[0] // CHIPS
    groups = slot_ref.shape[1] // width
    return [
        ((CORES * group + side) * slots, group * width, slots)
        for group in range(groups)
        for side in range(CORES)
    ]


def under_block(block, own, theirs, step):
    width = block.shape[1]
    parts = [
        (own, theirs)[part % CORES][step * slots : (step + 1) * slots, column : column + width]
        for part, (_, column, slots) in enumerate(slot_tiles(own, width))
    ]
    return jnp.concatenate([block, *parts], axis=0)


def spread(base, terms, own_slots, their_slots):
    halves = [half if isinstance(half, list) else [half] for half, _, _ in terms]
    arrays = [base]
    for parts, (_, near, far) in zip(halves, terms):
        arrays += [*parts, near, far]
    arrays += [own_slots, their_slots]
    height, width = base.shape
    count = height // CHIPS
    tall = count + CORES * own_slots.size // (CHIPS * width)

    def rows(columns):
        return pl.BlockSpec((count, columns), lambda step: (step, 0))

    def whole(array):
        return pl.BlockSpec(array.shape, lambda step: (0, 0))

    def part(array, place):
        last = CHIPS // 2 - 1
        block = (count, array.shape[1])
        if place == 0:
            return pl.BlockSpec(block, lambda step: (jnp.minimum(step, last), 0))
        return pl.BlockSpec(block, lambda step: (jnp.maximum(step - last - 1, 0), 0))

    specs = [rows(width)]
    for parts, (_, near, far) in zip(halves, terms):
        if len(parts) == 1:
            specs.append(rows(parts[0].shape[1]))
        else:
            specs += [part(array, place) for place, array in enumerate(parts)]
        specs += [whole(near), whole(far)]
    specs += [whole(own_slots), whole(their_slots)]

    def body(*refs):
        spread_kernel([len(parts) for parts in halves], *refs)

    return pl.pallas_call(
        body,
        name="spread",
        grid=(CHIPS,),
        out_shape=[jax.ShapeDtypeStruct((tall, width), jnp.bfloat16)] * CHIPS,
        in_specs=specs,
        out_specs=[pl.BlockSpec((tall, width), lambda step: (0, 0))] * CHIPS,
        compiler_params=pltpu.CompilerParams(vmem_limit_bytes=ROOM),
        cost_estimate=pl.CostEstimate(
            flops=2 * height * width * terms[0][1].shape[1] * len(terms),
            bytes_accessed=sum(array.size * array.dtype.itemsize for array in arrays),
            transcendentals=0,
        ),
    )(*arrays)


def pair_products(block_ref, count, near_ref, far_ref):
    return dot(block_ref[:count, :], jnp.concatenate([near_ref[...], far_ref[...]], axis=0))


def block_products(count, refs):
    total = None
    for step in range(CHIPS):
        term = pair_products(refs[step], count, refs[CHIPS + step], refs[2 * CHIPS + step])
        total = term if total is None else total + term
    return total


def token_kernel(*refs):
    refs[-1][...] = block_products(refs[-1].shape[0], refs[:-1])


def last_kernel(*refs):
    token_refs, refs = refs[:CHIPS], refs[CHIPS:]
    total_ref, product_refs = refs[0], refs[1:-2]
    share_ref, core_ref = refs[-2:]
    count = share_ref.shape[0]
    share_ref[...] = total_ref[...] + block_products(count, product_refs)
    width = token_refs[0].shape[1]
    slots = (token_refs[0].shape[0] - count) * width // core_ref.shape[0]

    def group(block_refs, column):
        start = count + column * slots
        return jnp.concatenate([ref[start : start + slots, :] for ref in block_refs], axis=0)

    groups = core_ref.shape[0] // width
    for left in range(groups):
        for right in range(groups):
            product = dot_first(group(token_refs, left), group(product_refs[:CHIPS], right))
            core_ref[
                left * width : (left + 1) * width, right * width : (right + 1) * width
            ] = product.astype(jnp.bfloat16)


def block_call(body, outs, arrays, flops):
    return pl.pallas_call(
        body,
        out_shape=outs,
        in_specs=[pl.BlockSpec(memory_space=pltpu.VMEM)] * len(arrays),
        out_specs=[pl.BlockSpec(memory_space=pltpu.VMEM)] * len(outs),
        compiler_params=pltpu.CompilerParams(vmem_limit_bytes=ROOM),
        cost_estimate=pl.CostEstimate(
            flops=flops,
            bytes_accessed=sum(array.size * array.dtype.itemsize for array in arrays),
            transcendentals=0,
        ),
    )(*arrays)


def after(value, earlier):
    return lax.optimization_barrier((value, earlier))[0]


def gathered_plan(inputs, teacher, gate, route, slot, factor, cores):
    bf16, f32 = jnp.bfloat16, jnp.float32
    shared = factor[0]
    channels, ranks = shared.shape
    devices = lax.axis_size("expert")
    micro_count, token_count = route.shape[1:]
    rows = micro_count * token_count
    here = lax.axis_index("expert")
    chip, core = here // CORES, here % CORES
    middle = jnp.logical_or(chip == 1, chip == 2)
    tokens = inputs[0].reshape(rows, channels)

    travelled = gather_cores(cores[0, 0])
    marks = row_marks(
        route[0].reshape(rows, 1), gate[0].reshape(rows, 1), chip, core, middle
    )

    down = [(3, 2), (1, 0)]
    two_down = [(3, 1), (2, 0)]
    own_half = chip_blocks(shared, chip, core)
    cut = own_half.shape[0] // 2
    half_two = [between_layers(own_half[:cut], two_down), between_layers(own_half[cut:], two_down)]
    half_down = between_layers(own_half, down)
    half_cross = [between_layers(half_two[0], [(0, 1)])]
    half_cross.append(between_layers(half_two[1], [(0, 1)]))
    half_late = [between_layers(half_down[:cut], [(2, 0)]), between_layers(half_two[1], [(1, 0)])]

    def cross_gram(parts):
        partial = dot_first(parts[0], own_half[:cut]) + dot_first(parts[1], own_half[cut:])
        partial = partial.astype(jnp.bfloat16)
        return partial, swap_cores(partial)

    turned = lax.optimization_barrier(tokens.T)
    wanted = lax.optimization_barrier(teacher[0].reshape(rows, channels).T)
    difference = (turned.astype(f32) - wanted.astype(f32)).astype(bf16)
    difference = chip_columns(difference, chip, core)
    step_down = between_layers(difference, down)
    upper = (difference.astype(f32) + step_down.astype(f32)).astype(bf16)
    step_up = between_layers(upper, [(2, 0)])

    capacity = max(2, 2 * token_count // devices)
    slots = micro_count * capacity
    micro = jnp.arange(rows, dtype=jnp.int32) // token_count
    expert = route[0].reshape(rows)
    near = (expert % CORES ^ core) * CHIPS + (expert // CORES ^ chip)
    place = near * slots + micro * capacity + slot[0].reshape(rows)
    picks = (jnp.arange(devices * slots, dtype=jnp.int32)[:, None] == place[None, :]).astype(bf16)

    def to_slots(values):
        held = dot(picks, values).astype(bf16)
        half = CHIPS * slots
        return held[:half], swap_cores(held[half:])

    projected = dot(tokens, shared).astype(bf16)
    own_gram = gram_pair(own_half, own_half)
    proj_slots = to_slots(projected)
    gram = gram_sum(own_gram)
    own_score = both_cores(dot_first(difference, own_half))
    turned = chip_columns(turned, chip, core)
    token_blocks = [
        under_block(
            turned[step * channels // devices : (step + 1) * channels // devices],
            *proj_slots,
            step,
        )
        for step in range(CHIPS)
    ]
    down_pair = gram_pair(half_down, own_half)
    down_gram = gram_sum(down_pair)
    two_gram = gram_sum(cross_gram(half_two))
    down_score = both_cores(dot_first(step_down, own_half))

    wide = (rows, ranks)
    product_flops = 2 * rows * ranks * ranks
    flag = middle.astype(jnp.int32).reshape(1)
    block = pltpu.VMEM((ranks, ranks), bf16)

    def core_call(body, sources, outs, arrays, scratch, products):
        flat = [ref for source in sources for ref in (source if type(source) is tuple else [source])]
        return pl.pallas_call(
            body,
            out_shape=outs,
            in_specs=[pl.BlockSpec(memory_space=pltpu.SMEM)]
            + [pl.BlockSpec(memory_space=pltpu.VMEM)] * len(arrays)
            + [pl.BlockSpec(memory_space=pl.ANY)] * len(flat),
            out_specs=[pl.BlockSpec(memory_space=pltpu.VMEM)] * len(outs),
            scratch_shapes=scratch + [pltpu.SemaphoreType.DMA((len(flat),))],
            compiler_params=pltpu.CompilerParams(vmem_limit_bytes=ROOM),
            cost_estimate=pl.CostEstimate(
                flops=product_flops * products,
                bytes_accessed=2 * len(sources) * ranks * ranks,
                transcendentals=0,
            ),
        )(flag, *arrays, *flat)

    part, *held = core_call(
        early_kernel,
        travelled[:-2],
        [jax.ShapeDtypeStruct(wide, f32)] + [block] * (devices - 2),
        [projected, marks],
        [],
        devices - 2,
    )
    scaled, slope, score, chain, *last = core_call(
        first_kernel,
        [*travelled[-2:], own_score, gram],
        [jax.ShapeDtypeStruct(wide, kind) for kind in (bf16, f32, f32, bf16)] + [block] * 2,
        [projected, marks, part, *held],
        [pltpu.VMEM(wide, f32), pltpu.VMEM((ranks, ranks), bf16)],
        devices + 3,
    )
    pieces = [*held, *last]

    def turn(score, late, terms):
        arrays = [array for pair in terms for array in pair]

        def body(*refs):
            turn_kernel(len(terms), bool(late), *refs)

        return call_rows(
            body,
            [(wide, f32), (wide, bf16), (wide, bf16), (wide, bf16)],
            [marks, scaled, slope, score, *late, *arrays, *pieces],
            product_flops * (devices + len(terms)),
        )

    chain_first = chain
    first_down = between_layers(chain, [(3, 2)])
    step_cross = between_layers(after(step_up, chain), [(0, 1)])
    first_two = between_layers(chain, [(3, 1)])
    scaled_rows = [scaled] + [across_chips(after(scaled, chain), step) for step in range(1, CHIPS)]
    token_blocks = token_blocks[:1] + [
        across_chips(after(token_blocks[step], chain), step) for step in range(1, CHIPS)
    ]
    score, _, _, chain = turn(score, [down_score], [(first_down, down_gram)])

    second_cross = between_layers(chain, [(2, 1)])
    second_two = between_layers(chain, [(2, 0)])
    first_three = between_layers(after(chain_first, chain), [(3, 0)])
    half_cross = [after(part, chain) for part in half_cross]
    step_cross = after(step_cross, chain)
    cross_pair = cross_gram(half_cross)
    late_steps = step_up + step_cross
    late_score = both_cores(dot_first(late_steps, own_half))
    cross_product = gram_sum(cross_pair)
    score, _, _, chain = turn(
        score, [late_score], [(first_two, two_gram), (second_cross, cross_product)]
    )

    third_down = between_layers(chain, [(1, 0)])
    half_late = [after(part, chain) for part in half_late]
    late_pair = cross_gram(half_late)
    steps_total = difference.astype(f32) + step_down.astype(f32)
    steps_total = (steps_total + after(late_steps, chain).astype(f32)).astype(bf16)
    late_product = gram_sum(late_pair)
    score, grad_pre, grad_proj, _ = turn(
        score, [], [(second_two, two_gram), (first_three, late_product), (third_down, down_gram)]
    )

    def with_swap(values):
        return values, swap_cores(values)

    proj_rows = gather_rows(grad_proj)
    grad_slots = to_slots(grad_pre)
    scaled_pair = with_swap(after(scaled, grad_proj))
    two_pair = with_swap(first_two + after(second_two, grad_proj))
    cross_pair = with_swap(after(second_cross, grad_proj))
    late_pair = with_swap(after(first_three, grad_proj))
    down_pair = with_swap(first_down + third_down)
    mixed_blocks = spread(
        steps_total,
        [
            (own_half, *scaled_pair),
            (half_two, *two_pair),
            (half_cross, *cross_pair),
            (half_late, *late_pair),
            (half_down, *down_pair),
        ],
        *grad_slots,
    )
    mixed_first = mixed_blocks[0]
    scaled_rows = [after(rows, mixed_first) for rows in scaled_rows]
    mixed_blocks = list(mixed_blocks[:1]) + [
        across_chips(mixed_blocks[step], step) for step in range(1, CHIPS)
    ]
    scaled_rows = scaled_rows + [scaled_pair[1]] + [swap_cores(rows) for rows in scaled_rows[1:]]
    share = jax.ShapeDtypeStruct((channels // devices, ranks), f32)
    share_flops = 2 * channels * rows * ranks
    token_share = block_call(token_kernel, [share], token_blocks + proj_rows, share_flops)
    factor_share, core_total = block_call(
        last_kernel,
        [share, jax.ShapeDtypeStruct((ranks, ranks), bf16)],
        [*token_blocks, *token_share, *mixed_blocks, *scaled_rows],
        share_flops,
    )
    return (factor_share[None], core_total[None, None])


def solution(mesh):
    placed = (
        P("section", None, "expert", None),
        P("section", None, "expert", None),
        P("section", None, "expert"),
        P("section", None, "expert"),
        P("section", None, "expert"),
        P("section", None, None),
        P("section", "expert", None, None),
    )
    drawn_for = (LAYERS, CHIPS * CORES)

    def per_device(*arrays):
        local_experts = arrays[-1].shape[1]
        ranks, width = arrays[-1].shape[-1], CORES * arrays[3].shape[1] * arrays[3].shape[2]
        fits = local_experts == 1 and ranks % width == 0
        if (mesh.shape["section"], mesh.shape["expert"]) == drawn_for and fits:
            return gathered_plan(*arrays)
        return general_plan(*arrays)

    return jax.shard_map(
        per_device,
        mesh=mesh,
        in_specs=placed,
        out_specs=(P("section", "expert", None), P("section", "expert", None, None)),
        check_vma=False,
    )
```

```python
import jax
import jax.numpy as jnp
from jax import lax
from jax.experimental import pallas as pl
from jax.experimental.pallas import tpu as pltpu
from jax.sharding import PartitionSpec as P


def from_behind(value, axis, steps):
    count = lax.axis_size(axis)
    leading, last = (max(0, -steps), min(count, count - steps))
    return lax.ppermute(value, axis, [(source, source + steps) for source in range(leading, last)])


def silu_slope(values):
    sigmoid = jax.nn.sigmoid(values)
    return sigmoid * (1.0 + values * (1.0 - sigmoid))


def times_transposed(left, shared):
    return lax.dot_general(
        left, shared, (((1,), (1,)), ((), ())), preferred_element_type=jnp.float32
    )


def factor_terms(tokens_flat, proj_flat, mixed_flat, hidden_flat):

    def factor_rows(start, count):
        first_term = lax.dot_general(
            tokens_flat, proj_flat, (((0,), (0,)), ((), ())), preferred_element_type=jnp.float32
        )
        second_term = lax.dot_general(
            mixed_flat, hidden_flat, (((0,), (0,)), ((), ())), preferred_element_type=jnp.float32
        )
        return first_term + second_term

    return factor_rows


def store_slice(store, fresh, picked, usable):
    former = lax.dynamic_index_in_dim(store, picked, 0, keepdims=False)
    kept = jnp.where(usable, fresh, former)
    return lax.dynamic_update_index_in_dim(store, kept, picked, 0)


def general_plan(inputs, teacher, gate, route, slot, factor, cores):
    tokens_all = inputs[0]
    targets_all = teacher[0]
    weights_all = gate[0]
    shared = factor[0]
    blocks = cores[0]
    micro_count, token_count, channels = tokens_all.shape
    ranks = shared.shape[1]
    local_experts = blocks.shape[0]
    expert_devices = lax.axis_size("expert")
    capacity = max(2, 2 * token_count // (local_experts * expert_devices))
    slot_count = local_experts * expert_devices * capacity
    places_all = route[0] * capacity + slot[0]
    micro_range = jnp.arange(micro_count, dtype=jnp.int32)[:, None]
    token_proj = jnp.dot(
        tokens_all.reshape(-1, channels), shared, preferred_element_type=jnp.float32
    ).astype(jnp.bfloat16)
    token_proj = token_proj.reshape(micro_count, token_count, ranks)
    proj_slots = (
        jnp.zeros((micro_count, slot_count, ranks), jnp.bfloat16)
        .at[micro_range, places_all]
        .set(token_proj)
    )
    projected = lax.all_to_all(proj_slots, "expert", split_axis=1, concat_axis=1, tiled=True)
    projected = projected.reshape(micro_count, expert_devices, local_experts, capacity, ranks)
    pre = jnp.einsum("mnecr,erk->mneck", projected, blocks, preferred_element_type=jnp.float32)
    active = jax.nn.silu(pre).astype(jnp.bfloat16)
    returned = lax.all_to_all(
        active.reshape(micro_count, slot_count, ranks),
        "expert",
        split_axis=1,
        concat_axis=1,
        tiled=True,
    )
    hidden = jnp.take_along_axis(returned, places_all[:, :, None], axis=1)
    mixed = times_transposed(hidden.reshape(-1, ranks), shared).reshape(
        micro_count, token_count, channels
    )
    output = tokens_all.astype(jnp.float32) + weights_all[:, :, None] * mixed
    errors = output - targets_all.astype(jnp.float32)
    section_count = lax.axis_size("section")
    section_here = lax.axis_index("section")
    incoming = jnp.zeros((token_count, channels), jnp.bfloat16)
    mixed_store = jnp.zeros((micro_count, token_count, channels), jnp.bfloat16)
    proj_store = jnp.zeros((micro_count, token_count, ranks), jnp.bfloat16)
    pre_store = jnp.zeros(
        (micro_count, expert_devices, local_experts, capacity, ranks), jnp.bfloat16
    )
    turn_total = micro_count + section_count - 1
    for turn_index in range(turn_total):
        micro_now = turn_index - (section_count - 1 - section_here)
        usable = jnp.logical_and(micro_now >= 0, micro_now < micro_count)
        picked = jnp.clip(micro_now, 0, micro_count - 1)
        grad_out = lax.dynamic_index_in_dim(errors, picked, 0, keepdims=False) + incoming.astype(
            jnp.float32
        )
        weight_now = lax.dynamic_index_in_dim(weights_all, picked, 0, keepdims=False)
        places = lax.dynamic_index_in_dim(places_all, picked, 0, keepdims=False)
        grad_mixed = (weight_now[:, None] * grad_out).astype(jnp.bfloat16)
        grad_hidden = jnp.dot(grad_mixed, shared, preferred_element_type=jnp.float32).astype(
            jnp.bfloat16
        )
        grad_slots = jnp.zeros((slot_count, ranks), jnp.bfloat16).at[places].set(grad_hidden)
        grad_recv = lax.all_to_all(grad_slots, "expert", split_axis=0, concat_axis=0, tiled=True)
        grad_recv = grad_recv.reshape(expert_devices, local_experts, capacity, ranks)
        pre_now = lax.dynamic_index_in_dim(pre, picked, 0, keepdims=False)
        grad_pre = (grad_recv.astype(jnp.float32) * silu_slope(pre_now)).astype(jnp.bfloat16)
        grad_routed = jnp.einsum(
            "neck,erk->necr", grad_pre, blocks, preferred_element_type=jnp.float32
        ).astype(jnp.bfloat16)
        grad_home = lax.all_to_all(
            grad_routed.reshape(slot_count, ranks),
            "expert",
            split_axis=0,
            concat_axis=0,
            tiled=True,
        )
        grad_proj = grad_home[places]
        grad_in = (grad_out + times_transposed(grad_proj, shared)).astype(jnp.bfloat16)
        if turn_index + 1 < turn_total:
            incoming = from_behind(grad_in, "section", -1)
        mixed_store = store_slice(mixed_store, grad_mixed, picked, usable)
        proj_store = store_slice(proj_store, grad_proj, picked, usable)
        pre_store = store_slice(pre_store, grad_pre, picked, usable)
    core_total = jnp.einsum(
        "mnecr,mneck->erk", projected, pre_store, preferred_element_type=jnp.float32
    )
    all_rows = factor_terms(
        tokens_all.reshape(-1, channels),
        proj_store.reshape(-1, ranks),
        mixed_store.reshape(-1, channels),
        hidden.reshape(-1, ranks),
    )
    factor_share = lax.psum_scatter(
        all_rows(jnp.int32(0), channels // expert_devices * lax.axis_size("expert")),
        "expert",
        scatter_dimension=0,
        tiled=True,
    )
    return (factor_share[None], core_total.astype(jnp.bfloat16)[None])


CORES = 2
CHIPS = 4
LAYERS = 4
ROOM = 16 * 2**20


def dot(left, right):
    return jnp.dot(left, right, preferred_element_type=jnp.float32)


def dot_first(left, right):
    return lax.dot_general(
        left, right, (((0,), (0,)), ((), ())), preferred_element_type=jnp.float32
    )


def on_chips(value, pairs):
    perm = [
        (CORES * source + core, CORES * target + core)
        for source, target in pairs
        for core in range(CORES)
    ]
    return lax.ppermute(value, "expert", perm)


def swap_cores(value):
    count = lax.axis_size("expert")
    return lax.ppermute(value, "expert", [(index, index ^ 1) for index in range(count)])


def between_layers(value, pairs):
    return lax.ppermute(value, "section", pairs)


def gather_cores(core):
    beside = on_chips(core, [(0, 1), (1, 0), (2, 3), (3, 2)])
    across = on_chips(core, [(1, 2), (2, 1)])
    half = core.shape[0] // 2
    far_a = on_chips(beside[:half], [(1, 2), (2, 1)])
    far_b = on_chips(beside[half:], [(1, 2), (2, 1)])
    outward = on_chips(across, [(1, 0), (2, 3)])
    last_a = on_chips(far_a, [(1, 0), (2, 3)])
    last_b = on_chips(far_b, [(1, 0), (2, 3)])
    held, swapped = [core, beside], [swap_cores(piece) for piece in (core, beside)]
    near = [(across, outward), (far_a, last_a, far_b, last_b)]
    far = [tuple(swap_cores(piece) for piece in pair) for pair in near]
    return [piece for both in zip(held + near, swapped + far) for piece in both]


def row_marks(route, weight, chip, core, middle):
    count = CHIPS * CORES
    place = lax.broadcasted_iota(jnp.int32, (1, 2 * count), 1)
    step = (place % count) // CORES
    turned = jnp.where(jnp.logical_and(step >= 2, middle), 5 - step, step)
    expert = CORES * (chip ^ turned) + (core ^ (place % CORES))
    marks = (route == expert).astype(jnp.float32)
    return jnp.where(place < count, marks, weight)


def across_chips(value, step):
    return on_chips(value, [(chip, chip ^ step) for chip in range(CHIPS)])


def gather_rows(rows):
    held = [rows] + [across_chips(rows, step) for step in range(1, CHIPS)]
    return held + [swap_cores(piece) for piece in held]


def chip_blocks(wide, chip, core):
    count = wide.shape[0] // (CHIPS * CORES)
    blocks = [
        lax.dynamic_slice_in_dim(wide, (CORES * (chip ^ step) + core) * count, count, 0)
        for step in range(CHIPS)
    ]
    return jnp.concatenate(blocks, axis=0)


def chip_columns(wide, chip, core):
    theirs = swap_cores(chip_blocks(wide, chip, 1 - core))
    return jnp.concatenate([chip_blocks(wide, chip, core), theirs], axis=1)


def both_cores(partial):
    rows = partial.shape[0] // CORES
    return partial[:rows] + swap_cores(partial[rows:])


def gram_pair(left, right):
    partial = dot_first(left, right).astype(jnp.bfloat16)
    return partial, swap_cores(partial)


def gram_sum(pair):
    return (pair[0].astype(jnp.float32) + pair[1].astype(jnp.float32)).astype(jnp.bfloat16)


def routed_product(rows, marks, start, core_refs, transposed, copies=None):
    dims = (((1,), (1 if transposed else 0,)), ((), ()))
    total = None
    for place, core_ref in enumerate(core_refs):
        if copies is not None:
            for move in copies[place]:
                move.wait()
        mark = marks[:, start + place : start + place + 1]
        chosen = jnp.where(mark > 0.5, rows, jnp.zeros_like(rows))
        term = lax.dot_general(
            chosen, core_ref[...], dims, preferred_element_type=jnp.float32
        )
        total = term if total is None else total + term
    return total


def backward_rows(score, slope, marks, core_refs):
    count = len(core_refs)
    grad_hidden = (marks[:, count : count + 1] * score).astype(jnp.bfloat16)
    grad_pre = (grad_hidden.astype(jnp.float32) * slope).astype(jnp.bfloat16)
    grad_proj = routed_product(grad_pre, marks, 0, core_refs, True)
    return grad_pre, grad_proj.astype(jnp.bfloat16)


def fetch(middle, sources, targets, arrived):
    copies, count = [], 0
    for source, target in zip(sources, targets):
        if not isinstance(source, tuple):
            move = pltpu.make_async_copy(source, target, arrived.at[count])
            move.start()
            copies.append([move])
            count += 1
            continue
        moves = []
        for place in range(0, len(source), 2):
            inner, outer = source[place : place + 2]
            part = target.at[pl.ds(place // 2 * inner.shape[0], inner.shape[0]), :]
            move = pltpu.make_async_copy(inner, part, arrived.at[count])
            pl.when(middle)(move.start)
            pl.when(jnp.logical_not(middle))(
                pltpu.make_async_copy(outer, part, arrived.at[count]).start
            )
            moves.append(move)
            count += 1
        copies.append(moves)
    return copies


def early_kernel(middle_ref, proj_ref, marks_ref, *refs):
    sources = [*refs[:4], (refs[4], refs[5]), (refs[6], refs[7])]
    part_ref, core_refs, arrived = refs[8], refs[9:-1], refs[-1]
    copies = fetch(middle_ref[0] > 0, sources, core_refs, arrived)
    part_ref[...] = routed_product(proj_ref[...], marks_ref[...], 0, core_refs, False, copies)


def first_kernel(middle_ref, proj_ref, marks_ref, part_ref, *refs):
    early = CHIPS * CORES - 2
    held, refs = refs[:early], refs[early:]
    sources = [tuple(refs[:4]), tuple(refs[4:8]), refs[8], refs[9]]
    scaled_ref, slope_ref, score_ref, chain_ref, near_ref, far_ref = refs[10:16]
    own_ref, gram_ref, arrived = refs[16:]
    last = [near_ref, far_ref]
    copies = fetch(middle_ref[0] > 0, sources, [*last, own_ref, gram_ref], arrived)
    core_refs, count = [*held, *last], early + 2
    marks = marks_ref[...]
    pre = part_ref[...] + routed_product(proj_ref[...], marks, early, last, False, copies)
    sigmoid = 1.0 / (1.0 + jnp.exp(-pre))
    hidden = (pre * sigmoid).astype(jnp.bfloat16)
    slope = sigmoid * (1.0 + pre * (1.0 - sigmoid))
    weight = marks[:, count : count + 1]
    scaled = (weight * hidden.astype(jnp.float32)).astype(jnp.bfloat16)
    for move in copies[2] + copies[3]:
        move.wait()
    score = own_ref[...] + dot(scaled, gram_ref[...])
    scaled_ref[...] = scaled
    slope_ref[...] = slope
    score_ref[...] = score
    _, grad_proj = backward_rows(score, slope, marks, core_refs)
    chain_ref[...] = (scaled.astype(jnp.float32) + grad_proj.astype(jnp.float32)).astype(
        jnp.bfloat16
    )


def turn_kernel(terms, late, marks_ref, scaled_ref, slope_ref, score_ref, *refs):
    score = score_ref[...]
    if late:
        score, refs = score + refs[0][...], refs[1:]
    core_refs = refs[2 * terms : len(refs) - 4]
    next_ref, grad_ref, proj_ref, chain_ref = refs[len(refs) - 4 :]
    for term in range(terms):
        score = score + dot(refs[2 * term][...], refs[2 * term + 1][...])
    next_ref[...] = score
    grad_pre, grad_proj = backward_rows(score, slope_ref[...], marks_ref[...], core_refs)
    grad_ref[...] = grad_pre
    proj_ref[...] = grad_proj
    chain_ref[...] = (scaled_ref[...].astype(jnp.float32) + grad_proj.astype(jnp.float32)).astype(
        jnp.bfloat16
    )


def call_rows(body, outs, arrays, flops, scalars=()):
    in_bytes = sum(array.size * array.dtype.itemsize for array in arrays)
    return pl.pallas_call(
        body,
        out_shape=[jax.ShapeDtypeStruct(shape, kind) for shape, kind in outs],
        in_specs=[pl.BlockSpec(memory_space=pltpu.SMEM)] * len(scalars)
        + [pl.BlockSpec(memory_space=pltpu.VMEM)] * len(arrays),
        out_specs=[pl.BlockSpec(memory_space=pltpu.VMEM)] * len(outs),
        compiler_params=pltpu.CompilerParams(vmem_limit_bytes=ROOM),
        cost_estimate=pl.CostEstimate(flops=flops, bytes_accessed=in_bytes, transcendentals=0),
    )(*scalars, *arrays)


def spread_kernel(terms, base_ref, *refs):
    total = base_ref[...].astype(jnp.float32)
    for term in range(terms):
        half_ref, near_ref, far_ref = refs[3 * term : 3 * term + 3]
        values = jnp.concatenate([near_ref[...], far_ref[...]], axis=0)
        total = total + times_transposed(half_ref[...], values)
    block = total.astype(jnp.bfloat16)
    slot_refs, outs = refs[3 * terms : 3 * terms + 2], refs[3 * terms + 2 :]
    count, width = block.shape
    for step, out_ref in enumerate(outs):

        @pl.when(pl.program_id(0) == step)
        def _():
            out_ref[:count, :] = block
            for part, (row, column, slots) in enumerate(slot_tiles(slot_refs[0], width)):
                slot_ref = slot_refs[part % CORES]
                out_ref[pl.ds(count + row, slots), :] = slot_ref[
                    step * slots : (step + 1) * slots, column : column + width
                ]


def slot_tiles(slot_ref, width):
    slots = slot_ref.shape[0] // CHIPS
    groups = slot_ref.shape[1] // width
    return [
        ((CORES * group + side) * slots, group * width, slots)
        for group in range(groups)
        for side in range(CORES)
    ]


def under_block(block, own, theirs, step):
    width = block.shape[1]
    parts = [
        (own, theirs)[part % CORES][step * slots : (step + 1) * slots, column : column + width]
        for part, (_, column, slots) in enumerate(slot_tiles(own, width))
    ]
    return jnp.concatenate([block, *parts], axis=0)


def spread(base, terms, own_slots, their_slots):
    arrays = [base] + [array for term in terms for array in term] + [own_slots, their_slots]
    height, width = base.shape
    count = height // CHIPS
    tall = count + CORES * own_slots.size // (CHIPS * width)

    def rows(columns):
        return pl.BlockSpec((count, columns), lambda step: (step, 0))

    def whole(array):
        return pl.BlockSpec(array.shape, lambda step: (0, 0))

    specs = [rows(width)]
    for half, near, far in terms:
        specs += [rows(half.shape[1]), whole(near), whole(far)]
    specs += [whole(own_slots), whole(their_slots)]

    def body(*refs):
        spread_kernel(len(terms), *refs)

    return pl.pallas_call(
        body,
        name="spread",
        grid=(CHIPS,),
        out_shape=[jax.ShapeDtypeStruct((tall, width), jnp.bfloat16)] * CHIPS,
        in_specs=specs,
        out_specs=[pl.BlockSpec((tall, width), lambda step: (0, 0))] * CHIPS,
        compiler_params=pltpu.CompilerParams(vmem_limit_bytes=ROOM),
        cost_estimate=pl.CostEstimate(
            flops=2 * height * width * terms[0][0].shape[1] * len(terms),
            bytes_accessed=sum(array.size * array.dtype.itemsize for array in arrays),
            transcendentals=0,
        ),
    )(*arrays)


def pair_products(block_ref, count, near_ref, far_ref):
    return dot(block_ref[:count, :], jnp.concatenate([near_ref[...], far_ref[...]], axis=0))


def block_products(count, refs):
    total = None
    for step in range(CHIPS):
        term = pair_products(refs[step], count, refs[CHIPS + step], refs[2 * CHIPS + step])
        total = term if total is None else total + term
    return total


def token_kernel(*refs):
    refs[-1][...] = block_products(refs[-1].shape[0], refs[:-1])


def last_kernel(*refs):
    token_refs, refs = refs[:CHIPS], refs[CHIPS:]
    total_ref, product_refs = refs[0], refs[1:-2]
    share_ref, core_ref = refs[-2:]
    count = share_ref.shape[0]
    share_ref[...] = total_ref[...] + block_products(count, product_refs)
    width = token_refs[0].shape[1]
    slots = (token_refs[0].shape[0] - count) * width // core_ref.shape[0]

    def group(block_refs, column):
        start = count + column * slots
        return jnp.concatenate([ref[start : start + slots, :] for ref in block_refs], axis=0)

    groups = core_ref.shape[0] // width
    for left in range(groups):
        for right in range(groups):
            product = dot_first(group(token_refs, left), group(product_refs[:CHIPS], right))
            core_ref[
                left * width : (left + 1) * width, right * width : (right + 1) * width
            ] = product.astype(jnp.bfloat16)


def block_call(body, outs, arrays, flops):
    return pl.pallas_call(
        body,
        out_shape=outs,
        in_specs=[pl.BlockSpec(memory_space=pltpu.VMEM)] * len(arrays),
        out_specs=[pl.BlockSpec(memory_space=pltpu.VMEM)] * len(outs),
        compiler_params=pltpu.CompilerParams(vmem_limit_bytes=ROOM),
        cost_estimate=pl.CostEstimate(
            flops=flops,
            bytes_accessed=sum(array.size * array.dtype.itemsize for array in arrays),
            transcendentals=0,
        ),
    )(*arrays)


def after(value, earlier):
    return lax.optimization_barrier((value, earlier))[0]


def gathered_plan(inputs, teacher, gate, route, slot, factor, cores):
    bf16, f32 = jnp.bfloat16, jnp.float32
    shared = factor[0]
    channels, ranks = shared.shape
    devices = lax.axis_size("expert")
    micro_count, token_count = route.shape[1:]
    rows = micro_count * token_count
    here = lax.axis_index("expert")
    chip, core = here // CORES, here % CORES
    middle = jnp.logical_or(chip == 1, chip == 2)
    tokens = inputs[0].reshape(rows, channels)

    travelled = gather_cores(cores[0, 0])
    marks = row_marks(
        route[0].reshape(rows, 1), gate[0].reshape(rows, 1), chip, core, middle
    )

    down = [(3, 2), (1, 0)]
    two_down = [(3, 1), (2, 0)]
    two_cross, down_cross = [(0, 1)], [(2, 0)]
    own_half = chip_blocks(shared, chip, core)
    half_down = between_layers(own_half, down)
    half_two = between_layers(own_half, two_down)
    half_cross = between_layers(half_two, two_cross)
    half_late = between_layers(half_down, down_cross)
    turned = lax.optimization_barrier(tokens.T)
    wanted = lax.optimization_barrier(teacher[0].reshape(rows, channels).T)
    difference = (turned.astype(f32) - wanted.astype(f32)).astype(bf16)
    difference = chip_columns(difference, chip, core)
    step_down = between_layers(difference, down)
    step_two = between_layers(difference, two_down)

    capacity = max(2, 2 * token_count // devices)
    slots = micro_count * capacity
    micro = jnp.arange(rows, dtype=jnp.int32) // token_count
    expert = route[0].reshape(rows)
    near = (expert % CORES ^ core) * CHIPS + (expert // CORES ^ chip)
    place = near * slots + micro * capacity + slot[0].reshape(rows)
    picks = (jnp.arange(devices * slots, dtype=jnp.int32)[:, None] == place[None, :]).astype(bf16)

    def to_slots(values):
        held = dot(picks, values).astype(bf16)
        half = CHIPS * slots
        return held[:half], swap_cores(held[half:])

    step_cross = between_layers(step_two, two_cross)
    step_late = between_layers(step_down, down_cross)
    projected = dot(tokens, shared).astype(bf16)
    own_gram = gram_pair(own_half, own_half)
    proj_slots = to_slots(projected)
    gram = gram_sum(own_gram)
    own_score = both_cores(dot_first(difference, own_half))
    turned = chip_columns(turned, chip, core)
    token_blocks = [
        under_block(
            turned[step * channels // devices : (step + 1) * channels // devices],
            *proj_slots,
            step,
        )
        for step in range(CHIPS)
    ]
    down_pair = gram_pair(half_down, own_half)
    down_gram = gram_sum(down_pair)
    two_gram = gram_sum(gram_pair(half_two, own_half))
    down_score = both_cores(dot_first(step_down, own_half))

    wide = (rows, ranks)
    product_flops = 2 * rows * ranks * ranks
    flag = middle.astype(jnp.int32).reshape(1)
    block = pltpu.VMEM((ranks, ranks), bf16)

    def core_call(body, sources, outs, arrays, scratch, products):
        flat = [ref for source in sources for ref in (source if type(source) is tuple else [source])]
        return pl.pallas_call(
            body,
            out_shape=outs,
            in_specs=[pl.BlockSpec(memory_space=pltpu.SMEM)]
            + [pl.BlockSpec(memory_space=pltpu.VMEM)] * len(arrays)
            + [pl.BlockSpec(memory_space=pl.ANY)] * len(flat),
            out_specs=[pl.BlockSpec(memory_space=pltpu.VMEM)] * len(outs),
            scratch_shapes=scratch + [pltpu.SemaphoreType.DMA((len(flat),))],
            compiler_params=pltpu.CompilerParams(vmem_limit_bytes=ROOM),
            cost_estimate=pl.CostEstimate(
                flops=product_flops * products,
                bytes_accessed=2 * len(sources) * ranks * ranks,
                transcendentals=0,
            ),
        )(flag, *arrays, *flat)

    part, *held = core_call(
        early_kernel,
        travelled[:-2],
        [jax.ShapeDtypeStruct(wide, f32)] + [block] * (devices - 2),
        [projected, marks],
        [],
        devices - 2,
    )
    scaled, slope, score, chain, *last = core_call(
        first_kernel,
        [*travelled[-2:], own_score, gram],
        [jax.ShapeDtypeStruct(wide, kind) for kind in (bf16, f32, f32, bf16)] + [block] * 2,
        [projected, marks, part, *held],
        [pltpu.VMEM(wide, f32), pltpu.VMEM((ranks, ranks), bf16)],
        devices + 3,
    )
    pieces = [*held, *last]

    def turn(score, late, terms):
        arrays = [array for pair in terms for array in pair]

        def body(*refs):
            turn_kernel(len(terms), bool(late), *refs)

        return call_rows(
            body,
            [(wide, f32), (wide, bf16), (wide, bf16), (wide, bf16)],
            [marks, scaled, slope, score, *late, *arrays, *pieces],
            product_flops * (devices + len(terms)),
        )

    chain_first = chain
    first_down = between_layers(chain, [(3, 2)])
    first_two = between_layers(chain, [(3, 1)])
    scaled_rows = [scaled] + [across_chips(after(scaled, chain), step) for step in range(1, CHIPS)]
    token_blocks = token_blocks[:1] + [
        across_chips(after(token_blocks[step], chain), step) for step in range(1, CHIPS)
    ]
    score, _, _, chain = turn(score, [down_score], [(first_down, down_gram)])

    second_cross = between_layers(chain, [(2, 1)])
    second_two = between_layers(chain, [(2, 0)])
    first_three = between_layers(after(chain_first, chain), [(3, 0)])
    half_cross = after(half_cross, chain)
    step_cross = after(step_cross, chain)
    cross_pair = gram_pair(half_cross, own_half)
    late_steps = (step_two.astype(f32) + step_cross.astype(f32)).astype(bf16)
    late_score = both_cores(dot_first(late_steps, own_half))
    cross_product = gram_sum(cross_pair)
    score, _, _, chain = turn(
        score, [late_score], [(first_two, two_gram), (second_cross, cross_product)]
    )

    third_down = between_layers(chain, [(1, 0)])
    half_late, step_late = after(half_late, chain), after(step_late, chain)
    late_pair = gram_pair(half_late, own_half)
    last_score = both_cores(dot_first(step_late, own_half))
    steps_total = difference.astype(f32) + step_down.astype(f32)
    steps_total = steps_total + after(late_steps, chain).astype(f32)
    steps_total = (steps_total + step_late.astype(f32)).astype(bf16)
    late_product = gram_sum(late_pair)
    score, grad_pre, grad_proj, _ = turn(
        score,
        [last_score],
        [(second_two, two_gram), (first_three, late_product), (third_down, down_gram)],
    )

    def with_swap(values):
        return values, swap_cores(values)

    proj_rows = gather_rows(grad_proj)
    grad_slots = to_slots(grad_pre)
    scaled_pair = with_swap(after(scaled, grad_proj))
    two_pair = with_swap(first_two + after(second_two, grad_proj))
    cross_pair = with_swap(after(second_cross, grad_proj))
    late_pair = with_swap(after(first_three, grad_proj))
    down_pair = with_swap(first_down + third_down)
    mixed_blocks = spread(
        steps_total,
        [
            (own_half, *scaled_pair),
            (half_two, *two_pair),
            (half_cross, *cross_pair),
            (half_late, *late_pair),
            (half_down, *down_pair),
        ],
        *grad_slots,
    )
    mixed_first = mixed_blocks[0]
    scaled_rows = [after(rows, mixed_first) for rows in scaled_rows]
    mixed_blocks = list(mixed_blocks[:1]) + [
        across_chips(mixed_blocks[step], step) for step in range(1, CHIPS)
    ]
    scaled_rows = scaled_rows + [scaled_pair[1]] + [swap_cores(rows) for rows in scaled_rows[1:]]
    share = jax.ShapeDtypeStruct((channels // devices, ranks), f32)
    share_flops = 2 * channels * rows * ranks
    token_share = block_call(token_kernel, [share], token_blocks + proj_rows, share_flops)
    factor_share, core_total = block_call(
        last_kernel,
        [share, jax.ShapeDtypeStruct((ranks, ranks), bf16)],
        [*token_blocks, *token_share, *mixed_blocks, *scaled_rows],
        share_flops,
    )
    return (factor_share[None], core_total[None, None])


def solution(mesh):
    placed = (
        P("section", None, "expert", None),
        P("section", None, "expert", None),
        P("section", None, "expert"),
        P("section", None, "expert"),
        P("section", None, "expert"),
        P("section", None, None),
        P("section", "expert", None, None),
    )
    drawn_for = (LAYERS, CHIPS * CORES)

    def per_device(*arrays):
        local_experts = arrays[-1].shape[1]
        ranks, width = arrays[-1].shape[-1], CORES * arrays[3].shape[1] * arrays[3].shape[2]
        fits = local_experts == 1 and ranks % width == 0
        if (mesh.shape["section"], mesh.shape["expert"]) == drawn_for and fits:
            return gathered_plan(*arrays)
        return general_plan(*arrays)

    return jax.shard_map(
        per_device,
        mesh=mesh,
        in_specs=placed,
        out_specs=(P("section", "expert", None), P("section", "expert", None, None)),
        check_vma=False,
    )
```

```python
import jax
import jax.numpy as jnp
from jax import lax
from jax.experimental import pallas as pl
from jax.experimental.pallas import tpu as pltpu
from jax.sharding import PartitionSpec as P


def from_behind(value, axis, steps):
    count = lax.axis_size(axis)
    leading, last = (max(0, -steps), min(count, count - steps))
    return lax.ppermute(value, axis, [(source, source + steps) for source in range(leading, last)])


def silu_slope(values):
    sigmoid = jax.nn.sigmoid(values)
    return sigmoid * (1.0 + values * (1.0 - sigmoid))


def times_transposed(left, shared):
    return lax.dot_general(
        left, shared, (((1,), (1,)), ((), ())), preferred_element_type=jnp.float32
    )


def factor_terms(tokens_flat, proj_flat, mixed_flat, hidden_flat):

    def factor_rows(start, count):
        first_term = lax.dot_general(
            tokens_flat, proj_flat, (((0,), (0,)), ((), ())), preferred_element_type=jnp.float32
        )
        second_term = lax.dot_general(
            mixed_flat, hidden_flat, (((0,), (0,)), ((), ())), preferred_element_type=jnp.float32
        )
        return first_term + second_term

    return factor_rows


def store_slice(store, fresh, picked, usable):
    former = lax.dynamic_index_in_dim(store, picked, 0, keepdims=False)
    kept = jnp.where(usable, fresh, former)
    return lax.dynamic_update_index_in_dim(store, kept, picked, 0)


def general_plan(inputs, teacher, gate, route, slot, factor, cores):
    tokens_all = inputs[0]
    targets_all = teacher[0]
    weights_all = gate[0]
    shared = factor[0]
    blocks = cores[0]
    micro_count, token_count, channels = tokens_all.shape
    ranks = shared.shape[1]
    local_experts = blocks.shape[0]
    expert_devices = lax.axis_size("expert")
    capacity = max(2, 2 * token_count // (local_experts * expert_devices))
    slot_count = local_experts * expert_devices * capacity
    places_all = route[0] * capacity + slot[0]
    micro_range = jnp.arange(micro_count, dtype=jnp.int32)[:, None]
    token_proj = jnp.dot(
        tokens_all.reshape(-1, channels), shared, preferred_element_type=jnp.float32
    ).astype(jnp.bfloat16)
    token_proj = token_proj.reshape(micro_count, token_count, ranks)
    proj_slots = (
        jnp.zeros((micro_count, slot_count, ranks), jnp.bfloat16)
        .at[micro_range, places_all]
        .set(token_proj)
    )
    projected = lax.all_to_all(proj_slots, "expert", split_axis=1, concat_axis=1, tiled=True)
    projected = projected.reshape(micro_count, expert_devices, local_experts, capacity, ranks)
    pre = jnp.einsum("mnecr,erk->mneck", projected, blocks, preferred_element_type=jnp.float32)
    active = jax.nn.silu(pre).astype(jnp.bfloat16)
    returned = lax.all_to_all(
        active.reshape(micro_count, slot_count, ranks),
        "expert",
        split_axis=1,
        concat_axis=1,
        tiled=True,
    )
    hidden = jnp.take_along_axis(returned, places_all[:, :, None], axis=1)
    mixed = times_transposed(hidden.reshape(-1, ranks), shared).reshape(
        micro_count, token_count, channels
    )
    output = tokens_all.astype(jnp.float32) + weights_all[:, :, None] * mixed
    errors = output - targets_all.astype(jnp.float32)
    section_count = lax.axis_size("section")
    section_here = lax.axis_index("section")
    incoming = jnp.zeros((token_count, channels), jnp.bfloat16)
    mixed_store = jnp.zeros((micro_count, token_count, channels), jnp.bfloat16)
    proj_store = jnp.zeros((micro_count, token_count, ranks), jnp.bfloat16)
    pre_store = jnp.zeros(
        (micro_count, expert_devices, local_experts, capacity, ranks), jnp.bfloat16
    )
    turn_total = micro_count + section_count - 1
    for turn_index in range(turn_total):
        micro_now = turn_index - (section_count - 1 - section_here)
        usable = jnp.logical_and(micro_now >= 0, micro_now < micro_count)
        picked = jnp.clip(micro_now, 0, micro_count - 1)
        grad_out = lax.dynamic_index_in_dim(errors, picked, 0, keepdims=False) + incoming.astype(
            jnp.float32
        )
        weight_now = lax.dynamic_index_in_dim(weights_all, picked, 0, keepdims=False)
        places = lax.dynamic_index_in_dim(places_all, picked, 0, keepdims=False)
        grad_mixed = (weight_now[:, None] * grad_out).astype(jnp.bfloat16)
        grad_hidden = jnp.dot(grad_mixed, shared, preferred_element_type=jnp.float32).astype(
            jnp.bfloat16
        )
        grad_slots = jnp.zeros((slot_count, ranks), jnp.bfloat16).at[places].set(grad_hidden)
        grad_recv = lax.all_to_all(grad_slots, "expert", split_axis=0, concat_axis=0, tiled=True)
        grad_recv = grad_recv.reshape(expert_devices, local_experts, capacity, ranks)
        pre_now = lax.dynamic_index_in_dim(pre, picked, 0, keepdims=False)
        grad_pre = (grad_recv.astype(jnp.float32) * silu_slope(pre_now)).astype(jnp.bfloat16)
        grad_routed = jnp.einsum(
            "neck,erk->necr", grad_pre, blocks, preferred_element_type=jnp.float32
        ).astype(jnp.bfloat16)
        grad_home = lax.all_to_all(
            grad_routed.reshape(slot_count, ranks),
            "expert",
            split_axis=0,
            concat_axis=0,
            tiled=True,
        )
        grad_proj = grad_home[places]
        grad_in = (grad_out + times_transposed(grad_proj, shared)).astype(jnp.bfloat16)
        if turn_index + 1 < turn_total:
            incoming = from_behind(grad_in, "section", -1)
        mixed_store = store_slice(mixed_store, grad_mixed, picked, usable)
        proj_store = store_slice(proj_store, grad_proj, picked, usable)
        pre_store = store_slice(pre_store, grad_pre, picked, usable)
    core_total = jnp.einsum(
        "mnecr,mneck->erk", projected, pre_store, preferred_element_type=jnp.float32
    )
    all_rows = factor_terms(
        tokens_all.reshape(-1, channels),
        proj_store.reshape(-1, ranks),
        mixed_store.reshape(-1, channels),
        hidden.reshape(-1, ranks),
    )
    factor_share = lax.psum_scatter(
        all_rows(jnp.int32(0), channels // expert_devices * lax.axis_size("expert")),
        "expert",
        scatter_dimension=0,
        tiled=True,
    )
    return (factor_share[None], core_total.astype(jnp.bfloat16)[None])


CORES = 2
CHIPS = 4
LAYERS = 4
ROOM = 16 * 2**20


def dot(left, right):
    return jnp.dot(left, right, preferred_element_type=jnp.float32)


def dot_first(left, right):
    return lax.dot_general(
        left, right, (((0,), (0,)), ((), ())), preferred_element_type=jnp.float32
    )


def on_chips(value, pairs):
    perm = [
        (CORES * source + core, CORES * target + core)
        for source, target in pairs
        for core in range(CORES)
    ]
    return lax.ppermute(value, "expert", perm)


def swap_cores(value):
    count = lax.axis_size("expert")
    return lax.ppermute(value, "expert", [(index, index ^ 1) for index in range(count)])


def between_layers(value, pairs):
    return lax.ppermute(value, "section", pairs)


def gather_cores(core):
    beside = on_chips(core, [(0, 1), (1, 0), (2, 3), (3, 2)])
    across = on_chips(core, [(1, 2), (2, 1)])
    far_across = on_chips(beside, [(1, 2), (2, 1)])
    outward = on_chips(across, [(1, 0), (2, 3)])
    far_outward = on_chips(far_across, [(1, 0), (2, 3)])
    held, swapped = [core, beside], [swap_cores(piece) for piece in (core, beside)]
    near = [(across, outward), (far_across, far_outward)]
    far = [tuple(swap_cores(piece) for piece in pair) for pair in near]
    return [piece for both in zip(held + near, swapped + far) for piece in both]


def row_marks(route, weight, chip, core, middle):
    count = CHIPS * CORES
    place = lax.broadcasted_iota(jnp.int32, (1, 2 * count), 1)
    step = (place % count) // CORES
    turned = jnp.where(jnp.logical_and(step >= 2, middle), 5 - step, step)
    expert = CORES * (chip ^ turned) + (core ^ (place % CORES))
    marks = (route == expert).astype(jnp.float32)
    return jnp.where(place < count, marks, weight)


def across_chips(value, step):
    return on_chips(value, [(chip, chip ^ step) for chip in range(CHIPS)])


def gather_rows(rows):
    held = [rows] + [across_chips(rows, step) for step in range(1, CHIPS)]
    return held + [swap_cores(piece) for piece in held]


def chip_blocks(wide, chip, core):
    count = wide.shape[0] // (CHIPS * CORES)
    blocks = [
        lax.dynamic_slice_in_dim(wide, (CORES * (chip ^ step) + core) * count, count, 0)
        for step in range(CHIPS)
    ]
    return jnp.concatenate(blocks, axis=0)


def chip_columns(wide, chip, core):
    theirs = swap_cores(chip_blocks(wide, chip, 1 - core))
    return jnp.concatenate([chip_blocks(wide, chip, core), theirs], axis=1)


def both_cores(partial):
    rows = partial.shape[0] // CORES
    return partial[:rows] + swap_cores(partial[rows:])


def gram_pair(left, right):
    partial = dot_first(left, right).astype(jnp.bfloat16)
    return partial, swap_cores(partial)


def gram_sum(pair):
    return (pair[0].astype(jnp.float32) + pair[1].astype(jnp.float32)).astype(jnp.bfloat16)


def routed_product(rows, marks, start, core_refs, transposed, copies=None):
    dims = (((1,), (1 if transposed else 0,)), ((), ()))
    total = None
    for place, core_ref in enumerate(core_refs):
        if copies is not None:
            copies[place].wait()
        mark = marks[:, start + place : start + place + 1]
        chosen = jnp.where(mark > 0.5, rows, jnp.zeros_like(rows))
        term = lax.dot_general(
            chosen, core_ref[...], dims, preferred_element_type=jnp.float32
        )
        total = term if total is None else total + term
    return total


def backward_rows(score, slope, marks, core_refs):
    count = len(core_refs)
    grad_hidden = (marks[:, count : count + 1] * score).astype(jnp.bfloat16)
    grad_pre = (grad_hidden.astype(jnp.float32) * slope).astype(jnp.bfloat16)
    grad_proj = routed_product(grad_pre, marks, 0, core_refs, True)
    return grad_pre, grad_proj.astype(jnp.bfloat16)


def fetch(middle, sources, targets, arrived):
    copies = []
    for place, (source, target) in enumerate(zip(sources, targets)):
        choices = source if isinstance(source, tuple) else (source,)
        moves = [pltpu.make_async_copy(ref, target, arrived.at[place]) for ref in choices]
        copies.append(moves[0])
        if len(moves) == 1:
            moves[0].start()
        else:
            pl.when(middle)(moves[0].start)
            pl.when(jnp.logical_not(middle))(moves[1].start)
    return copies


def early_kernel(middle_ref, proj_ref, marks_ref, *refs):
    sources = [*refs[:4], (refs[4], refs[5]), (refs[6], refs[7])]
    part_ref, core_refs, arrived = refs[8], refs[9:-1], refs[-1]
    copies = fetch(middle_ref[0] > 0, sources, core_refs, arrived)
    part_ref[...] = routed_product(proj_ref[...], marks_ref[...], 0, core_refs, False, copies)


def first_kernel(middle_ref, proj_ref, marks_ref, part_ref, *refs):
    early = CHIPS * CORES - 2
    held, refs = refs[:early], refs[early:]
    sources = [(refs[0], refs[1]), (refs[2], refs[3]), refs[4], refs[5]]
    token_refs, refs = refs[6 : 5 + CHIPS], refs[5 + CHIPS :]
    scaled_ref, slope_ref, score_ref, chain_ref = refs[:4]
    sent_refs, (near_ref, far_ref) = refs[4 : 3 + CHIPS], refs[3 + CHIPS : 5 + CHIPS]
    own_ref, gram_ref, arrived, moved = refs[5 + CHIPS :]
    tall, width = token_refs[0].shape
    moves = [
        pltpu.make_async_copy(token_ref, sent_ref.at[pl.ds(0, tall), :], moved.at[place])
        for place, (token_ref, sent_ref) in enumerate(zip(token_refs, sent_refs))
    ]
    for move in moves:
        move.start()
    last = [near_ref, far_ref]
    copies = fetch(middle_ref[0] > 0, sources, [*last, own_ref, gram_ref], arrived)
    core_refs, count = [*held, *last], early + 2
    marks = marks_ref[...]
    pre = part_ref[...] + routed_product(proj_ref[...], marks, early, last, False, copies)
    sigmoid = 1.0 / (1.0 + jnp.exp(-pre))
    hidden = (pre * sigmoid).astype(jnp.bfloat16)
    slope = sigmoid * (1.0 + pre * (1.0 - sigmoid))
    weight = marks[:, count : count + 1]
    scaled = (weight * hidden.astype(jnp.float32)).astype(jnp.bfloat16)
    copies[2].wait()
    copies[3].wait()
    score = own_ref[...] + dot(scaled, gram_ref[...])
    scaled_ref[...] = scaled
    rows = scaled.shape[0]
    for sent_ref in sent_refs:
        for group in range(scaled.shape[1] // width):
            sent_ref[pl.ds(tall + group * rows, rows), :] = scaled[
                :, group * width : (group + 1) * width
            ]
    slope_ref[...] = slope
    score_ref[...] = score
    _, grad_proj = backward_rows(score, slope, marks, core_refs)
    chain_ref[...] = (scaled.astype(jnp.float32) + grad_proj.astype(jnp.float32)).astype(
        jnp.bfloat16
    )
    for move in moves:
        move.wait()


def turn_kernel(terms, late, marks_ref, scaled_ref, slope_ref, score_ref, *refs):
    score = score_ref[...]
    if late:
        score, refs = score + refs[0][...], refs[1:]
    core_refs = refs[2 * terms : len(refs) - 4]
    next_ref, grad_ref, proj_ref, chain_ref = refs[len(refs) - 4 :]
    for term in range(terms):
        score = score + dot(refs[2 * term][...], refs[2 * term + 1][...])
    next_ref[...] = score
    grad_pre, grad_proj = backward_rows(score, slope_ref[...], marks_ref[...], core_refs)
    grad_ref[...] = grad_pre
    proj_ref[...] = grad_proj
    chain_ref[...] = (scaled_ref[...].astype(jnp.float32) + grad_proj.astype(jnp.float32)).astype(
        jnp.bfloat16
    )


def call_rows(body, outs, arrays, flops, scalars=()):
    in_bytes = sum(array.size * array.dtype.itemsize for array in arrays)
    return pl.pallas_call(
        body,
        out_shape=[jax.ShapeDtypeStruct(shape, kind) for shape, kind in outs],
        in_specs=[pl.BlockSpec(memory_space=pltpu.SMEM)] * len(scalars)
        + [pl.BlockSpec(memory_space=pltpu.VMEM)] * len(arrays),
        out_specs=[pl.BlockSpec(memory_space=pltpu.VMEM)] * len(outs),
        compiler_params=pltpu.CompilerParams(vmem_limit_bytes=ROOM),
        cost_estimate=pl.CostEstimate(flops=flops, bytes_accessed=in_bytes, transcendentals=0),
    )(*scalars, *arrays)


def spread_kernel(terms, base_ref, *refs):
    total = base_ref[...].astype(jnp.float32)
    for term in range(terms):
        half_ref, near_ref, far_ref = refs[3 * term : 3 * term + 3]
        values = jnp.concatenate([near_ref[...], far_ref[...]], axis=0)
        total = total + times_transposed(half_ref[...], values)
    block = total.astype(jnp.bfloat16)
    slot_refs, outs = refs[3 * terms : 3 * terms + 2], refs[3 * terms + 2 :]
    count, width = block.shape
    for step, out_ref in enumerate(outs):

        @pl.when(pl.program_id(0) == step)
        def _():
            out_ref[:count, :] = block
            for part, (row, column, slots) in enumerate(slot_tiles(slot_refs[0], width)):
                slot_ref = slot_refs[part % CORES]
                out_ref[pl.ds(count + row, slots), :] = slot_ref[
                    step * slots : (step + 1) * slots, column : column + width
                ]


def slot_tiles(slot_ref, width):
    slots = slot_ref.shape[0] // CHIPS
    groups = slot_ref.shape[1] // width
    return [
        ((CORES * group + side) * slots, group * width, slots)
        for group in range(groups)
        for side in range(CORES)
    ]


def under_block(block, own, theirs, step):
    width = block.shape[1]
    parts = [
        (own, theirs)[part % CORES][step * slots : (step + 1) * slots, column : column + width]
        for part, (_, column, slots) in enumerate(slot_tiles(own, width))
    ]
    return jnp.concatenate([block, *parts], axis=0)


def spread(base, terms, own_slots, their_slots):
    arrays = [base] + [array for term in terms for array in term] + [own_slots, their_slots]
    height, width = base.shape
    count = height // CHIPS
    tall = count + CORES * own_slots.size // (CHIPS * width)

    def rows(columns):
        return pl.BlockSpec((count, columns), lambda step: (step, 0))

    def whole(array):
        return pl.BlockSpec(array.shape, lambda step: (0, 0))

    specs = [rows(width)]
    for half, near, far in terms:
        specs += [rows(half.shape[1]), whole(near), whole(far)]
    specs += [whole(own_slots), whole(their_slots)]

    def body(*refs):
        spread_kernel(len(terms), *refs)

    return pl.pallas_call(
        body,
        name="spread",
        grid=(CHIPS,),
        out_shape=[jax.ShapeDtypeStruct((tall, width), jnp.bfloat16)] * CHIPS,
        in_specs=specs,
        out_specs=[pl.BlockSpec((tall, width), lambda step: (0, 0))] * CHIPS,
        compiler_params=pltpu.CompilerParams(vmem_limit_bytes=ROOM),
        cost_estimate=pl.CostEstimate(
            flops=2 * height * width * terms[0][0].shape[1] * len(terms),
            bytes_accessed=sum(array.size * array.dtype.itemsize for array in arrays),
            transcendentals=0,
        ),
    )(*arrays)


def pair_products(block_ref, count, near_ref, far_ref):
    return dot(block_ref[:count, :], jnp.concatenate([near_ref[...], far_ref[...]], axis=0))


def block_products(count, refs):
    total = None
    for step in range(CHIPS):
        term = pair_products(refs[step], count, refs[CHIPS + step], refs[2 * CHIPS + step])
        total = term if total is None else total + term
    return total


def token_kernel(*refs):
    refs[-1][...] = block_products(refs[-1].shape[0], refs[:-1])


def grouped_rows(ref, start, rows):
    groups = (ref.shape[0] - start) // rows
    return jnp.concatenate(
        [ref[start + group * rows : start + (group + 1) * rows, :] for group in range(groups)],
        axis=1,
    )


def last_kernel(*refs):
    token_refs, refs = refs[:CHIPS], refs[CHIPS:]
    total_ref, product_refs, scaled_refs = refs[0], refs[1 : 1 + CHIPS], refs[1 + CHIPS : -2]
    share_ref, core_ref = refs[-2:]
    count = share_ref.shape[0]
    rows, tall = scaled_refs[0].shape[0], token_refs[0].shape[0]
    total = total_ref[...]
    for step in range(CHIPS):
        if step == 0:
            near, far = scaled_refs[0][...], scaled_refs[1][...]
        else:
            near = grouped_rows(token_refs[step], tall, rows)
            far = grouped_rows(scaled_refs[1 + step], 0, rows)
        total = total + dot(product_refs[step][:count, :], jnp.concatenate([near, far], axis=0))
    share_ref[...] = total
    width = token_refs[0].shape[1]
    slots = (token_refs[0].shape[0] - count) * width // core_ref.shape[0]

    def group(block_refs, column):
        start = count + column * slots
        return jnp.concatenate([ref[start : start + slots, :] for ref in block_refs], axis=0)

    groups = core_ref.shape[0] // width
    for left in range(groups):
        for right in range(groups):
            product = dot_first(group(token_refs, left), group(product_refs[:CHIPS], right))
            core_ref[
                left * width : (left + 1) * width, right * width : (right + 1) * width
            ] = product.astype(jnp.bfloat16)


def block_call(body, outs, arrays, flops):
    return pl.pallas_call(
        body,
        out_shape=outs,
        in_specs=[pl.BlockSpec(memory_space=pltpu.VMEM)] * len(arrays),
        out_specs=[pl.BlockSpec(memory_space=pltpu.VMEM)] * len(outs),
        compiler_params=pltpu.CompilerParams(vmem_limit_bytes=ROOM),
        cost_estimate=pl.CostEstimate(
            flops=flops,
            bytes_accessed=sum(array.size * array.dtype.itemsize for array in arrays),
            transcendentals=0,
        ),
    )(*arrays)


def after(value, earlier):
    return lax.optimization_barrier((value, earlier))[0]


def gathered_plan(inputs, teacher, gate, route, slot, factor, cores):
    bf16, f32 = jnp.bfloat16, jnp.float32
    shared = factor[0]
    channels, ranks = shared.shape
    devices = lax.axis_size("expert")
    micro_count, token_count = route.shape[1:]
    rows = micro_count * token_count
    here = lax.axis_index("expert")
    chip, core = here // CORES, here % CORES
    middle = jnp.logical_or(chip == 1, chip == 2)
    tokens = inputs[0].reshape(rows, channels)

    travelled = gather_cores(cores[0, 0])
    marks = row_marks(
        route[0].reshape(rows, 1), gate[0].reshape(rows, 1), chip, core, middle
    )

    down = [(3, 2), (1, 0)]
    two_down = [(3, 1), (2, 0)]
    two_cross, down_cross = [(0, 1)], [(2, 0)]
    own_half = chip_blocks(shared, chip, core)
    half_down = between_layers(own_half, down)
    half_two = between_layers(own_half, two_down)
    half_cross = between_layers(half_two, two_cross)
    half_late = between_layers(half_down, down_cross)
    turned = lax.optimization_barrier(tokens.T)
    wanted = lax.optimization_barrier(teacher[0].reshape(rows, channels).T)
    difference = (turned.astype(f32) - wanted.astype(f32)).astype(bf16)
    difference = chip_columns(difference, chip, core)
    step_down = between_layers(difference, down)
    step_two = between_layers(difference, two_down)

    capacity = max(2, 2 * token_count // devices)
    slots = micro_count * capacity
    micro = jnp.arange(rows, dtype=jnp.int32) // token_count
    expert = route[0].reshape(rows)
    near = (expert % CORES ^ core) * CHIPS + (expert // CORES ^ chip)
    place = near * slots + micro * capacity + slot[0].reshape(rows)
    picks = (jnp.arange(devices * slots, dtype=jnp.int32)[:, None] == place[None, :]).astype(bf16)

    def to_slots(values):
        held = dot(picks, values).astype(bf16)
        half = CHIPS * slots
        return held[:half], swap_cores(held[half:])

    step_cross = between_layers(step_two, two_cross)
    step_late = between_layers(step_down, down_cross)
    projected = dot(tokens, shared).astype(bf16)
    own_gram = gram_pair(own_half, own_half)
    proj_slots = to_slots(projected)
    gram = gram_sum(own_gram)
    own_score = both_cores(dot_first(difference, own_half))
    turned = chip_columns(turned, chip, core)
    token_blocks = [
        under_block(
            turned[step * channels // devices : (step + 1) * channels // devices],
            *proj_slots,
            step,
        )
        for step in range(CHIPS)
    ]
    down_gram = gram_sum(gram_pair(half_down, own_half))
    two_gram = gram_sum(gram_pair(half_two, own_half))
    down_score = both_cores(dot_first(step_down, own_half))

    wide = (rows, ranks)
    product_flops = 2 * rows * ranks * ranks
    flag = middle.astype(jnp.int32).reshape(1)
    block = pltpu.VMEM((ranks, ranks), bf16)

    def core_call(body, sources, outs, arrays, scratch, products, extra=()):
        flat = [ref for source in sources for ref in (source if type(source) is tuple else [source])]
        moved = [pltpu.SemaphoreType.DMA((len(extra),))] if extra else []
        return pl.pallas_call(
            body,
            out_shape=outs,
            in_specs=[pl.BlockSpec(memory_space=pltpu.SMEM)]
            + [pl.BlockSpec(memory_space=pltpu.VMEM)] * len(arrays)
            + [pl.BlockSpec(memory_space=pl.ANY)] * (len(flat) + len(extra)),
            out_specs=[pl.BlockSpec(memory_space=pltpu.VMEM)] * len(outs),
            scratch_shapes=scratch + [pltpu.SemaphoreType.DMA((len(sources),))] + moved,
            compiler_params=pltpu.CompilerParams(vmem_limit_bytes=ROOM),
            cost_estimate=pl.CostEstimate(
                flops=product_flops * products,
                bytes_accessed=2 * len(sources) * ranks * ranks,
                transcendentals=0,
            ),
        )(flag, *arrays, *flat, *extra)

    part, *held = core_call(
        early_kernel,
        travelled[:-2],
        [jax.ShapeDtypeStruct(wide, f32)] + [block] * (devices - 2),
        [projected, marks],
        [],
        devices - 2,
    )
    sent = pltpu.VMEM((token_blocks[0].shape[0] + ranks // CORES, CORES * rows), bf16)
    scaled, slope, score, chain, *last = core_call(
        first_kernel,
        [*travelled[-2:], own_score, gram],
        [jax.ShapeDtypeStruct(wide, kind) for kind in (bf16, f32, f32, bf16)]
        + [sent] * (CHIPS - 1)
        + [block] * 2,
        [projected, marks, part, *held],
        [pltpu.VMEM(wide, f32), pltpu.VMEM((ranks, ranks), bf16)],
        devices + 3,
        token_blocks[1:],
    )
    sent, last = last[: CHIPS - 1], last[CHIPS - 1 :]
    pieces = [*held, *last]

    def turn(score, late, terms):
        arrays = [array for pair in terms for array in pair]

        def body(*refs):
            turn_kernel(len(terms), bool(late), *refs)

        return call_rows(
            body,
            [(wide, f32), (wide, bf16), (wide, bf16), (wide, bf16)],
            [marks, scaled, slope, score, *late, *arrays, *pieces],
            product_flops * (devices + len(terms)),
        )

    chain_first = chain
    first_down = between_layers(chain, [(3, 2)])
    first_two = between_layers(chain, [(3, 1)])
    token_blocks = token_blocks[:1] + [
        across_chips(sent[step - 1], step) for step in range(1, CHIPS)
    ]
    score, _, _, chain = turn(score, [down_score], [(first_down, down_gram)])

    second_cross = between_layers(chain, [(2, 1)])
    second_two = between_layers(chain, [(2, 0)])
    first_three = between_layers(after(chain_first, chain), [(3, 0)])
    half_cross = after(half_cross, chain)
    step_cross = after(step_cross, chain)
    cross_pair = gram_pair(half_cross, own_half)
    late_steps = (step_two.astype(f32) + step_cross.astype(f32)).astype(bf16)
    late_score = both_cores(dot_first(late_steps, own_half))
    cross_product = gram_sum(cross_pair)
    score, _, _, chain = turn(
        score, [late_score], [(first_two, two_gram), (second_cross, cross_product)]
    )

    third_down = between_layers(chain, [(1, 0)])
    half_late, step_late = after(half_late, chain), after(step_late, chain)
    late_pair = gram_pair(half_late, own_half)
    last_score = both_cores(dot_first(step_late, own_half))
    steps_total = difference.astype(f32) + step_down.astype(f32)
    steps_total = steps_total + after(late_steps, chain).astype(f32)
    steps_total = (steps_total + step_late.astype(f32)).astype(bf16)
    late_product = gram_sum(late_pair)
    score, grad_pre, grad_proj, _ = turn(
        score,
        [last_score],
        [(second_two, two_gram), (first_three, late_product), (third_down, down_gram)],
    )

    def with_swap(values):
        return values, swap_cores(values)

    proj_rows = gather_rows(grad_proj)
    grad_slots = to_slots(grad_pre)
    scaled_pair = with_swap(after(scaled, grad_proj))
    two_pair = with_swap(first_two + after(second_two, grad_proj))
    cross_pair = with_swap(after(second_cross, grad_proj))
    late_pair = with_swap(after(first_three, grad_proj))
    down_pair = with_swap(first_down + third_down)
    mixed_blocks = spread(
        steps_total,
        [
            (own_half, *scaled_pair),
            (half_two, *two_pair),
            (half_cross, *cross_pair),
            (half_late, *late_pair),
            (half_down, *down_pair),
        ],
        *grad_slots,
    )
    mixed_first = mixed_blocks[0]
    tall = token_blocks[0].shape[0]
    scaled_parts = [after(part, mixed_first)[tall:] for part in token_blocks[1:]]
    mixed_blocks = list(mixed_blocks[:1]) + [
        across_chips(mixed_blocks[step], step) for step in range(1, CHIPS)
    ]
    scaled_rows = [*scaled_pair, *(swap_cores(part) for part in scaled_parts)]
    share = jax.ShapeDtypeStruct((channels // devices, ranks), f32)
    share_flops = 2 * channels * rows * ranks
    token_share = block_call(token_kernel, [share], token_blocks + proj_rows, share_flops)
    factor_share, core_total = block_call(
        last_kernel,
        [share, jax.ShapeDtypeStruct((ranks, ranks), bf16)],
        [*token_blocks, *token_share, *mixed_blocks, *scaled_rows],
        share_flops,
    )
    return (factor_share[None], core_total[None, None])


def solution(mesh):
    placed = (
        P("section", None, "expert", None),
        P("section", None, "expert", None),
        P("section", None, "expert"),
        P("section", None, "expert"),
        P("section", None, "expert"),
        P("section", None, None),
        P("section", "expert", None, None),
    )
    drawn_for = (LAYERS, CHIPS * CORES)

    def per_device(*arrays):
        local_experts = arrays[-1].shape[1]
        ranks, width = arrays[-1].shape[-1], CORES * arrays[3].shape[1] * arrays[3].shape[2]
        fits = local_experts == 1 and ranks % width == 0
        if (mesh.shape["section"], mesh.shape["expert"]) == drawn_for and fits:
            return gathered_plan(*arrays)
        return general_plan(*arrays)

    return jax.shard_map(
        per_device,
        mesh=mesh,
        in_specs=placed,
        out_specs=(P("section", "expert", None), P("section", "expert", None, None)),
        check_vma=False,
    )
```

```python
import jax
import jax.numpy as jnp
from jax import lax
from jax.experimental import pallas as pl
from jax.experimental.pallas import tpu as pltpu
from jax.sharding import PartitionSpec as P


def from_behind(value, axis, steps):
    count = lax.axis_size(axis)
    leading, last = (max(0, -steps), min(count, count - steps))
    return lax.ppermute(value, axis, [(source, source + steps) for source in range(leading, last)])


def silu_slope(values):
    sigmoid = jax.nn.sigmoid(values)
    return sigmoid * (1.0 + values * (1.0 - sigmoid))


def times_transposed(left, shared):
    return lax.dot_general(
        left, shared, (((1,), (1,)), ((), ())), preferred_element_type=jnp.float32
    )


def factor_terms(tokens_flat, proj_flat, mixed_flat, hidden_flat):

    def factor_rows(start, count):
        first_term = lax.dot_general(
            tokens_flat, proj_flat, (((0,), (0,)), ((), ())), preferred_element_type=jnp.float32
        )
        second_term = lax.dot_general(
            mixed_flat, hidden_flat, (((0,), (0,)), ((), ())), preferred_element_type=jnp.float32
        )
        return first_term + second_term

    return factor_rows


def store_slice(store, fresh, picked, usable):
    former = lax.dynamic_index_in_dim(store, picked, 0, keepdims=False)
    kept = jnp.where(usable, fresh, former)
    return lax.dynamic_update_index_in_dim(store, kept, picked, 0)


def general_plan(inputs, teacher, gate, route, slot, factor, cores):
    tokens_all = inputs[0]
    targets_all = teacher[0]
    weights_all = gate[0]
    shared = factor[0]
    blocks = cores[0]
    micro_count, token_count, channels = tokens_all.shape
    ranks = shared.shape[1]
    local_experts = blocks.shape[0]
    expert_devices = lax.axis_size("expert")
    capacity = max(2, 2 * token_count // (local_experts * expert_devices))
    slot_count = local_experts * expert_devices * capacity
    places_all = route[0] * capacity + slot[0]
    micro_range = jnp.arange(micro_count, dtype=jnp.int32)[:, None]
    token_proj = jnp.dot(
        tokens_all.reshape(-1, channels), shared, preferred_element_type=jnp.float32
    ).astype(jnp.bfloat16)
    token_proj = token_proj.reshape(micro_count, token_count, ranks)
    proj_slots = (
        jnp.zeros((micro_count, slot_count, ranks), jnp.bfloat16)
        .at[micro_range, places_all]
        .set(token_proj)
    )
    projected = lax.all_to_all(proj_slots, "expert", split_axis=1, concat_axis=1, tiled=True)
    projected = projected.reshape(micro_count, expert_devices, local_experts, capacity, ranks)
    pre = jnp.einsum("mnecr,erk->mneck", projected, blocks, preferred_element_type=jnp.float32)
    active = jax.nn.silu(pre).astype(jnp.bfloat16)
    returned = lax.all_to_all(
        active.reshape(micro_count, slot_count, ranks),
        "expert",
        split_axis=1,
        concat_axis=1,
        tiled=True,
    )
    hidden = jnp.take_along_axis(returned, places_all[:, :, None], axis=1)
    mixed = times_transposed(hidden.reshape(-1, ranks), shared).reshape(
        micro_count, token_count, channels
    )
    output = tokens_all.astype(jnp.float32) + weights_all[:, :, None] * mixed
    errors = output - targets_all.astype(jnp.float32)
    section_count = lax.axis_size("section")
    section_here = lax.axis_index("section")
    incoming = jnp.zeros((token_count, channels), jnp.bfloat16)
    mixed_store = jnp.zeros((micro_count, token_count, channels), jnp.bfloat16)
    proj_store = jnp.zeros((micro_count, token_count, ranks), jnp.bfloat16)
    pre_store = jnp.zeros(
        (micro_count, expert_devices, local_experts, capacity, ranks), jnp.bfloat16
    )
    turn_total = micro_count + section_count - 1
    for turn_index in range(turn_total):
        micro_now = turn_index - (section_count - 1 - section_here)
        usable = jnp.logical_and(micro_now >= 0, micro_now < micro_count)
        picked = jnp.clip(micro_now, 0, micro_count - 1)
        grad_out = lax.dynamic_index_in_dim(errors, picked, 0, keepdims=False) + incoming.astype(
            jnp.float32
        )
        weight_now = lax.dynamic_index_in_dim(weights_all, picked, 0, keepdims=False)
        places = lax.dynamic_index_in_dim(places_all, picked, 0, keepdims=False)
        grad_mixed = (weight_now[:, None] * grad_out).astype(jnp.bfloat16)
        grad_hidden = jnp.dot(grad_mixed, shared, preferred_element_type=jnp.float32).astype(
            jnp.bfloat16
        )
        grad_slots = jnp.zeros((slot_count, ranks), jnp.bfloat16).at[places].set(grad_hidden)
        grad_recv = lax.all_to_all(grad_slots, "expert", split_axis=0, concat_axis=0, tiled=True)
        grad_recv = grad_recv.reshape(expert_devices, local_experts, capacity, ranks)
        pre_now = lax.dynamic_index_in_dim(pre, picked, 0, keepdims=False)
        grad_pre = (grad_recv.astype(jnp.float32) * silu_slope(pre_now)).astype(jnp.bfloat16)
        grad_routed = jnp.einsum(
            "neck,erk->necr", grad_pre, blocks, preferred_element_type=jnp.float32
        ).astype(jnp.bfloat16)
        grad_home = lax.all_to_all(
            grad_routed.reshape(slot_count, ranks),
            "expert",
            split_axis=0,
            concat_axis=0,
            tiled=True,
        )
        grad_proj = grad_home[places]
        grad_in = (grad_out + times_transposed(grad_proj, shared)).astype(jnp.bfloat16)
        if turn_index + 1 < turn_total:
            incoming = from_behind(grad_in, "section", -1)
        mixed_store = store_slice(mixed_store, grad_mixed, picked, usable)
        proj_store = store_slice(proj_store, grad_proj, picked, usable)
        pre_store = store_slice(pre_store, grad_pre, picked, usable)
    core_total = jnp.einsum(
        "mnecr,mneck->erk", projected, pre_store, preferred_element_type=jnp.float32
    )
    all_rows = factor_terms(
        tokens_all.reshape(-1, channels),
        proj_store.reshape(-1, ranks),
        mixed_store.reshape(-1, channels),
        hidden.reshape(-1, ranks),
    )
    factor_share = lax.psum_scatter(
        all_rows(jnp.int32(0), channels // expert_devices * lax.axis_size("expert")),
        "expert",
        scatter_dimension=0,
        tiled=True,
    )
    return (factor_share[None], core_total.astype(jnp.bfloat16)[None])


CORES = 2
CHIPS = 4
LAYERS = 4
ROOM = 16 * 2**20


def dot(left, right):
    return jnp.dot(left, right, preferred_element_type=jnp.float32)


def dot_first(left, right):
    return lax.dot_general(
        left, right, (((0,), (0,)), ((), ())), preferred_element_type=jnp.float32
    )


def on_chips(value, pairs):
    perm = [
        (CORES * source + core, CORES * target + core)
        for source, target in pairs
        for core in range(CORES)
    ]
    return lax.ppermute(value, "expert", perm)


def swap_cores(value):
    count = lax.axis_size("expert")
    return lax.ppermute(value, "expert", [(index, index ^ 1) for index in range(count)])


def between_layers(value, pairs):
    return lax.ppermute(value, "section", pairs)


def gather_cores(core):
    beside = on_chips(core, [(0, 1), (1, 0), (2, 3), (3, 2)])
    across = on_chips(core, [(1, 2), (2, 1)])
    far_across = on_chips(beside, [(1, 2), (2, 1)])
    outward = on_chips(across, [(1, 0), (2, 3)])
    far_outward = on_chips(far_across, [(1, 0), (2, 3)])
    held, swapped = [core, beside], [swap_cores(piece) for piece in (core, beside)]
    near = [(across, outward), (far_across, far_outward)]
    far = [tuple(swap_cores(piece) for piece in pair) for pair in near]
    return [piece for both in zip(held + near, swapped + far) for piece in both]


def row_marks(route, weight, chip, core, middle):
    count = CHIPS * CORES
    place = lax.broadcasted_iota(jnp.int32, (1, 2 * count), 1)
    step = (place % count) // CORES
    turned = jnp.where(jnp.logical_and(step >= 2, middle), 5 - step, step)
    expert = CORES * (chip ^ turned) + (core ^ (place % CORES))
    marks = (route == expert).astype(jnp.float32)
    return jnp.where(place < count, marks, weight)


def across_chips(value, step):
    return on_chips(value, [(chip, chip ^ step) for chip in range(CHIPS)])


def chip_blocks(wide, chip, core):
    count = wide.shape[0] // (CHIPS * CORES)
    blocks = [
        lax.dynamic_slice_in_dim(wide, (CORES * (chip ^ step) + core) * count, count, 0)
        for step in range(CHIPS)
    ]
    return jnp.concatenate(blocks, axis=0)


def chip_columns(wide, chip, core):
    theirs = swap_cores(chip_blocks(wide, chip, 1 - core))
    return jnp.concatenate([chip_blocks(wide, chip, core), theirs], axis=1)


def both_cores(partial):
    rows = partial.shape[0] // CORES
    return partial[:rows] + swap_cores(partial[rows:])


def gram_pair(left, right):
    partial = dot_first(left, right).astype(jnp.bfloat16)
    return partial, swap_cores(partial)


def gram_sum(pair):
    return (pair[0].astype(jnp.float32) + pair[1].astype(jnp.float32)).astype(jnp.bfloat16)


def routed_product(rows, marks, start, core_refs, transposed, copies=None):
    dims = (((1,), (1 if transposed else 0,)), ((), ()))
    total = None
    for place, core_ref in enumerate(core_refs):
        if copies is not None:
            copies[place].wait()
        mark = marks[:, start + place : start + place + 1]
        chosen = jnp.where(mark > 0.5, rows, jnp.zeros_like(rows))
        term = lax.dot_general(
            chosen, core_ref[...], dims, preferred_element_type=jnp.float32
        )
        total = term if total is None else total + term
    return total


def backward_rows(score, slope, marks, core_refs):
    count = len(core_refs)
    grad_hidden = (marks[:, count : count + 1] * score).astype(jnp.bfloat16)
    grad_pre = (grad_hidden.astype(jnp.float32) * slope).astype(jnp.bfloat16)
    grad_proj = routed_product(grad_pre, marks, 0, core_refs, True)
    return grad_pre, grad_proj.astype(jnp.bfloat16)


def fetch(middle, sources, targets, arrived):
    copies = []
    for place, (source, target) in enumerate(zip(sources, targets)):
        choices = source if isinstance(source, tuple) else (source,)
        moves = [pltpu.make_async_copy(ref, target, arrived.at[place]) for ref in choices]
        copies.append(moves[0])
        if len(moves) == 1:
            moves[0].start()
        else:
            pl.when(middle)(moves[0].start)
            pl.when(jnp.logical_not(middle))(moves[1].start)
    return copies


def early_kernel(middle_ref, proj_ref, marks_ref, *refs):
    sources = [*refs[:4], (refs[4], refs[5]), (refs[6], refs[7])]
    part_ref, core_refs, arrived = refs[8], refs[9:-1], refs[-1]
    copies = fetch(middle_ref[0] > 0, sources, core_refs, arrived)
    part_ref[...] = routed_product(proj_ref[...], marks_ref[...], 0, core_refs, False, copies)


def first_kernel(middle_ref, proj_ref, marks_ref, part_ref, *refs):
    early = CHIPS * CORES - 2
    held, refs = refs[:early], refs[early:]
    sources = [(refs[0], refs[1]), (refs[2], refs[3]), refs[4], refs[5]]
    token_refs, refs = refs[6 : 5 + CHIPS], refs[5 + CHIPS :]
    scaled_ref, slope_ref, score_ref, chain_ref = refs[:4]
    sent_refs, (near_ref, far_ref) = refs[4 : 3 + CHIPS], refs[3 + CHIPS : 5 + CHIPS]
    own_ref, gram_ref, arrived, moved = refs[5 + CHIPS :]
    tall, width = token_refs[0].shape
    moves = [
        pltpu.make_async_copy(token_ref, sent_ref.at[pl.ds(0, tall), :], moved.at[place])
        for place, (token_ref, sent_ref) in enumerate(zip(token_refs, sent_refs))
    ]
    for move in moves:
        move.start()
    last = [near_ref, far_ref]
    copies = fetch(middle_ref[0] > 0, sources, [*last, own_ref, gram_ref], arrived)
    core_refs, count = [*held, *last], early + 2
    marks = marks_ref[...]
    pre = part_ref[...] + routed_product(proj_ref[...], marks, early, last, False, copies)
    sigmoid = 1.0 / (1.0 + jnp.exp(-pre))
    hidden = (pre * sigmoid).astype(jnp.bfloat16)
    slope = sigmoid * (1.0 + pre * (1.0 - sigmoid))
    weight = marks[:, count : count + 1]
    scaled = (weight * hidden.astype(jnp.float32)).astype(jnp.bfloat16)
    copies[2].wait()
    copies[3].wait()
    score = own_ref[...] + dot(scaled, gram_ref[...])
    scaled_ref[...] = scaled
    rows = scaled.shape[0]
    for sent_ref in sent_refs:
        for group in range(scaled.shape[1] // width):
            sent_ref[pl.ds(tall + group * rows, rows), :] = scaled[
                :, group * width : (group + 1) * width
            ]
    slope_ref[...] = slope
    score_ref[...] = score
    _, grad_proj = backward_rows(score, slope, marks, core_refs)
    chain_ref[...] = (scaled.astype(jnp.float32) + grad_proj.astype(jnp.float32)).astype(
        jnp.bfloat16
    )
    for move in moves:
        move.wait()


def turn_kernel(terms, late, marks_ref, scaled_ref, slope_ref, score_ref, *refs):
    score = score_ref[...]
    if late:
        score, refs = score + refs[0][...], refs[1:]
    core_refs = refs[2 * terms : len(refs) - 4]
    next_ref, grad_ref, proj_ref, chain_ref = refs[len(refs) - 4 :]
    for term in range(terms):
        score = score + dot(refs[2 * term][...], refs[2 * term + 1][...])
    next_ref[...] = score
    grad_pre, grad_proj = backward_rows(score, slope_ref[...], marks_ref[...], core_refs)
    grad_ref[...] = grad_pre
    proj_ref[...] = grad_proj
    chain_ref[...] = (scaled_ref[...].astype(jnp.float32) + grad_proj.astype(jnp.float32)).astype(
        jnp.bfloat16
    )


def call_rows(body, outs, arrays, flops, scalars=()):
    in_bytes = sum(array.size * array.dtype.itemsize for array in arrays)
    return pl.pallas_call(
        body,
        out_shape=[jax.ShapeDtypeStruct(shape, kind) for shape, kind in outs],
        in_specs=[pl.BlockSpec(memory_space=pltpu.SMEM)] * len(scalars)
        + [pl.BlockSpec(memory_space=pltpu.VMEM)] * len(arrays),
        out_specs=[pl.BlockSpec(memory_space=pltpu.VMEM)] * len(outs),
        compiler_params=pltpu.CompilerParams(vmem_limit_bytes=ROOM),
        cost_estimate=pl.CostEstimate(flops=flops, bytes_accessed=in_bytes, transcendentals=0),
    )(*scalars, *arrays)


def spread_kernel(terms, base_ref, *refs):
    total = base_ref[...].astype(jnp.float32)
    for term in range(terms):
        half_ref, near_ref, far_ref = refs[3 * term : 3 * term + 3]
        values = jnp.concatenate([near_ref[...], far_ref[...]], axis=0)
        total = total + times_transposed(half_ref[...], values)
    block = total.astype(jnp.bfloat16)
    slot_refs, outs = refs[3 * terms : 3 * terms + 2], refs[3 * terms + 2 :]
    count, width = block.shape
    for step, out_ref in enumerate(outs):

        @pl.when(pl.program_id(0) == step)
        def _():
            out_ref[:count, :] = block
            for part, (row, column, slots) in enumerate(slot_tiles(slot_refs[0], width)):
                slot_ref = slot_refs[part % CORES]
                out_ref[pl.ds(count + row, slots), :] = slot_ref[
                    step * slots : (step + 1) * slots, column : column + width
                ]


def slot_tiles(slot_ref, width):
    slots = slot_ref.shape[0] // CHIPS
    groups = slot_ref.shape[1] // width
    return [
        ((CORES * group + side) * slots, group * width, slots)
        for group in range(groups)
        for side in range(CORES)
    ]


def under_block(block, own, theirs, step):
    width = block.shape[1]
    parts = [
        (own, theirs)[part % CORES][step * slots : (step + 1) * slots, column : column + width]
        for part, (_, column, slots) in enumerate(slot_tiles(own, width))
    ]
    return jnp.concatenate([block, *parts], axis=0)


def spread(base, terms, own_slots, their_slots):
    arrays = [base] + [array for term in terms for array in term] + [own_slots, their_slots]
    height, width = base.shape
    count = height // CHIPS
    tall = count + CORES * own_slots.size // (CHIPS * width)

    def rows(columns):
        return pl.BlockSpec((count, columns), lambda step: (step, 0))

    def whole(array):
        return pl.BlockSpec(array.shape, lambda step: (0, 0))

    specs = [rows(width)]
    for half, near, far in terms:
        specs += [rows(half.shape[1]), whole(near), whole(far)]
    specs += [whole(own_slots), whole(their_slots)]

    def body(*refs):
        spread_kernel(len(terms), *refs)

    return pl.pallas_call(
        body,
        name="spread",
        grid=(CHIPS,),
        out_shape=[jax.ShapeDtypeStruct((tall, width), jnp.bfloat16)] * CHIPS,
        in_specs=specs,
        out_specs=[pl.BlockSpec((tall, width), lambda step: (0, 0))] * CHIPS,
        compiler_params=pltpu.CompilerParams(vmem_limit_bytes=ROOM),
        cost_estimate=pl.CostEstimate(
            flops=2 * height * width * terms[0][0].shape[1] * len(terms),
            bytes_accessed=sum(array.size * array.dtype.itemsize for array in arrays),
            transcendentals=0,
        ),
    )(*arrays)


def token_kernel(flag_ref, *refs):
    blocks, pieces, out_ref = refs[:CHIPS], refs[CHIPS:-1], refs[-1]
    count, rows = out_ref.shape[0], pieces[0].shape[0]
    middle = flag_ref[0] > 0
    third, fourth = blocks[2][:count, :], blocks[3][:count, :]
    lefts = [blocks[0][:count, :], blocks[1][:count, :]]
    lefts += [jnp.where(middle, fourth, third), jnp.where(middle, third, fourth)]
    rights = [[ref[...] for ref in pieces[:2]], [ref[...] for ref in pieces[2:4]]]
    rights += [[ref[start : start + rows, :] for ref in pieces[4:]] for start in (0, rows)]
    total = None
    for left, right in zip(lefts, rights):
        term = dot(left, jnp.concatenate(right, axis=0))
        total = term if total is None else total + term
    out_ref[...] = total


def grouped_rows(ref, start, rows):
    groups = (ref.shape[0] - start) // rows
    return jnp.concatenate(
        [ref[start + group * rows : start + (group + 1) * rows, :] for group in range(groups)],
        axis=1,
    )


def last_kernel(*refs):
    token_refs, refs = refs[:CHIPS], refs[CHIPS:]
    total_ref, product_refs, scaled_refs = refs[0], refs[1 : 1 + CHIPS], refs[1 + CHIPS : -2]
    share_ref, core_ref = refs[-2:]
    count = share_ref.shape[0]
    rows, tall = scaled_refs[0].shape[0], token_refs[0].shape[0]
    total = total_ref[...]
    for step in range(CHIPS):
        if step == 0:
            near, far = scaled_refs[0][...], scaled_refs[1][...]
        else:
            near = grouped_rows(token_refs[step], tall, rows)
            far = grouped_rows(scaled_refs[1 + step], 0, rows)
        total = total + dot(product_refs[step][:count, :], jnp.concatenate([near, far], axis=0))
    share_ref[...] = total
    width = token_refs[0].shape[1]
    slots = (token_refs[0].shape[0] - count) * width // core_ref.shape[0]

    def group(block_refs, column):
        start = count + column * slots
        return jnp.concatenate([ref[start : start + slots, :] for ref in block_refs], axis=0)

    groups = core_ref.shape[0] // width
    for left in range(groups):
        for right in range(groups):
            product = dot_first(group(token_refs, left), group(product_refs[:CHIPS], right))
            core_ref[
                left * width : (left + 1) * width, right * width : (right + 1) * width
            ] = product.astype(jnp.bfloat16)


def block_call(body, outs, arrays, flops, scalars=()):
    return pl.pallas_call(
        body,
        out_shape=outs,
        in_specs=[pl.BlockSpec(memory_space=pltpu.SMEM)] * len(scalars)
        + [pl.BlockSpec(memory_space=pltpu.VMEM)] * len(arrays),
        out_specs=[pl.BlockSpec(memory_space=pltpu.VMEM)] * len(outs),
        compiler_params=pltpu.CompilerParams(vmem_limit_bytes=ROOM),
        cost_estimate=pl.CostEstimate(
            flops=flops,
            bytes_accessed=sum(array.size * array.dtype.itemsize for array in arrays),
            transcendentals=0,
        ),
    )(*scalars, *arrays)


def after(value, earlier):
    return lax.optimization_barrier((value, earlier))[0]


def gathered_plan(inputs, teacher, gate, route, slot, factor, cores):
    bf16, f32 = jnp.bfloat16, jnp.float32
    shared = factor[0]
    channels, ranks = shared.shape
    devices = lax.axis_size("expert")
    micro_count, token_count = route.shape[1:]
    rows = micro_count * token_count
    here = lax.axis_index("expert")
    chip, core = here // CORES, here % CORES
    middle = jnp.logical_or(chip == 1, chip == 2)
    tokens = inputs[0].reshape(rows, channels)

    travelled = gather_cores(cores[0, 0])
    marks = row_marks(
        route[0].reshape(rows, 1), gate[0].reshape(rows, 1), chip, core, middle
    )

    down = [(3, 2), (1, 0)]
    two_down = [(3, 1), (2, 0)]
    two_cross, down_cross = [(0, 1)], [(2, 0)]
    own_half = chip_blocks(shared, chip, core)
    half_down = between_layers(own_half, down)
    half_two = between_layers(own_half, two_down)
    half_cross = between_layers(half_two, two_cross)
    half_late = between_layers(half_down, down_cross)
    turned = lax.optimization_barrier(tokens.T)
    wanted = lax.optimization_barrier(teacher[0].reshape(rows, channels).T)
    difference = (turned.astype(f32) - wanted.astype(f32)).astype(bf16)
    difference = chip_columns(difference, chip, core)
    step_down = between_layers(difference, down)
    step_two = between_layers(difference, two_down)

    capacity = max(2, 2 * token_count // devices)
    slots = micro_count * capacity
    micro = jnp.arange(rows, dtype=jnp.int32) // token_count
    expert = route[0].reshape(rows)
    near = (expert % CORES ^ core) * CHIPS + (expert // CORES ^ chip)
    place = near * slots + micro * capacity + slot[0].reshape(rows)
    picks = (jnp.arange(devices * slots, dtype=jnp.int32)[:, None] == place[None, :]).astype(bf16)

    def to_slots(values):
        held = dot(picks, values).astype(bf16)
        half = CHIPS * slots
        return held[:half], swap_cores(held[half:])

    step_cross = between_layers(step_two, two_cross)
    step_late = between_layers(step_down, down_cross)
    projected = dot(tokens, shared).astype(bf16)
    own_gram = gram_pair(own_half, own_half)
    proj_slots = to_slots(projected)
    gram = gram_sum(own_gram)
    own_score = both_cores(dot_first(difference, own_half))
    turned = chip_columns(turned, chip, core)
    token_blocks = [
        under_block(
            turned[step * channels // devices : (step + 1) * channels // devices],
            *proj_slots,
            step,
        )
        for step in range(CHIPS)
    ]
    down_gram = gram_sum(gram_pair(half_down, own_half))
    two_gram = gram_sum(gram_pair(half_two, own_half))
    down_score = both_cores(dot_first(step_down, own_half))

    wide = (rows, ranks)
    product_flops = 2 * rows * ranks * ranks
    flag = middle.astype(jnp.int32).reshape(1)
    block = pltpu.VMEM((ranks, ranks), bf16)

    def core_call(body, sources, outs, arrays, scratch, products, extra=()):
        flat = [ref for source in sources for ref in (source if type(source) is tuple else [source])]
        moved = [pltpu.SemaphoreType.DMA((len(extra),))] if extra else []
        return pl.pallas_call(
            body,
            out_shape=outs,
            in_specs=[pl.BlockSpec(memory_space=pltpu.SMEM)]
            + [pl.BlockSpec(memory_space=pltpu.VMEM)] * len(arrays)
            + [pl.BlockSpec(memory_space=pl.ANY)] * (len(flat) + len(extra)),
            out_specs=[pl.BlockSpec(memory_space=pltpu.VMEM)] * len(outs),
            scratch_shapes=scratch + [pltpu.SemaphoreType.DMA((len(sources),))] + moved,
            compiler_params=pltpu.CompilerParams(vmem_limit_bytes=ROOM),
            cost_estimate=pl.CostEstimate(
                flops=product_flops * products,
                bytes_accessed=2 * len(sources) * ranks * ranks,
                transcendentals=0,
            ),
        )(flag, *arrays, *flat, *extra)

    part, *held = core_call(
        early_kernel,
        travelled[:-2],
        [jax.ShapeDtypeStruct(wide, f32)] + [block] * (devices - 2),
        [projected, marks],
        [],
        devices - 2,
    )
    sent = pltpu.VMEM((token_blocks[0].shape[0] + ranks // CORES, CORES * rows), bf16)
    scaled, slope, score, chain, *last = core_call(
        first_kernel,
        [*travelled[-2:], own_score, gram],
        [jax.ShapeDtypeStruct(wide, kind) for kind in (bf16, f32, f32, bf16)]
        + [sent] * (CHIPS - 1)
        + [block] * 2,
        [projected, marks, part, *held],
        [pltpu.VMEM(wide, f32), pltpu.VMEM((ranks, ranks), bf16)],
        devices + 3,
        token_blocks[1:],
    )
    sent, last = last[: CHIPS - 1], last[CHIPS - 1 :]
    pieces = [*held, *last]

    def turn(score, late, terms):
        arrays = [array for pair in terms for array in pair]

        def body(*refs):
            turn_kernel(len(terms), bool(late), *refs)

        return call_rows(
            body,
            [(wide, f32), (wide, bf16), (wide, bf16), (wide, bf16)],
            [marks, scaled, slope, score, *late, *arrays, *pieces],
            product_flops * (devices + len(terms)),
        )

    chain_first = chain
    first_down = between_layers(chain, [(3, 2)])
    first_two = between_layers(chain, [(3, 1)])
    token_blocks = token_blocks[:1] + [
        across_chips(sent[step - 1], step) for step in range(1, CHIPS)
    ]
    score, _, _, chain = turn(score, [down_score], [(first_down, down_gram)])

    second_cross = between_layers(chain, [(2, 1)])
    second_two = between_layers(chain, [(2, 0)])
    first_three = between_layers(after(chain_first, chain), [(3, 0)])
    half_cross = after(half_cross, chain)
    step_cross = after(step_cross, chain)
    cross_pair = gram_pair(half_cross, own_half)
    late_steps = (step_two.astype(f32) + step_cross.astype(f32)).astype(bf16)
    late_score = both_cores(dot_first(late_steps, own_half))
    cross_product = gram_sum(cross_pair)
    score, _, _, chain = turn(
        score, [late_score], [(first_two, two_gram), (second_cross, cross_product)]
    )

    third_down = between_layers(chain, [(1, 0)])
    half_late, step_late = after(half_late, chain), after(step_late, chain)
    late_pair = gram_pair(half_late, own_half)
    last_score = both_cores(dot_first(step_late, own_half))
    steps_total = difference.astype(f32) + step_down.astype(f32)
    steps_total = steps_total + after(late_steps, chain).astype(f32)
    steps_total = (steps_total + step_late.astype(f32)).astype(bf16)
    late_product = gram_sum(late_pair)
    score, grad_pre, grad_proj, _ = turn(
        score,
        [last_score],
        [(second_two, two_gram), (first_three, late_product), (third_down, down_gram)],
    )

    def with_swap(values):
        return values, swap_cores(values)

    near_rows = on_chips(grad_proj, [(0, 1), (1, 0), (2, 3), (3, 2)])
    grad_slots = to_slots(grad_pre)
    scaled_pair = with_swap(after(scaled, grad_proj))
    two_pair = with_swap(first_two + after(second_two, grad_proj))
    cross_pair = with_swap(after(second_cross, grad_proj))
    late_pair = with_swap(after(first_three, grad_proj))
    down_pair = with_swap(first_down + third_down)
    mixed_blocks = spread(
        steps_total,
        [
            (own_half, *scaled_pair),
            (half_two, *two_pair),
            (half_cross, *cross_pair),
            (half_late, *late_pair),
            (half_down, *down_pair),
        ],
        *grad_slots,
    )
    mixed_first = mixed_blocks[0]
    both_rows = jnp.concatenate([grad_proj, near_rows], axis=0)
    mid_rows = on_chips(both_rows, [(1, 2), (2, 1)])
    tall = token_blocks[0].shape[0]
    scaled_parts = [after(part, mid_rows)[tall:] for part in token_blocks[1:]]
    end_rows = on_chips(mid_rows, [(1, 0), (2, 3)])
    far_rows = jnp.where(middle, mid_rows, end_rows)
    proj_rows = [grad_proj, swap_cores(after(grad_proj, mixed_first))]
    proj_rows += [near_rows, swap_cores(after(near_rows, mixed_first))]
    proj_rows += [far_rows, swap_cores(far_rows)]
    mixed_blocks = list(mixed_blocks[:1]) + [
        across_chips(mixed_blocks[step], step) for step in range(1, CHIPS)
    ]
    scaled_rows = [*scaled_pair, *(swap_cores(part) for part in scaled_parts)]
    share = jax.ShapeDtypeStruct((channels // devices, ranks), f32)
    share_flops = 2 * channels * rows * ranks
    token_share = block_call(token_kernel, [share], token_blocks + proj_rows, share_flops, [flag])
    factor_share, core_total = block_call(
        last_kernel,
        [share, jax.ShapeDtypeStruct((ranks, ranks), bf16)],
        [*token_blocks, *token_share, *mixed_blocks, *scaled_rows],
        share_flops,
    )
    return (factor_share[None], core_total[None, None])


def solution(mesh):
    placed = (
        P("section", None, "expert", None),
        P("section", None, "expert", None),
        P("section", None, "expert"),
        P("section", None, "expert"),
        P("section", None, "expert"),
        P("section", None, None),
        P("section", "expert", None, None),
    )
    drawn_for = (LAYERS, CHIPS * CORES)

    def per_device(*arrays):
        local_experts = arrays[-1].shape[1]
        ranks, width = arrays[-1].shape[-1], CORES * arrays[3].shape[1] * arrays[3].shape[2]
        fits = local_experts == 1 and ranks % width == 0
        if (mesh.shape["section"], mesh.shape["expert"]) == drawn_for and fits:
            return gathered_plan(*arrays)
        return general_plan(*arrays)

    return jax.shard_map(
        per_device,
        mesh=mesh,
        in_specs=placed,
        out_specs=(P("section", "expert", None), P("section", "expert", None, None)),
        check_vma=False,
    )
```
